32 devices in a mesh: batch: 2 (over y), blk: 8 (over z, core), head: 2 (over x).
Axes of the slice: x: 2, y: 2, z: 4, core: 2. Of those that a mesh axis runs over, the one named last changes fastest.
Arguments:
- layer_input: bfloat16 [8, 4096, 768], P('batch', ('blk', 'head')), may hold values from -6 to 6
- lengths: int32 [8], P('batch'), may hold values from 1024 to 4096, as said below
- cotangent: bfloat16 [8, 4096, 768], P('batch', ('blk', 'head')), may hold values from -6 to 6
- w_query: bfloat16 [768, 768], P(('batch', 'blk', 'head')), may hold values from -0.3125 to 0.3125
- b_query: bfloat16 [768], P(('batch', 'blk', 'head')), may hold values from -3 to 3
- w_key: bfloat16 [768, 768], P(('batch', 'blk', 'head')), may hold values from -0.3125 to 0.3125
- w_value: bfloat16 [768, 768], P(('batch', 'blk', 'head')), may hold values from -0.21875 to 0.21875
- b_value: bfloat16 [768], P(('batch', 'blk', 'head')), may hold values from -0.59765625 to 0.59765625
- w_attn_out: bfloat16 [768, 768], P(('batch', 'blk', 'head')), may hold values from -1.5 to 1.5
- b_attn_out: bfloat16 [768], P(('batch', 'blk', 'head')), may hold values from -2 to 2
- norm1_gain: bfloat16 [768], P(('batch', 'blk', 'head')), may hold values from 0.5 to 1.5
- norm1_bias: bfloat16 [768], P(('batch', 'blk', 'head')), may hold values from -2 to 2
- w_inner: bfloat16 [768, 3072], P(('batch', 'blk', 'head')), may hold values from -0.21875 to 0.21875
- b_inner: bfloat16 [3072], P(('batch', 'blk', 'head')), may hold values from -2 to 2
- w_outer: bfloat16 [3072, 768], P(('batch', 'blk', 'head')), may hold values from -0.109375 to 0.109375
- b_outer: bfloat16 [768], P(('batch', 'blk', 'head')), may hold values from -2 to 2
- norm2_gain: bfloat16 [768], P(('batch', 'blk', 'head')), may hold values from 0.5 to 1.5
- norm2_bias: bfloat16 [768], P(('batch', 'blk', 'head')), may hold values from -2 to 2
Outputs:
- output: bfloat16 [8, 4096, 768], P('batch', ('blk', 'head'))
- input_grad: bfloat16 [8, 4096, 768], P('batch', ('blk', 'head'))
- grad_w_query: float32 [768, 768], P(('batch', 'blk', 'head'))
- grad_b_query: float32 [768], P(('batch', 'blk', 'head'))
- grad_w_key: float32 [768, 768], P(('batch', 'blk', 'head'))
- grad_w_value: float32 [768, 768], P(('batch', 'blk', 'head'))
- grad_b_value: float32 [768], P(('batch', 'blk', 'head'))
- grad_w_attn_out: float32 [768, 768], P(('batch', 'blk', 'head'))
- grad_b_attn_out: float32 [768], P(('batch', 'blk', 'head'))
- grad_norm1_gain: float32 [768], P(('batch', 'blk', 'head'))
- grad_norm1_bias: float32 [768], P(('batch', 'blk', 'head'))
- grad_w_inner: float32 [768, 3072], P(('batch', 'blk', 'head'))
- grad_b_inner: float32 [3072], P(('batch', 'blk', 'head'))
- grad_w_outer: float32 [3072, 768], P(('batch', 'blk', 'head'))
- grad_b_outer: float32 [768], P(('batch', 'blk', 'head'))
- grad_norm2_gain: float32 [768], P(('batch', 'blk', 'head'))
- grad_norm2_bias: float32 [768], P(('batch', 'blk', 'head'))
The draws below stay inside these ranges and needn't reach their ends.
Inputs may be any that keep to these rules, and one draw needn't show every extreme that they name: `lengths`: each sequence's number of valid positions; later positions are padding. In every draw some sequence has exactly 4096 and some exactly 1024.
All inputs are finite; a program needn't handle non-finite values.
Results may differ from the reference program's by a relative error of at most 0.03.
Values may be sent and summed in bfloat16 or wider, within the bound.
No kernel may reach another device: no remote copies, remote signals or barrier semaphores. Data moves between devices by JAX's collectives and lax.ppermute only.
A program may use at most 120 MiB of HBM per device.

```python
import math
import jax
import jax.numpy as jnp
from jax import lax

D = 768
HEADS = 12
HEAD_DIM = 64
FF = 3072
LEN = 4096
MIN_LEN = 1024
SEQS = 8


def draw_lengths(key, part):
    base_lengths = jax.random.randint(jax.random.fold_in(key, 11), (SEQS,), MIN_LEN, LEN + 1)
    chosen = jax.random.permutation(jax.random.fold_in(key, 12), SEQS)
    places = jnp.arange(SEQS, dtype=jnp.int32)
    base_lengths = jnp.where(places == chosen[0], LEN, base_lengths)
    base_lengths = jnp.where(places == chosen[1], MIN_LEN, base_lengths)
    return base_lengths.astype(jnp.int32)


def steps_of(key, dims, split, least, top_value):
    loudness, own = 1.0, jax.random.fold_in(key, 6)
    for dim, parts in split:
        draws = jnp.exp(jax.random.uniform(jax.random.fold_in(own, dim), (parts,), jnp.float32, least / len(split), top_value / len(split)))
        loudness = loudness * jnp.repeat(draws, dims[dim] // parts).reshape([-1 if axis == dim else 1 for axis in range(len(dims))])
    return loudness


def noise(rng, dims, scale, bound, pieces=(), kind=jnp.bfloat16):
    level = steps_of(rng, dims, pieces, -0.22, 0.18) if pieces else 1.0
    values = jax.random.normal(rng, dims, jnp.float32) * scale * level
    return jnp.minimum(jnp.maximum(values, -bound), bound).astype(kind)


def setup_inputs(seed: int = 0) -> dict:
    streams_of = jax.random.split(jax.random.key(seed), 19)
    layer_input = noise(streams_of[0], (SEQS, LEN, D), 1.0, 6.0, ((0, 2), (1, 16)))
    lengths = draw_lengths(jax.random.fold_in(streams_of[18], 71), 0)
    cotangent = noise(streams_of[2], (SEQS, LEN, D), 1.0, 6.0, ((0, 2), (1, 16)))
    w_query = noise(streams_of[3], (D, D), (D // 2) ** -0.5, 0.3125, ((0, 32),))
    b_query = noise(streams_of[4], (D,), 0.5, 3.0, ((0, 32),))
    w_key = noise(streams_of[5], (D, D), (D // 2) ** -0.5, 0.3125, ((0, 32),))
    w_value = noise(streams_of[6], (D, D), D ** -0.5, 0.21875, ((0, 32),))
    b_value = noise(streams_of[7], (D,), 0.1, 0.59765625, ((0, 32),))
    w_attn_out = noise(streams_of[8], (D, D), 16 ** -0.5, 1.5, ((0, 32),))
    b_attn_out = noise(streams_of[9], (D,), 0.3, 2.0, ((0, 32),))
    norm1_gain = jnp.clip(1.0 + 0.1 * jax.random.normal(streams_of[10], (D,), jnp.float32), 0.5, 1.5).astype(jnp.bfloat16)
    norm1_bias = noise(streams_of[11], (D,), 0.3, 2.0, ((0, 32),))
    w_inner = noise(streams_of[12], (D, FF), D ** -0.5, 0.21875, ((0, 32),))
    b_inner = noise(streams_of[13], (FF,), 0.3, 2.0, ((0, 32),))
    w_outer = noise(streams_of[14], (FF, D), FF ** -0.5, 0.109375, ((0, 32),))
    b_outer = noise(streams_of[15], (D,), 0.3, 2.0, ((0, 32),))
    norm2_gain = jnp.clip(1.0 + 0.1 * jax.random.normal(streams_of[16], (D,), jnp.float32), 0.5, 1.5).astype(jnp.bfloat16)
    norm2_bias = noise(streams_of[17], (D,), 0.3, 2.0, ((0, 32),))
    return dict(layer_input=layer_input, lengths=lengths, cotangent=cotangent, w_query=w_query, b_query=b_query, w_key=w_key, w_value=w_value, b_value=b_value, w_attn_out=w_attn_out, b_attn_out=b_attn_out, norm1_gain=norm1_gain, norm1_bias=norm1_bias, w_inner=w_inner, b_inner=b_inner, w_outer=w_outer, b_outer=b_outer, norm2_gain=norm2_gain, norm2_bias=norm2_bias)


NEG_BIG = -1e+30
EPSILON = 1e-06

@jax.custom_vjp
def low(v):
    return lax.optimization_barrier(v.astype(jnp.bfloat16)).astype(jnp.float32)

@jax.custom_vjp
def low_back(v):
    return v

def low_keep(v):
    return (low(v), None)

def low_pass(kept, grad):
    return (grad,)

def back_keep(v):
    return (v, None)

def back_low(kept, grad):
    return (low(grad),)
low.defvjp(low_keep, low_pass)
low_back.defvjp(back_keep, back_low)

def rounded_both(values_in):
    return low(low_back(values_in))

def matmul(left_op, right_op):
    return jnp.dot(left_op, right_op, precision=lax.Precision.HIGHEST, preferred_element_type=jnp.float32)

def norm_apply(residue, gain_row, shift_row):
    center = lax.optimization_barrier(jnp.mean(residue, axis=-1, keepdims=True))
    centred = residue - center
    spread = lax.optimization_barrier(jnp.mean(centred * centred, axis=-1, keepdims=True))
    return centred * lax.rsqrt(spread + EPSILON) * gain_row + shift_row

def split_heads(packed):
    return jnp.transpose(packed.reshape(LEN, HEADS, HEAD_DIM), (1, 0, 2))

def sequence_forward(weights_all, tokens, seq_len):
    w_q, b_q, w_k, w_v, b_v, w_o, b_o, gain_a, shift_a, w_i, b_i, w_d, b_d, gain_b, shift_b = weights_all
    key_valid = jnp.arange(LEN, dtype=jnp.int32) < seq_len
    score_scale = 1.0 / math.sqrt(HEAD_DIM)
    queries = rounded_both(matmul(tokens, w_q) + b_q)
    keys_all = rounded_both(matmul(tokens, w_k))
    values_all = rounded_both(matmul(tokens, w_v) + b_v)

    def one_head(head_parts):
        head_query, head_key, head_value = head_parts
        scores = low_back(jnp.where(key_valid[None, :], matmul(head_query, head_key.T) * score_scale, NEG_BIG))
        row_top = lax.optimization_barrier(jnp.max(scores, axis=-1, keepdims=True))
        expo = jnp.exp(scores - row_top)
        row_probs = expo / lax.optimization_barrier(jnp.sum(expo, axis=-1, keepdims=True))
        return matmul(low(row_probs), head_value)
    mixed_heads = lax.map(jax.checkpoint(one_head), (split_heads(queries), split_heads(keys_all), split_heads(values_all)))
    attended = rounded_both(jnp.transpose(mixed_heads, (1, 0, 2)).reshape(LEN, HEADS * HEAD_DIM))
    branch = low_back(matmul(attended, w_o) + b_o)
    normed1 = norm_apply(tokens + branch, gain_a, shift_a)
    inner_pre = low_back(matmul(low(normed1), w_i) + b_i)
    active = low(jax.nn.gelu(inner_pre, approximate=False))
    outer_out = low_back(matmul(active, w_d) + b_d)
    return norm_apply(normed1 + outer_out, gain_b, shift_b)

def reference(layer_input, lengths, cotangent, w_query, b_query, w_key, w_value, b_value, w_attn_out, b_attn_out, norm1_gain, norm1_bias, w_inner, b_inner, w_outer, b_outer, norm2_gain, norm2_bias):
    weights_all = tuple((member.astype(jnp.float32) for member in (w_query, b_query, w_key, w_value, b_value, w_attn_out, b_attn_out, norm1_gain, norm1_bias, w_inner, b_inner, w_outer, b_outer, norm2_gain, norm2_bias)))

    def per_seq(totals, seq_item):
        tokens, cot_rows, seq_len = seq_item
        row_keep = (jnp.arange(LEN, dtype=jnp.int32) < seq_len)[:, None]
        result, pull_back = jax.vjp(lambda params_in, tokens_in: sequence_forward(params_in, tokens_in, seq_len), weights_all, tokens.astype(jnp.float32))
        grad_all, grad_tokens = pull_back(jnp.where(row_keep, cot_rows.astype(jnp.float32), 0.0))
        totals = jax.tree.map(lambda first_op, second_op: first_op + second_op, totals, grad_all)
        return (totals, (result.astype(jnp.bfloat16), grad_tokens.astype(jnp.bfloat16)))
    zeros_all = tuple((jnp.zeros_like(member) for member in weights_all))
    totals, (outputs, input_grad) = lax.scan(per_seq, zeros_all, (layer_input, cotangent, lengths))
    return (outputs, input_grad, totals[0], totals[1], totals[2], totals[3], totals[4], totals[5], totals[6], totals[7], totals[8], totals[9], totals[10], totals[11], totals[12], totals[13], totals[14])
```

```python
import functools
import math

import jax
import jax.numpy as jnp
from jax import lax
from jax.experimental import pallas as pl
from jax.experimental.pallas import tpu as pltpu
from jax.sharding import PartitionSpec as P

HEADS = 12
HEAD_DIM = 64
CORES = 2
MEMBERS = 4
EXTRA = 16
NEG_BIG = -1e30
EPSILON = 1e-06
F32 = jnp.float32
BF16 = jnp.bfloat16
ALL_AXES = ("batch", "blk", "head")
VMEM_LIMIT = 56 * 2**20


def dot(left_op, right_op, left_dim, right_dim):
    return lax.dot_general(
        left_op, right_op, (((left_dim,), (right_dim,)), ((), ())), preferred_element_type=F32
    )


def shift_planes(array, distance):
    size = lax.axis_size("blk")
    route = [(i, (i + CORES * distance) % size) for i in range(size)]
    return lax.ppermute(array, "blk", route)


def shift_batch(array, distance):
    size = lax.axis_size("batch")
    return lax.ppermute(array, "batch", [(i, (i + distance) % size) for i in range(size)])


def swap_member(array, member):
    size = lax.axis_size("blk")
    if member == 1:
        return lax.ppermute(array, "head", [(0, 1), (1, 0)])
    if member == 2:
        return lax.ppermute(array, "blk", [(i, i ^ 1) for i in range(size)])
    route = [(i * 2 + j, (i ^ 1) * 2 + (j ^ 1)) for i in range(size) for j in range(2)]
    return lax.ppermute(array, ("blk", "head"), route)


def pick(array, index):
    return lax.dynamic_index_in_dim(array, index, 0, keepdims=False)


def reorder_members(stack, core, head_place):
    stack = jnp.where(core == 1, jnp.concatenate([stack[2:], stack[:2]]), stack)
    swapped = jnp.stack([stack[1], stack[0], stack[3], stack[2]])
    return jnp.where(head_place == 1, swapped, stack)


def forward_kernel(block_q, block_k, q_ref, k_ref, v_ref, mask_ref, out_ref, sums_ref, keys, values):
    key_count = k_ref.shape[1]
    query_count = q_ref.shape[1]
    rows = lax.broadcasted_iota(jnp.int32, (EXTRA, key_count), 0)
    joined = jnp.concatenate([k_ref[...], mask_ref[...]], axis=0)
    keys[...] = joined.astype(F32).T.astype(BF16)
    values[:HEAD_DIM, :] = v_ref[...]
    values[HEAD_DIM:, :] = jnp.where(rows == 0, 1.0, 0.0).astype(BF16)
    rows_q = lax.broadcasted_iota(jnp.int32, (EXTRA, block_q), 0)
    ones_row = jnp.where(rows_q == 0, 1.0, 0.0).astype(BF16)
    scale = 1.0 / math.sqrt(HEAD_DIM)

    def query_block(i, unused):
        q_start = pl.multiple_of(i * block_q, block_q)
        scaled = (q_ref[:, pl.ds(q_start, block_q)].astype(F32) * scale).astype(BF16)
        query = jnp.concatenate([scaled, ones_row], axis=0)

        def key_block(j, carry):
            top, acc = carry
            k_start = pl.multiple_of(j * block_k, block_k)
            scores = dot(keys[pl.ds(k_start, block_k), :], query, 1, 0)
            new_top = jnp.maximum(top, jnp.max(scores, axis=0, keepdims=True))
            probs = jnp.exp(scores - new_top)
            acc = acc * jnp.exp(top - new_top) + dot(
                values[:, pl.ds(k_start, block_k)], probs.astype(BF16), 1, 0
            )
            return new_top, acc

        top, acc = lax.fori_loop(
            0,
            key_count // block_k,
            key_block,
            (
                jnp.full((1, block_q), NEG_BIG, F32),
                jnp.zeros((HEAD_DIM + EXTRA, block_q), F32),
            ),
        )
        total = acc[HEAD_DIM : HEAD_DIM + 1, :]
        out_ref[:, pl.ds(q_start, block_q)] = (acc[:HEAD_DIM, :] / total).astype(BF16)
        sums_ref[0, :, pl.ds(q_start, block_q)] = top + jnp.log(total)
        return 0

    lax.fori_loop(0, query_count // block_q, query_block, 0)


def attention_forward(queries, keys, values, mask_rows):
    heads = queries.shape[0] // HEAD_DIM
    query_count = queries.shape[1]
    key_count = keys.shape[1]
    block_q = min(1024, query_count)
    block_k = min(1024, key_count)
    spec_q = pl.BlockSpec((HEAD_DIM, query_count), lambda h: (h, 0))
    spec_k = pl.BlockSpec((HEAD_DIM, key_count), lambda h: (h, 0))
    return pl.pallas_call(
        functools.partial(forward_kernel, block_q, block_k),
        grid=(heads,),
        in_specs=[spec_q, spec_k, spec_k, pl.BlockSpec((EXTRA, key_count), lambda h: (0, 0))],
        out_specs=[spec_q, pl.BlockSpec((1, 1, query_count), lambda h: (h, 0, 0))],
        out_shape=[
            jax.ShapeDtypeStruct((heads * HEAD_DIM, query_count), BF16),
            jax.ShapeDtypeStruct((heads, 1, query_count), F32),
        ],
        scratch_shapes=[
            pltpu.VMEM((key_count, HEAD_DIM + EXTRA), BF16),
            pltpu.VMEM((HEAD_DIM + EXTRA, key_count), BF16),
        ],
        compiler_params=pltpu.CompilerParams(vmem_limit_bytes=VMEM_LIMIT),
        cost_estimate=pl.CostEstimate(
            flops=heads * 16 * HEAD_DIM * query_count * key_count,
            transcendentals=heads * query_count * key_count,
            bytes_accessed=heads * 8 * HEAD_DIM * key_count,
        ),
    )(queries, keys, values, mask_rows)


def split_three(row):
    high = row.astype(BF16)
    rest = row - high.astype(F32)
    middle = rest.astype(BF16)
    low = (rest - middle.astype(F32)).astype(BF16)
    return high.astype(F32), middle.astype(F32), low.astype(F32)


def backward_kernel(
    block_q,
    block_k,
    q_ref,
    k_ref,
    v_ref,
    mask_ref,
    out_ref,
    sums_ref,
    grad_ref,
    dq_ref,
    dk_ref,
    dv_ref,
    query_rows,
    keys,
    grad_rows,
    values,
    scaled_q,
    dq_acc,
):
    key_count = k_ref.shape[1]
    query_count = q_ref.shape[1]
    scale = 1.0 / math.sqrt(HEAD_DIM)
    places_q = lax.broadcasted_iota(jnp.int32, (EXTRA, query_count), 0)
    places_k = lax.broadcasted_iota(jnp.int32, (EXTRA, key_count), 0)

    def extra_rows(row, fourth):
        high, middle, low = split_three(row)
        rows = jnp.where(
            places_q == 0, high, jnp.where(places_q == 1, middle, jnp.where(places_q == 2, low, 0.0))
        )
        return jnp.where(places_q == 3, fourth, rows).astype(BF16)

    query = (q_ref[...].astype(F32) * scale).astype(BF16)
    scaled_q[...] = query
    grads = grad_ref[...]
    deltas = jnp.sum(grads.astype(F32) * out_ref[...].astype(F32), axis=0, keepdims=True)
    joined_q = jnp.concatenate([query, extra_rows(-sums_ref[0], 1.0)], axis=0)
    query_rows[...] = joined_q.astype(F32).T.astype(BF16)
    joined_g = jnp.concatenate([grads, extra_rows(-deltas, 0.0)], axis=0)
    grad_rows[...] = joined_g.astype(F32).T.astype(BF16)
    ones_rows = jnp.where(places_k < 3, 1.0, 0.0)
    mask_row = mask_ref[0:1, :].astype(F32)
    keys[:HEAD_DIM, :] = k_ref[...]
    keys[HEAD_DIM:, :] = jnp.where(places_k == 3, mask_row, ones_rows).astype(BF16)
    values[:HEAD_DIM, :] = v_ref[...]
    values[HEAD_DIM:, :] = ones_rows.astype(BF16)
    dq_acc[...] = jnp.zeros_like(dq_acc)

    def key_block(j, unused):
        k_start = pl.multiple_of(j * block_k, block_k)
        key_part = keys[:, pl.ds(k_start, block_k)]
        value_part = values[:, pl.ds(k_start, block_k)]
        plain_keys = k_ref[:, pl.ds(k_start, block_k)]

        def query_block(i, carry):
            dk, dv = carry
            q_start = pl.multiple_of(i * block_q, block_q)
            probs = jnp.exp(dot(query_rows[pl.ds(q_start, block_q), :], key_part, 1, 0))
            moved = dot(grad_rows[pl.ds(q_start, block_q), :], value_part, 1, 0)
            grad_scores = (probs * moved).astype(BF16)
            dv = dv + dot(grad_ref[:, pl.ds(q_start, block_q)], probs.astype(BF16), 1, 0)
            dk = dk + dot(scaled_q[:, pl.ds(q_start, block_q)], grad_scores, 1, 0)
            dq_acc[:, pl.ds(q_start, block_q)] += dot(plain_keys, grad_scores, 1, 1)
            return dk, dv

        zeros = jnp.zeros((HEAD_DIM, block_k), F32)
        dk, dv = lax.fori_loop(0, query_count // block_q, query_block, (zeros, zeros))
        dk_ref[:, pl.ds(k_start, block_k)] = dk.astype(BF16)
        dv_ref[:, pl.ds(k_start, block_k)] = dv.astype(BF16)
        return 0

    lax.fori_loop(0, key_count // block_k, key_block, 0)
    dq_ref[...] = (dq_acc[...] * scale).astype(BF16)


def attention_backward(queries, keys, values, mask_rows, outs, sums, grads):
    heads = queries.shape[0] // HEAD_DIM
    query_count = queries.shape[1]
    key_count = keys.shape[1]
    block_q = min(1024, query_count)
    block_k = min(1024, key_count)
    spec_q = pl.BlockSpec((HEAD_DIM, query_count), lambda h: (h, 0))
    spec_k = pl.BlockSpec((HEAD_DIM, key_count), lambda h: (h, 0))
    wide = HEAD_DIM + EXTRA
    return pl.pallas_call(
        functools.partial(backward_kernel, block_q, block_k),
        grid=(heads,),
        in_specs=[
            spec_q,
            spec_k,
            spec_k,
            pl.BlockSpec((EXTRA, key_count), lambda h: (0, 0)),
            spec_q,
            pl.BlockSpec((1, 1, query_count), lambda h: (h, 0, 0)),
            spec_q,
        ],
        out_specs=[spec_q, spec_k, spec_k],
        out_shape=[
            jax.ShapeDtypeStruct((heads * HEAD_DIM, query_count), BF16),
            jax.ShapeDtypeStruct((heads * HEAD_DIM, key_count), BF16),
            jax.ShapeDtypeStruct((heads * HEAD_DIM, key_count), BF16),
        ],
        scratch_shapes=[
            pltpu.VMEM((query_count, wide), BF16),
            pltpu.VMEM((wide, key_count), BF16),
            pltpu.VMEM((query_count, wide), BF16),
            pltpu.VMEM((wide, key_count), BF16),
            pltpu.VMEM((HEAD_DIM, query_count), BF16),
            pltpu.VMEM((HEAD_DIM, query_count), F32),
        ],
        compiler_params=pltpu.CompilerParams(vmem_limit_bytes=VMEM_LIMIT),
        cost_estimate=pl.CostEstimate(
            flops=heads * 40 * HEAD_DIM * query_count * key_count,
            transcendentals=heads * query_count * key_count,
            bytes_accessed=heads * 16 * HEAD_DIM * key_count,
        ),
    )(queries, keys, values, mask_rows, outs, sums, grads)


def norm_apply(residue, gain_row, shift_row):
    center = jnp.mean(residue, axis=-1, keepdims=True)
    centred = residue - center
    spread = jnp.mean(centred * centred, axis=-1, keepdims=True)
    return centred * lax.rsqrt(spread + EPSILON) * gain_row + shift_row


def gelu_exact(pre_act):
    return jax.nn.gelu(pre_act, approximate=False)


def pad_rows(array, count):
    return jnp.concatenate([array, jnp.zeros((count,) + array.shape[1:], array.dtype)])


def local(
    layer_input,
    lengths,
    cotangent,
    w_query,
    b_query,
    w_key,
    w_value,
    b_value,
    w_attn_out,
    b_attn_out,
    norm1_gain,
    norm1_bias,
    w_inner,
    b_inner,
    w_outer,
    b_outer,
    norm2_gain,
    norm2_bias,
):
    seqs, part_rows, width = layer_input.shape
    batches = lax.axis_size("batch")
    planes = lax.axis_size("blk") // CORES
    devices = batches * planes * MEMBERS
    spread_planes = planes // seqs
    piece = part_rows // spread_planes
    row_count = planes * piece
    share = width // devices
    wide_share = w_outer.shape[0]
    hidden = wide_share * devices
    folds = hidden // width
    group = width // MEMBERS

    plane = lax.axis_index("blk") // CORES
    core = lax.axis_index("blk") % CORES
    head_place = lax.axis_index("head")
    batch_place = lax.axis_index("batch")
    device = (batch_place * planes + plane) * MEMBERS + core * 2 + head_place
    seq_length = pick(lengths, plane // spread_planes)
    part = plane % spread_planes

    def places(other_plane):
        source = (other_plane - jnp.arange(planes, dtype=jnp.int32)) % planes
        member = jnp.arange(MEMBERS, dtype=jnp.int32)
        cores = core ^ (member // 2)
        heads = head_place ^ (member % 2)
        base = (source[None, :] * CORES + cores[:, None]) * 2 + heads[:, None]
        offset = (other_plane % spread_planes) * piece + jnp.arange(piece, dtype=jnp.int32)
        return (base[:, :, None] * part_rows + offset).reshape(-1)

    def to_planes(array):
        chunks = array.reshape(planes, piece, width)
        pieces = [pick(chunks, plane)]
        for distance in range(1, planes):
            chunk = pick(chunks, (plane + distance) % planes)
            pieces.append(shift_planes(chunk, distance))
        return pieces

    def from_planes(array):
        pieces = array.reshape(planes, piece, width)
        back = [pieces[0]]
        for distance in range(1, planes):
            back.append(shift_planes(pieces[distance], -distance))
        doubled = jnp.concatenate([jnp.stack(back)] * 2)
        ordered = lax.dynamic_slice_in_dim(doubled, planes - plane, planes, 0)
        return ordered.reshape(seqs, part_rows, width)

    small = jnp.concatenate(
        [b_query, b_value, b_attn_out, norm1_gain, norm1_bias, b_outer, norm2_gain, norm2_bias]
        + [b_inner]
    )
    small_row = jnp.pad(small, (0, width - small.shape[0]))[None]
    first_rows = 3 * share
    first_pack = jnp.concatenate([w_query, w_key, w_value, small_row])
    first_pack = pad_rows(first_pack, -first_pack.shape[0] % 16)
    first = lax.all_gather(first_pack, ALL_AXES, axis=0, tiled=False)
    inner_rows = jnp.swapaxes(w_inner.reshape(share, folds, width), 0, 1).reshape(-1, width)
    second_pack = jnp.concatenate([w_attn_out, inner_rows, w_outer])
    second = lax.all_gather(second_pack, ALL_AXES, axis=0, tiled=False)

    small_all = first[:, first_rows]
    vectors = jnp.swapaxes(small_all[:, : 8 * share].reshape(devices, 8, share), 0, 1)
    vectors = vectors.reshape(8, width).astype(F32)
    bias_query, bias_value, bias_out, gain_first = vectors[:4]
    shift_first, bias_outer, gain_second, shift_second = vectors[4:]
    bias_inner = small_all[:, 8 * share : 8 * share + wide_share].reshape(hidden).astype(F32)

    weights_qkv = [
        first[:, i * share : (i + 1) * share].reshape(width, MEMBERS, group) for i in range(3)
    ]
    by_group = jnp.stack([jnp.moveaxis(weight, 1, 0) for weight in weights_qkv], axis=2)
    by_member = reorder_members(by_group, core, head_place).reshape(MEMBERS, width, 3 * group)
    own_weight = by_member[0]
    own_group = core * 2 + head_place
    own_bias = jnp.concatenate(
        [
            pick(bias_query.reshape(MEMBERS, group), own_group),
            jnp.zeros((group,), F32),
            pick(bias_value.reshape(MEMBERS, group), own_group),
        ]
    )

    own_pieces = to_planes(layer_input)
    head_pieces = [swap_member(part_in, 1) for part_in in own_pieces]
    core_pieces = [swap_member(part_in, 2) for part_in in own_pieces]
    both_pieces = [swap_member(part_in, 2) for part_in in head_pieces]
    rows_own = jnp.concatenate(own_pieces)
    rows_all = jnp.concatenate(own_pieces + head_pieces + core_pieces + both_pieces)

    cot_own = jnp.concatenate(to_planes(cotangent))

    valid_own = places(plane) < seq_length
    row_keep = valid_own[:row_count, None]

    def other_plane(distance):
        return (plane // spread_planes) * spread_planes + (part - distance) % spread_planes

    def shift_parts(array, distance):
        size = lax.axis_size("blk")
        route = []
        for i in range(size):
            start = i // CORES // spread_planes * spread_planes
            target = start + (i // CORES - start + distance) % spread_planes
            route.append((i, target * CORES + i % CORES))
        return lax.ppermute(array, "blk", route)

    qkv = dot(own_weight, rows_all, 0, 1) + own_bias[:, None]
    qkv = qkv.astype(BF16)
    queries, keys, values = qkv[:group], qkv[group : 2 * group], qkv[2 * group :]
    valid_keys = [valid_own]
    if spread_planes > 1:
        more = [shift_parts(qkv[group:], distance) for distance in range(1, spread_planes)]
        keys = jnp.concatenate([keys] + [array[:group] for array in more], axis=1)
        values = jnp.concatenate([values] + [array[group:] for array in more], axis=1)
        for distance in range(1, spread_planes):
            valid_keys.append(places(other_plane(distance)) < seq_length)
    valid = jnp.concatenate(valid_keys)
    mask_row = jnp.where(valid, 0.0, NEG_BIG).astype(BF16)[None]
    mask_rows = pad_rows(mask_row, EXTRA - 1)

    outs, sums = attention_forward(queries, keys, values, mask_rows)

    def to_members(array):
        parts = [array[:, :row_count]]
        for member in range(1, MEMBERS):
            sent = array[:, member * row_count : (member + 1) * row_count]
            parts.append(swap_member(sent, member))
        return parts

    attended = jnp.concatenate(to_members(outs))

    weight_out = second[:, :share].reshape(MEMBERS, group, width)
    weight_out = reorder_members(weight_out, core, head_place).reshape(width, width)
    weight_inner = second[:, share : share + share * folds].reshape(devices, folds, share, width)
    weight_inner = jnp.swapaxes(weight_inner, 1, 2).reshape(width, hidden)
    weight_outer = second[:, share + share * folds :].reshape(hidden, width)

    branch = dot(attended, weight_out, 0, 0) + bias_out
    normed1, back_first = jax.vjp(
        norm_apply, rows_own.astype(F32) + branch, gain_first, shift_first
    )
    normed_low = normed1.astype(BF16)
    inner_pre = dot(normed_low, weight_inner, 1, 0) + bias_inner
    active, back_gelu = jax.vjp(gelu_exact, inner_pre)
    active_low = active.astype(BF16)
    outer_out = dot(active_low, weight_outer, 1, 0) + bias_outer
    final_rows, back_second = jax.vjp(
        norm_apply, normed1 + outer_out, gain_second, shift_second
    )
    output = from_planes(final_rows.astype(BF16))

    grad_final = jnp.where(row_keep, cot_own.astype(F32), 0.0)
    grad_resid2, grad_gain2, grad_shift2 = back_second(grad_final)
    grad_outer = grad_resid2.astype(BF16)
    grad_bias_outer = jnp.sum(grad_outer.astype(F32), axis=0)
    grad_weight_outer = dot(active_low, grad_outer, 0, 0)
    (grad_inner_pre,) = back_gelu(dot(grad_outer, weight_outer, 1, 1))
    grad_inner = grad_inner_pre.astype(BF16)
    grad_bias_inner = jnp.sum(grad_inner.astype(F32), axis=0)
    grad_weight_inner = dot(normed_low, grad_inner, 0, 0)
    grad_normed1 = grad_resid2 + dot(grad_inner, weight_inner, 1, 1)
    grad_resid1, grad_gain1, grad_shift1 = back_first(grad_normed1)
    grad_branch = grad_resid1.astype(BF16)
    grad_bias_out = jnp.sum(grad_branch.astype(F32), axis=0)
    grad_weight_out = dot(attended, grad_branch, 1, 0).astype(BF16)
    grad_weight_out = reorder_members(
        grad_weight_out.reshape(MEMBERS, group, width), core, head_place
    )
    grad_attended = dot(weight_out, grad_branch, 1, 1).astype(BF16)

    vector_grads = [
        grad_bias_out,
        grad_gain1,
        grad_shift1,
        grad_bias_outer,
        grad_gain2,
        grad_shift2,
    ]
    vector_pack = jnp.concatenate(
        [vector.reshape(devices, share) for vector in vector_grads]
        + [grad_bias_inner.reshape(devices, wide_share)],
        axis=1,
    )
    vector_pack = jnp.pad(vector_pack, ((0, 0), (0, width - vector_pack.shape[1])))
    inner_pack = jnp.swapaxes(
        grad_weight_inner.astype(BF16).reshape(devices, share, folds, width), 1, 2
    ).reshape(devices, folds * share, width)
    grad_pack = jnp.concatenate(
        [
            grad_weight_out.reshape(devices, share, width),
            inner_pack,
            grad_weight_outer.astype(BF16).reshape(devices, wide_share, width),
            vector_pack.astype(BF16)[:, None],
        ],
        axis=1,
    )
    grad_pack = jnp.pad(grad_pack, ((0, 0), (0, -grad_pack.shape[1] % 16), (0, 0)))
    owned = lax.psum_scatter(grad_pack, ALL_AXES, scatter_dimension=0, tiled=True)[0].astype(F32)
    owned_out = owned[:share]
    owned_inner = owned[share : share + folds * share].reshape(folds, share, width)
    owned_inner = jnp.swapaxes(owned_inner, 0, 1).reshape(share, hidden)
    outer_start = share + folds * share
    owned_outer = owned[outer_start : outer_start + wide_share]
    owned_vectors = owned[outer_start + wide_share]

    grad_parts = [grad_attended[:group]]
    for member in range(1, MEMBERS):
        sent = grad_attended[member * group : (member + 1) * group]
        grad_parts.append(swap_member(sent, member))
    grad_side = jnp.concatenate(grad_parts, axis=1)
    grad_q, grad_k, grad_v = attention_backward(
        queries, keys, values, mask_rows, outs, sums, grad_side
    )
    if spread_planes > 1:
        grad_kv = jnp.concatenate([grad_k, grad_v])
        plane_rows = MEMBERS * row_count
        total = grad_kv[:, :plane_rows].astype(F32)
        for distance in range(1, spread_planes):
            sent = grad_kv[:, distance * plane_rows : (distance + 1) * plane_rows]
            total = total + shift_parts(sent, -distance).astype(F32)
        grad_k, grad_v = total[:group].astype(BF16), total[group:].astype(BF16)
    grad_qkv = jnp.concatenate([grad_q, grad_k, grad_v])

    grad_rows = jnp.concatenate(to_members(grad_qkv))
    weight_rows = jnp.swapaxes(by_member, 0, 1).reshape(width, MEMBERS * 3 * group)
    grad_input = (grad_resid1 + dot(grad_rows, weight_rows, 0, 1)).astype(BF16)
    input_grad = from_planes(grad_input)

    grad_weight = dot(rows_all, grad_qkv, 0, 1).astype(BF16)
    grad_bias = jnp.sum(grad_qkv.astype(F32), axis=1).astype(BF16)
    chunk_rows = width // (batches * planes)
    extra = -chunk_rows % 16 + 16
    bias_block = jnp.pad(grad_bias[None], ((0, extra - 1), (0, 0)))
    chunks = grad_weight.reshape(batches * planes, chunk_rows, 3 * group)
    bias_blocks = jnp.broadcast_to(bias_block, (batches * planes,) + bias_block.shape)
    chunks = jnp.concatenate([chunks, bias_blocks], axis=1)
    chunks = chunks.reshape((batches, planes) + chunks.shape[1:])
    total = pick(chunks, batch_place).astype(F32)
    for distance in range(1, batches):
        sent = pick(chunks, (batch_place + distance) % batches)
        total = total + shift_batch(sent, distance).astype(F32)
    sending = total.astype(BF16)
    total = pick(total, plane)
    for distance in range(1, planes):
        sent = pick(sending, (plane + distance) % planes)
        total = total + shift_planes(sent, distance).astype(F32)
    bias_total = total[chunk_rows]
    member_rows = total[:chunk_rows].reshape(MEMBERS, share, 3 * group)
    member_rows = reorder_members(member_rows, core, head_place)
    tail = jnp.zeros((MEMBERS, -share % 16 + 16, 3 * group), F32).at[:, 0].set(bias_total)
    sending = jnp.concatenate([member_rows, tail], axis=1)
    bias_at = sending.shape[1] - tail.shape[1]
    got = [sending[0]] + [
        swap_member(sending[member], member) for member in range(1, MEMBERS)
    ]
    got = reorder_members(jnp.stack(got), core, head_place)
    got = got.reshape(MEMBERS, got.shape[1], 3, group)
    matrices = [
        jnp.swapaxes(got[:, :share, i], 0, 1).reshape(share, width) for i in range(3)
    ]
    biases = [
        lax.dynamic_slice_in_dim(got[:, bias_at, i].reshape(width), device * share, share)
        for i in (0, 2)
    ]

    def vector(index):
        return owned_vectors[index * share : (index + 1) * share]

    return (
        output,
        input_grad,
        matrices[0],
        biases[0],
        matrices[1],
        matrices[2],
        biases[1],
        owned_out,
        vector(0),
        vector(1),
        vector(2),
        owned_inner,
        owned_vectors[6 * share : 6 * share + wide_share],
        owned_outer,
        vector(3),
        vector(4),
        vector(5),
    )


def solution(mesh):
    rows = P("batch", ("blk", "head"), None)
    matrix = P(ALL_AXES, None)
    vector = P(ALL_AXES)
    parameters = (
        matrix,
        vector,
        matrix,
        matrix,
        vector,
        matrix,
        vector,
        vector,
        vector,
        matrix,
        vector,
        matrix,
        vector,
        vector,
        vector,
    )
    return jax.shard_map(
        local,
        mesh=mesh,
        in_specs=(rows, P("batch"), rows) + parameters,
        out_specs=(rows, rows) + parameters,
        check_vma=False,
    )
```

```python
import functools
import math

import jax
import jax.numpy as jnp
from jax import lax
from jax.experimental import pallas as pl
from jax.experimental.pallas import tpu as pltpu
from jax.sharding import PartitionSpec as P

HEADS = 12
HEAD_DIM = 64
CORES = 2
MEMBERS = 4
EXTRA = 16
NEG_BIG = -1e30
EPSILON = 1e-06
F32 = jnp.float32
BF16 = jnp.bfloat16
ALL_AXES = ("batch", "blk", "head")
VMEM_LIMIT = 56 * 2**20


def dot(left_op, right_op, left_dim, right_dim):
    return lax.dot_general(
        left_op, right_op, (((left_dim,), (right_dim,)), ((), ())), preferred_element_type=F32
    )


def shift_planes(array, distance):
    size = lax.axis_size("blk")
    route = [(i, (i + CORES * distance) % size) for i in range(size)]
    return lax.ppermute(array, "blk", route)


def shift_batch(array, distance):
    size = lax.axis_size("batch")
    return lax.ppermute(array, "batch", [(i, (i + distance) % size) for i in range(size)])


def swap_member(array, member):
    size = lax.axis_size("blk")
    if member == 1:
        return lax.ppermute(array, "head", [(0, 1), (1, 0)])
    if member == 2:
        return lax.ppermute(array, "blk", [(i, i ^ 1) for i in range(size)])
    route = [(i * 2 + j, (i ^ 1) * 2 + (j ^ 1)) for i in range(size) for j in range(2)]
    return lax.ppermute(array, ("blk", "head"), route)


def pick(array, index):
    return lax.dynamic_index_in_dim(array, index, 0, keepdims=False)


def reorder_members(stack, core, head_place):
    stack = jnp.where(core == 1, jnp.concatenate([stack[2:], stack[:2]]), stack)
    swapped = jnp.stack([stack[1], stack[0], stack[3], stack[2]])
    return jnp.where(head_place == 1, swapped, stack)


def in_order(pieces, place):
    stack = jnp.stack(pieces[::-1] * 2)
    return lax.dynamic_slice_in_dim(stack, len(pieces) - 1 - place, len(pieces), 0)


def forward_kernel(block_q, block_k, q_ref, k_ref, v_ref, mask_ref, out_ref, sums_ref, keys, values):
    key_count = k_ref.shape[1]
    query_count = q_ref.shape[1]
    rows = lax.broadcasted_iota(jnp.int32, (EXTRA, key_count), 0)
    joined = jnp.concatenate([k_ref[...], mask_ref[...]], axis=0)
    keys[...] = joined.astype(F32).T.astype(BF16)
    values[:HEAD_DIM, :] = v_ref[...]
    values[HEAD_DIM:, :] = jnp.where(rows == 0, 1.0, 0.0).astype(BF16)
    rows_q = lax.broadcasted_iota(jnp.int32, (EXTRA, block_q), 0)
    ones_row = jnp.where(rows_q == 0, 1.0, 0.0).astype(BF16)
    scale = 1.0 / math.sqrt(HEAD_DIM)

    def query_block(i, unused):
        q_start = pl.multiple_of(i * block_q, block_q)
        scaled = (q_ref[:, pl.ds(q_start, block_q)].astype(F32) * scale).astype(BF16)
        query = jnp.concatenate([scaled, ones_row], axis=0)

        def key_block(j, carry):
            top, acc = carry
            k_start = pl.multiple_of(j * block_k, block_k)
            scores = dot(keys[pl.ds(k_start, block_k), :], query, 1, 0)
            new_top = jnp.maximum(top, jnp.max(scores, axis=0, keepdims=True))
            probs = jnp.exp(scores - new_top)
            acc = acc * jnp.exp(top - new_top) + dot(
                values[:, pl.ds(k_start, block_k)], probs.astype(BF16), 1, 0
            )
            return new_top, acc

        top, acc = lax.fori_loop(
            0,
            key_count // block_k,
            key_block,
            (
                jnp.full((1, block_q), NEG_BIG, F32),
                jnp.zeros((HEAD_DIM + EXTRA, block_q), F32),
            ),
        )
        total = acc[HEAD_DIM : HEAD_DIM + 1, :]
        out_ref[:, pl.ds(q_start, block_q)] = (acc[:HEAD_DIM, :] / total).astype(BF16)
        sums_ref[:, pl.ds(q_start, block_q)] = top + jnp.log(total)
        return 0

    lax.fori_loop(0, query_count // block_q, query_block, 0)


def attention_forward(queries, keys, values, places, mask_rows):
    query_count = queries.shape[1]
    key_count = keys.shape[1]
    block_q = min(1024, query_count)
    block_k = min(1024, key_count)
    in_specs = [
        pl.BlockSpec((HEAD_DIM, array.shape[1]), functools.partial(lambda at, i: (at, 0), place))
        for array, place in zip((queries, keys, values), places)
    ]
    return pl.pallas_call(
        functools.partial(forward_kernel, block_q, block_k),
        grid=(1,),
        in_specs=in_specs + [pl.BlockSpec((EXTRA, key_count), lambda i: (0, 0))],
        out_specs=[
            pl.BlockSpec((HEAD_DIM, query_count), lambda i: (0, 0)),
            pl.BlockSpec((1, query_count), lambda i: (0, 0)),
        ],
        out_shape=[
            jax.ShapeDtypeStruct((HEAD_DIM, query_count), BF16),
            jax.ShapeDtypeStruct((1, query_count), F32),
        ],
        scratch_shapes=[
            pltpu.VMEM((key_count, HEAD_DIM + EXTRA), BF16),
            pltpu.VMEM((HEAD_DIM + EXTRA, key_count), BF16),
        ],
        compiler_params=pltpu.CompilerParams(vmem_limit_bytes=VMEM_LIMIT),
        cost_estimate=pl.CostEstimate(
            flops=16 * HEAD_DIM * query_count * key_count,
            transcendentals=query_count * key_count,
            bytes_accessed=8 * HEAD_DIM * key_count,
        ),
    )(queries, keys, values, mask_rows)


def split_three(row):
    high = row.astype(BF16)
    rest = row - high.astype(F32)
    middle = rest.astype(BF16)
    low = (rest - middle.astype(F32)).astype(BF16)
    return high.astype(F32), middle.astype(F32), low.astype(F32)


def backward_kernel(
    block_q,
    block_k,
    q_ref,
    k_ref,
    v_ref,
    mask_ref,
    out_ref,
    sums_ref,
    grad_ref,
    grads_out,
    query_rows,
    keys,
    grad_rows,
    values,
    scaled_q,
    dq_acc,
):
    key_count = k_ref.shape[1]
    query_count = q_ref.shape[1]
    scale = 1.0 / math.sqrt(HEAD_DIM)
    places_q = lax.broadcasted_iota(jnp.int32, (EXTRA, query_count), 0)
    places_k = lax.broadcasted_iota(jnp.int32, (EXTRA, key_count), 0)

    def extra_rows(row, fourth):
        high, middle, low = split_three(row)
        rows = jnp.where(
            places_q == 0, high, jnp.where(places_q == 1, middle, jnp.where(places_q == 2, low, 0.0))
        )
        return jnp.where(places_q == 3, fourth, rows).astype(BF16)

    query = (q_ref[...].astype(F32) * scale).astype(BF16)
    scaled_q[...] = query
    grads = grad_ref[...]
    deltas = jnp.sum(grads.astype(F32) * out_ref[...].astype(F32), axis=0, keepdims=True)
    joined_q = jnp.concatenate([query, extra_rows(-sums_ref[...], 1.0)], axis=0)
    query_rows[...] = joined_q.astype(F32).T.astype(BF16)
    joined_g = jnp.concatenate([grads, extra_rows(-deltas, 0.0)], axis=0)
    grad_rows[...] = joined_g.astype(F32).T.astype(BF16)
    ones_rows = jnp.where(places_k < 3, 1.0, 0.0)
    mask_row = mask_ref[0:1, :].astype(F32)
    keys[:HEAD_DIM, :] = k_ref[...]
    keys[HEAD_DIM:, :] = jnp.where(places_k == 3, mask_row, ones_rows).astype(BF16)
    values[:HEAD_DIM, :] = v_ref[...]
    values[HEAD_DIM:, :] = ones_rows.astype(BF16)
    dq_acc[...] = jnp.zeros_like(dq_acc)

    def key_block(j, unused):
        k_start = pl.multiple_of(j * block_k, block_k)
        key_part = keys[:, pl.ds(k_start, block_k)]
        value_part = values[:, pl.ds(k_start, block_k)]
        plain_keys = k_ref[:, pl.ds(k_start, block_k)]

        def query_block(i, carry):
            dk, dv = carry
            q_start = pl.multiple_of(i * block_q, block_q)
            probs = jnp.exp(dot(query_rows[pl.ds(q_start, block_q), :], key_part, 1, 0))
            moved = dot(grad_rows[pl.ds(q_start, block_q), :], value_part, 1, 0)
            grad_scores = (probs * moved).astype(BF16)
            dv = dv + dot(grad_ref[:, pl.ds(q_start, block_q)], probs.astype(BF16), 1, 0)
            dk = dk + dot(scaled_q[:, pl.ds(q_start, block_q)], grad_scores, 1, 0)
            dq_acc[:, pl.ds(q_start, block_q)] += dot(plain_keys, grad_scores, 1, 1)
            return dk, dv

        zeros = jnp.zeros((HEAD_DIM, block_k), F32)
        dk, dv = lax.fori_loop(0, query_count // block_q, query_block, (zeros, zeros))
        grads_out[HEAD_DIM : 2 * HEAD_DIM, pl.ds(k_start, block_k)] = dk.astype(BF16)
        grads_out[2 * HEAD_DIM :, pl.ds(k_start, block_k)] = dv.astype(BF16)
        return 0

    lax.fori_loop(0, key_count // block_k, key_block, 0)
    grads_out[:HEAD_DIM, :query_count] = (dq_acc[...] * scale).astype(BF16)


def attention_backward(queries, keys, values, places, mask_rows, outs, sums, grads):
    query_count = queries.shape[1]
    key_count = keys.shape[1]
    block_q = min(1024, query_count)
    block_k = min(1024, key_count)
    in_specs = [
        pl.BlockSpec((HEAD_DIM, array.shape[1]), functools.partial(lambda at, i: (at, 0), place))
        for array, place in zip((queries, keys, values), places)
    ]
    spec_q = pl.BlockSpec((HEAD_DIM, query_count), lambda i: (0, 0))
    wide = HEAD_DIM + EXTRA
    return pl.pallas_call(
        functools.partial(backward_kernel, block_q, block_k),
        grid=(1,),
        in_specs=in_specs
        + [
            pl.BlockSpec((EXTRA, key_count), lambda i: (0, 0)),
            spec_q,
            pl.BlockSpec((1, query_count), lambda i: (0, 0)),
            spec_q,
        ],
        out_specs=pl.BlockSpec((3 * HEAD_DIM, key_count), lambda i: (0, 0)),
        out_shape=jax.ShapeDtypeStruct((3 * HEAD_DIM, key_count), BF16),
        scratch_shapes=[
            pltpu.VMEM((query_count, wide), BF16),
            pltpu.VMEM((wide, key_count), BF16),
            pltpu.VMEM((query_count, wide), BF16),
            pltpu.VMEM((wide, key_count), BF16),
            pltpu.VMEM((HEAD_DIM, query_count), BF16),
            pltpu.VMEM((HEAD_DIM, query_count), F32),
        ],
        compiler_params=pltpu.CompilerParams(vmem_limit_bytes=VMEM_LIMIT),
        cost_estimate=pl.CostEstimate(
            flops=40 * HEAD_DIM * query_count * key_count,
            transcendentals=query_count * key_count,
            bytes_accessed=16 * HEAD_DIM * key_count,
        ),
    )(queries, keys, values, mask_rows, outs, sums, grads)


def norm_apply(residue, gain_row, shift_row):
    center = jnp.mean(residue, axis=-1, keepdims=True)
    centred = residue - center
    spread = jnp.mean(centred * centred, axis=-1, keepdims=True)
    return centred * lax.rsqrt(spread + EPSILON) * gain_row + shift_row


def gelu_exact(pre_act):
    return jax.nn.gelu(pre_act, approximate=False)


def pad_rows(array, count):
    return jnp.concatenate([array, jnp.zeros((count,) + array.shape[1:], array.dtype)])


def local(
    layer_input,
    lengths,
    cotangent,
    w_query,
    b_query,
    w_key,
    w_value,
    b_value,
    w_attn_out,
    b_attn_out,
    norm1_gain,
    norm1_bias,
    w_inner,
    b_inner,
    w_outer,
    b_outer,
    norm2_gain,
    norm2_bias,
):
    seqs, part_rows, width = layer_input.shape
    batches = lax.axis_size("batch")
    planes = lax.axis_size("blk") // CORES
    devices = batches * planes * MEMBERS
    spread_planes = planes // seqs
    piece = part_rows // spread_planes
    row_count = planes * piece
    share = width // devices
    wide_share = w_outer.shape[0]
    hidden = wide_share * devices
    folds = hidden // width
    group = width // MEMBERS

    plane = lax.axis_index("blk") // CORES
    core = lax.axis_index("blk") % CORES
    head_place = lax.axis_index("head")
    batch_place = lax.axis_index("batch")
    device = (batch_place * planes + plane) * MEMBERS + core * 2 + head_place
    seq_length = pick(lengths, plane // spread_planes)
    part = plane % spread_planes

    def places(other_plane):
        source = (other_plane - jnp.arange(planes, dtype=jnp.int32)) % planes
        member = jnp.arange(MEMBERS, dtype=jnp.int32)
        cores = core ^ (member // 2)
        heads = head_place ^ (member % 2)
        base = (source[None, :] * CORES + cores[:, None]) * 2 + heads[:, None]
        offset = (other_plane % spread_planes) * piece + jnp.arange(piece, dtype=jnp.int32)
        return (base[:, :, None] * part_rows + offset).reshape(-1)

    def to_planes(array):
        chunks = array.reshape(planes, piece, width)
        pieces = [pick(chunks, plane)]
        for distance in range(1, planes):
            chunk = pick(chunks, (plane + distance) % planes)
            pieces.append(shift_planes(chunk, distance))
        return pieces

    def from_planes(array):
        pieces = array.reshape(planes, piece, width)
        back = [pieces[0]]
        for distance in range(1, planes):
            back.append(shift_planes(pieces[distance], -distance))
        doubled = jnp.concatenate([jnp.stack(back)] * 2)
        ordered = lax.dynamic_slice_in_dim(doubled, planes - plane, planes, 0)
        return ordered.reshape(seqs, part_rows, width)

    own_group = core * 2 + head_place
    heads_here = HEADS // MEMBERS
    piece_rows = (share // 8 + 1) * 8
    kinds = jnp.stack([w_query, w_key, w_value], axis=1)
    kinds = kinds.reshape(share, 3, MEMBERS, group)
    by_group = jnp.moveaxis(kinds, 2, 0).reshape(MEMBERS, share, 3 * group)
    bias_row = jnp.pad(jnp.concatenate([b_query, b_value]), (0, 3 * group - 2 * share))
    tail_rows = jnp.pad(bias_row[None], ((0, piece_rows - share - 1), (0, 0)))
    tail_rows = jnp.broadcast_to(tail_rows, (MEMBERS,) + tail_rows.shape)
    by_group = jnp.concatenate([by_group, tail_rows], axis=1)
    by_member = reorder_members(by_group, core, head_place)
    gathered = [by_member[0]] + [
        swap_member(by_member[member], member) for member in range(1, MEMBERS)
    ]
    gathered = reorder_members(jnp.stack(gathered), core, head_place)
    gathered = in_order(
        [gathered] + [shift_planes(gathered, distance) for distance in range(1, planes)], plane
    )
    gathered = in_order(
        [gathered] + [shift_batch(gathered, distance) for distance in range(1, batches)],
        batch_place,
    )
    gathered = gathered.reshape(devices, piece_rows, 3 * group)
    own_weight = gathered[:, :share].reshape(width, 3 * group)
    bias_query = gathered[:, share, :share].reshape(MEMBERS, group)
    bias_value = gathered[:, share, share : 2 * share].reshape(MEMBERS, group)
    own_bias = jnp.concatenate(
        [
            pick(bias_query, own_group),
            jnp.zeros((group,), BF16),
            pick(bias_value, own_group),
        ]
    ).astype(F32)

    own_pieces = to_planes(layer_input)
    head_pieces = [swap_member(part_in, 1) for part_in in own_pieces]
    core_pieces = [swap_member(part_in, 2) for part_in in own_pieces]
    both_pieces = [swap_member(part_in, 2) for part_in in head_pieces]
    rows_own = jnp.concatenate(own_pieces)
    rows_all = jnp.concatenate(own_pieces + head_pieces + core_pieces + both_pieces)

    valid_own = places(plane) < seq_length
    row_keep = valid_own[:row_count, None]

    def other_plane(distance):
        return (plane // spread_planes) * spread_planes + (part - distance) % spread_planes

    def shift_parts(array, distance):
        size = lax.axis_size("blk")
        route = []
        for i in range(size):
            start = i // CORES // spread_planes * spread_planes
            target = start + (i // CORES - start + distance) % spread_planes
            route.append((i, target * CORES + i % CORES))
        return lax.ppermute(array, "blk", route)

    qkv = dot(own_weight, rows_all, 0, 1) + own_bias[:, None]
    qkv = qkv.astype(BF16)
    late_cotangent, late_out, late_inner, late_outer, qkv = lax.optimization_barrier(
        (cotangent, w_attn_out, w_inner, w_outer, qkv)
    )
    cot_own = jnp.concatenate(to_planes(late_cotangent))

    small = jnp.concatenate(
        [b_attn_out, norm1_gain, norm1_bias, b_outer, norm2_gain, norm2_bias, b_inner]
    )
    small_row = jnp.pad(small, (0, width - small.shape[0]))[None]
    inner_rows = jnp.swapaxes(late_inner.reshape(share, folds, width), 0, 1).reshape(-1, width)
    second_pack = jnp.concatenate([late_outer, inner_rows, late_out, small_row])
    second_pack = pad_rows(second_pack, -second_pack.shape[0] % 8)
    second = lax.all_gather(second_pack, ALL_AXES, axis=0, tiled=False)
    slots = jnp.stack([w_query, w_key, w_value], axis=1)
    slots = slots.reshape(share, 3, MEMBERS, heads_here, HEAD_DIM)
    slots = jnp.transpose(slots, (3, 0, 2, 1, 4)).reshape(heads_here * share, width)
    slots, second = lax.optimization_barrier((slots, second))
    third = lax.all_gather(slots, ALL_AXES, axis=0, tiled=False)

    inner_start = wide_share
    out_start = wide_share + share * folds
    small_all = second[:, out_start + share]
    vectors = jnp.swapaxes(small_all[:, : 6 * share].reshape(devices, 6, share), 0, 1)
    vectors = vectors.reshape(6, width).astype(F32)
    bias_out, gain_first, shift_first, bias_outer, gain_second, shift_second = vectors
    bias_inner = small_all[:, 6 * share : 6 * share + wide_share].reshape(hidden).astype(F32)
    weight_out = second[:, out_start : out_start + share].reshape(MEMBERS, group, width)
    weight_out = reorder_members(weight_out, core, head_place).reshape(width, width)
    weight_inner = second[:, inner_start:out_start].reshape(devices, folds, share, width)
    weight_inner = jnp.swapaxes(weight_inner, 1, 2).reshape(width, hidden)
    weight_outer = second[:, :wide_share].reshape(hidden, width)

    queries = keys = values = qkv
    starts = (0, heads_here, 2 * heads_here)
    valid_keys = [valid_own]
    if spread_planes > 1:
        sides = [qkv[group:]]
        for distance in range(1, spread_planes):
            sides.append(shift_parts(qkv[group:], distance))
            valid_keys.append(places(other_plane(distance)) < seq_length)
        keys = values = jnp.concatenate(sides, axis=1)
        starts = (0, 0, heads_here)
    valid = jnp.concatenate(valid_keys)
    mask_row = jnp.where(valid, 0.0, NEG_BIG).astype(BF16)[None]
    mask_rows = pad_rows(mask_row, EXTRA - 1)

    def to_members(array):
        parts = [array[:, :row_count]]
        for member in range(1, MEMBERS):
            sent = array[:, member * row_count : (member + 1) * row_count]
            parts.append(swap_member(sent, member))
        return parts

    outs, sums, parts = [], [], []
    for slot in range(heads_here):
        slot_at = tuple(start + slot for start in starts)
        out, total = attention_forward(queries, keys, values, slot_at, mask_rows)
        outs.append(out)
        sums.append(total)
        parts.append(to_members(out))
    attended = jnp.concatenate(
        [parts[slot][member] for member in range(MEMBERS) for slot in range(heads_here)]
    )

    branch = dot(attended, weight_out, 0, 0) + bias_out
    normed1, back_first = jax.vjp(
        norm_apply, rows_own.astype(F32) + branch, gain_first, shift_first
    )
    normed_low = normed1.astype(BF16)
    inner_pre = dot(normed_low, weight_inner, 1, 0) + bias_inner
    active, back_gelu = jax.vjp(gelu_exact, inner_pre)
    active_low = active.astype(BF16)
    outer_out = dot(active_low, weight_outer, 1, 0) + bias_outer
    final_rows, back_second = jax.vjp(
        norm_apply, normed1 + outer_out, gain_second, shift_second
    )
    output = from_planes(final_rows.astype(BF16))

    grad_final = jnp.where(row_keep, cot_own.astype(F32), 0.0)
    grad_resid2, grad_gain2, grad_shift2 = back_second(grad_final)
    grad_outer = grad_resid2.astype(BF16)
    grad_bias_outer = jnp.sum(grad_outer.astype(F32), axis=0)
    grad_weight_outer = dot(active_low, grad_outer, 0, 0)
    (grad_inner_pre,) = back_gelu(dot(grad_outer, weight_outer, 1, 1))
    grad_inner = grad_inner_pre.astype(BF16)
    grad_bias_inner = jnp.sum(grad_inner.astype(F32), axis=0)
    grad_weight_inner = dot(normed_low, grad_inner, 0, 0)
    grad_normed1 = grad_resid2 + dot(grad_inner, weight_inner, 1, 1)
    grad_resid1, grad_gain1, grad_shift1 = back_first(grad_normed1)
    grad_branch = grad_resid1.astype(BF16)
    grad_bias_out = jnp.sum(grad_branch.astype(F32), axis=0)
    grad_weight_out = dot(attended, grad_branch, 1, 0).astype(BF16)
    grad_weight_out = reorder_members(
        grad_weight_out.reshape(MEMBERS, group, width), core, head_place
    )
    grad_attended = dot(weight_out, grad_branch, 1, 1).astype(BF16)

    vector_grads = [
        grad_bias_out,
        grad_gain1,
        grad_shift1,
        grad_bias_outer,
        grad_gain2,
        grad_shift2,
    ]
    vector_pack = jnp.concatenate(
        [vector.reshape(devices, share) for vector in vector_grads]
        + [grad_bias_inner.reshape(devices, wide_share)],
        axis=1,
    )
    vector_pack = jnp.pad(vector_pack, ((0, 0), (0, width - vector_pack.shape[1])))
    inner_pack = jnp.swapaxes(
        grad_weight_inner.astype(BF16).reshape(devices, share, folds, width), 1, 2
    ).reshape(devices, folds * share, width)
    grad_pack = jnp.concatenate(
        [
            grad_weight_outer.astype(BF16).reshape(devices, wide_share, width),
            inner_pack,
            grad_weight_out.reshape(devices, share, width),
            vector_pack.astype(BF16)[:, None],
        ],
        axis=1,
    )
    grad_pack = jnp.pad(grad_pack, ((0, 0), (0, -grad_pack.shape[1] % 16), (0, 0)))
    owned = lax.psum_scatter(grad_pack, ALL_AXES, scatter_dimension=0, tiled=True)[0].astype(F32)
    owned_outer = owned[:wide_share]
    owned_inner = owned[inner_start:out_start].reshape(folds, share, width)
    owned_inner = jnp.swapaxes(owned_inner, 0, 1).reshape(share, hidden)
    owned_out = owned[out_start : out_start + share]
    owned_vectors = owned[out_start + share]

    chunk_rows = width // (batches * planes)
    extra = -chunk_rows % 16 + 16

    def reduce_weights(slot_grads):
        columns = slot_grads.shape[0]
        grad_weight = dot(slot_grads, rows_all, 1, 0).T.astype(BF16)
        grad_bias = jnp.sum(slot_grads.astype(F32), axis=1).astype(BF16)
        bias_block = jnp.pad(grad_bias[None], ((0, extra - 1), (0, 0)))
        chunks = grad_weight.reshape(batches * planes, chunk_rows, columns)
        bias_blocks = jnp.broadcast_to(bias_block, (batches * planes,) + bias_block.shape)
        chunks = jnp.concatenate([chunks, bias_blocks], axis=1)
        return chunks.reshape((batches, planes) + chunks.shape[1:])

    def finish_weights(chunks):
        columns = chunks.shape[-1]
        total = pick(chunks, batch_place).astype(F32)
        for distance in range(1, batches):
            sent = pick(chunks, (batch_place + distance) % batches)
            total = total + shift_batch(sent, distance).astype(F32)
        sending = total.astype(BF16)
        total = pick(total, plane)
        for distance in range(1, planes):
            sent = pick(sending, (plane + distance) % planes)
            total = total + shift_planes(sent, distance).astype(F32)
        bias_total = total[chunk_rows]
        member_rows = total[:chunk_rows].reshape(MEMBERS, share, columns)
        member_rows = reorder_members(member_rows, core, head_place)
        tail = jnp.broadcast_to(bias_total, (MEMBERS, piece_rows - share, columns))
        sending = jnp.concatenate([member_rows, tail], axis=1)
        got = [sending[0]] + [
            swap_member(sending[member], member) for member in range(1, MEMBERS)
        ]
        got = reorder_members(jnp.stack(got), core, head_place)
        return got.reshape(MEMBERS, piece_rows, columns // (3 * HEAD_DIM), 3, HEAD_DIM)

    plane_rows = MEMBERS * row_count
    slot_grads = []
    grad_input = grad_resid1
    early = None
    for slot in range(heads_here):
        grad_parts = []
        for member in range(MEMBERS):
            start = member * group + slot * HEAD_DIM
            sent = grad_attended[start : start + HEAD_DIM]
            grad_parts.append(swap_member(sent, member) if member else sent)
        grad_side = jnp.concatenate(grad_parts, axis=1)
        if slot == heads_here - 1:
            early = reduce_weights(jnp.concatenate(slot_grads))
            early, grad_side, grad_input = lax.optimization_barrier(
                (early, grad_side, grad_input)
            )
        slot_at = tuple(start + slot for start in starts)
        grads = attention_backward(
            queries, keys, values, slot_at, mask_rows, outs[slot], sums[slot], grad_side
        )
        if spread_planes > 1:
            total = grads[HEAD_DIM:, :plane_rows].astype(F32)
            for distance in range(1, spread_planes):
                sent = grads[HEAD_DIM:, distance * plane_rows : (distance + 1) * plane_rows]
                total = total + shift_parts(sent, -distance).astype(F32)
            grads = jnp.concatenate([grads[:HEAD_DIM, :plane_rows], total.astype(BF16)])
        slot_grads.append(grads)
        arrived = reorder_members(jnp.stack(to_members(grads)), core, head_place)
        slot_weight = third[:, slot * share : (slot + 1) * share].reshape(width, width)
        grad_input = grad_input + dot(arrived.reshape(width, row_count), slot_weight, 0, 1)
    input_grad = from_planes(grad_input.astype(BF16))

    got = jnp.concatenate(
        [finish_weights(early), finish_weights(reduce_weights(slot_grads[-1]))], axis=2
    )
    matrices = [
        jnp.swapaxes(got[:, :share, :, i], 0, 1).reshape(share, width) for i in range(3)
    ]
    biases = [
        lax.dynamic_slice_in_dim(got[:, share, :, i].reshape(width), device * share, share)
        for i in (0, 2)
    ]

    def vector(index):
        return owned_vectors[index * share : (index + 1) * share]

    return (
        output,
        input_grad,
        matrices[0],
        biases[0],
        matrices[1],
        matrices[2],
        biases[1],
        owned_out,
        vector(0),
        vector(1),
        vector(2),
        owned_inner,
        owned_vectors[6 * share : 6 * share + wide_share],
        owned_outer,
        vector(3),
        vector(4),
        vector(5),
    )


def solution(mesh):
    rows = P("batch", ("blk", "head"), None)
    matrix = P(ALL_AXES, None)
    vector = P(ALL_AXES)
    parameters = (
        matrix,
        vector,
        matrix,
        matrix,
        vector,
        matrix,
        vector,
        vector,
        vector,
        matrix,
        vector,
        matrix,
        vector,
        vector,
        vector,
    )
    return jax.shard_map(
        local,
        mesh=mesh,
        in_specs=(rows, P("batch"), rows) + parameters,
        out_specs=(rows, rows) + parameters,
        check_vma=False,
    )
```

```python
import functools
import math

import jax
import jax.numpy as jnp
from jax import lax
from jax.experimental import pallas as pl
from jax.experimental.pallas import tpu as pltpu
from jax.sharding import PartitionSpec as P

HEADS = 12
HEAD_DIM = 64
CORES = 2
MEMBERS = 4
EXTRA = 16
NEG_BIG = -1e30
EPSILON = 1e-06
F32 = jnp.float32
BF16 = jnp.bfloat16
ALL_AXES = ("batch", "blk", "head")
VMEM_LIMIT = 56 * 2**20
LAYER_VMEM = 60 * 2**20


def dot(left_op, right_op, left_dim, right_dim):
    return lax.dot_general(
        left_op, right_op, (((left_dim,), (right_dim,)), ((), ())), preferred_element_type=F32
    )


def shift_planes(array, distance):
    size = lax.axis_size("blk")
    route = [(i, (i + CORES * distance) % size) for i in range(size)]
    return lax.ppermute(array, "blk", route)


def shift_batch(array, distance):
    size = lax.axis_size("batch")
    return lax.ppermute(array, "batch", [(i, (i + distance) % size) for i in range(size)])


def swap_member(array, member):
    size = lax.axis_size("blk")
    if member == 1:
        return lax.ppermute(array, "head", [(0, 1), (1, 0)])
    if member == 2:
        return lax.ppermute(array, "blk", [(i, i ^ 1) for i in range(size)])
    route = [(i * 2 + j, (i ^ 1) * 2 + (j ^ 1)) for i in range(size) for j in range(2)]
    return lax.ppermute(array, ("blk", "head"), route)


def pick(array, index):
    return lax.dynamic_index_in_dim(array, index, 0, keepdims=False)


def reorder_members(stack, core, head_place):
    stack = jnp.where(core == 1, jnp.concatenate([stack[2:], stack[:2]]), stack)
    swapped = jnp.stack([stack[1], stack[0], stack[3], stack[2]])
    return jnp.where(head_place == 1, swapped, stack)


def in_order(pieces, place):
    stack = jnp.stack(pieces[::-1] * 2)
    return lax.dynamic_slice_in_dim(stack, len(pieces) - 1 - place, len(pieces), 0)


def forward_kernel(block_k, q_ref, k_ref, v_ref, mask_ref, *rest):
    out_refs, (sums_ref, keys, values) = rest[:MEMBERS], rest[MEMBERS:]
    key_count = k_ref.shape[1]
    block_q = q_ref.shape[1] // MEMBERS
    rows = lax.broadcasted_iota(jnp.int32, (EXTRA, key_count), 0)
    joined = jnp.concatenate([k_ref[...], mask_ref[...]], axis=0)
    keys[...] = joined.astype(F32).T.astype(BF16)
    values[:HEAD_DIM, :] = v_ref[...]
    values[HEAD_DIM:, :] = jnp.where(rows == 0, 1.0, 0.0).astype(BF16)
    rows_q = lax.broadcasted_iota(jnp.int32, (EXTRA, block_q), 0)
    ones_row = jnp.where(rows_q == 0, 1.0, 0.0).astype(BF16)
    scale = 1.0 / math.sqrt(HEAD_DIM)

    for member in range(MEMBERS):
        q_places = pl.ds(member * block_q, block_q)
        scaled = (q_ref[:, q_places].astype(F32) * scale).astype(BF16)
        query = jnp.concatenate([scaled, ones_row], axis=0)

        def key_block(j, carry):
            top, acc = carry
            k_start = pl.multiple_of(j * block_k, block_k)
            scores = dot(keys[pl.ds(k_start, block_k), :], query, 1, 0)
            new_top = jnp.maximum(top, jnp.max(scores, axis=0, keepdims=True))
            probs = jnp.exp(scores - new_top)
            acc = acc * jnp.exp(top - new_top) + dot(
                values[:, pl.ds(k_start, block_k)], probs.astype(BF16), 1, 0
            )
            return new_top, acc

        top, acc = lax.fori_loop(
            0,
            key_count // block_k,
            key_block,
            (
                jnp.full((1, block_q), NEG_BIG, F32),
                jnp.zeros((HEAD_DIM + EXTRA, block_q), F32),
            ),
        )
        total = acc[HEAD_DIM : HEAD_DIM + 1, :]
        out_refs[member][...] = (acc[:HEAD_DIM, :] / total).astype(BF16)
        sums_ref[:, q_places] = top + jnp.log(total)


def head_specs(arrays, places):
    return [
        pl.BlockSpec((HEAD_DIM, array.shape[1]), functools.partial(lambda at, i: (at, 0), place))
        for array, place in zip(arrays, places)
    ]


def whole(shape):
    return pl.BlockSpec(shape, lambda *unused: (0,) * len(shape))


def attention_forward(queries, keys, values, places, mask_rows):
    query_count = queries.shape[1]
    key_count = keys.shape[1]
    part = (HEAD_DIM, query_count // MEMBERS)
    result = pl.pallas_call(
        functools.partial(forward_kernel, min(1024, key_count)),
        grid=(1,),
        in_specs=head_specs((queries, keys, values), places) + [whole((EXTRA, key_count))],
        out_specs=[whole(part)] * MEMBERS + [whole((1, query_count))],
        out_shape=[jax.ShapeDtypeStruct(part, BF16)] * MEMBERS
        + [jax.ShapeDtypeStruct((1, query_count), F32)],
        scratch_shapes=[
            pltpu.VMEM((key_count, HEAD_DIM + EXTRA), BF16),
            pltpu.VMEM((HEAD_DIM + EXTRA, key_count), BF16),
        ],
        compiler_params=pltpu.CompilerParams(vmem_limit_bytes=VMEM_LIMIT),
        cost_estimate=pl.CostEstimate(
            flops=16 * HEAD_DIM * query_count * key_count,
            transcendentals=query_count * key_count,
            bytes_accessed=8 * HEAD_DIM * key_count,
        ),
    )(queries, keys, values, mask_rows)
    return result[:MEMBERS], result[MEMBERS]


def split_three(row):
    high = row.astype(BF16)
    rest = row - high.astype(F32)
    middle = rest.astype(BF16)
    low = (rest - middle.astype(F32)).astype(BF16)
    return high.astype(F32), middle.astype(F32), low.astype(F32)


def backward_kernel(block_q, block_k, pieces, q_ref, k_ref, v_ref, mask_ref, sums_ref, *rest):
    out_refs, rest = rest[:MEMBERS], rest[MEMBERS:]
    grad_refs, rest = rest[:MEMBERS], rest[MEMBERS:]
    result_refs, rest = rest[:pieces], rest[pieces:]
    query_rows, keys, grad_rows, values, scaled_q, grads, dq_acc, dkv = rest
    key_count = k_ref.shape[1]
    query_count = q_ref.shape[1]
    part = query_count // MEMBERS
    scale = 1.0 / math.sqrt(HEAD_DIM)
    places_q = lax.broadcasted_iota(jnp.int32, (EXTRA, query_count), 0)
    places_k = lax.broadcasted_iota(jnp.int32, (EXTRA, key_count), 0)

    def extra_rows(row, fourth):
        high, middle, low = split_three(row)
        rows = jnp.where(
            places_q == 0, high, jnp.where(places_q == 1, middle, jnp.where(places_q == 2, low, 0.0))
        )
        return jnp.where(places_q == 3, fourth, rows).astype(BF16)

    query = (q_ref[...].astype(F32) * scale).astype(BF16)
    scaled_q[...] = query
    deltas = []
    for member in range(MEMBERS):
        grad = grad_refs[member][...]
        grads[:, member * part : (member + 1) * part] = grad
        product = grad.astype(F32) * out_refs[member][...].astype(F32)
        deltas.append(jnp.sum(product, axis=0, keepdims=True))
    deltas = jnp.concatenate(deltas, axis=1)
    joined_q = jnp.concatenate([query, extra_rows(-sums_ref[...], 1.0)], axis=0)
    query_rows[...] = joined_q.astype(F32).T.astype(BF16)
    joined_g = jnp.concatenate([grads[...], extra_rows(-deltas, 0.0)], axis=0)
    grad_rows[...] = joined_g.astype(F32).T.astype(BF16)
    ones_rows = jnp.where(places_k < 3, 1.0, 0.0)
    mask_row = mask_ref[0:1, :].astype(F32)
    keys[:HEAD_DIM, :] = k_ref[...]
    keys[HEAD_DIM:, :] = jnp.where(places_k == 3, mask_row, ones_rows).astype(BF16)
    values[:HEAD_DIM, :] = v_ref[...]
    values[HEAD_DIM:, :] = ones_rows.astype(BF16)
    dq_acc[...] = jnp.zeros_like(dq_acc)

    def key_block(j, unused):
        k_start = pl.multiple_of(j * block_k, block_k)
        key_part = keys[:, pl.ds(k_start, block_k)]
        value_part = values[:, pl.ds(k_start, block_k)]
        plain_keys = k_ref[:, pl.ds(k_start, block_k)]

        def query_block(i, carry):
            dk, dv = carry
            q_start = pl.multiple_of(i * block_q, block_q)
            probs = jnp.exp(dot(query_rows[pl.ds(q_start, block_q), :], key_part, 1, 0))
            moved = dot(grad_rows[pl.ds(q_start, block_q), :], value_part, 1, 0)
            grad_scores = (probs * moved).astype(BF16)
            dv = dv + dot(grads[:, pl.ds(q_start, block_q)], probs.astype(BF16), 1, 0)
            dk = dk + dot(scaled_q[:, pl.ds(q_start, block_q)], grad_scores, 1, 0)
            dq_acc[:, pl.ds(q_start, block_q)] += dot(plain_keys, grad_scores, 1, 1)
            return dk, dv

        zeros = jnp.zeros((HEAD_DIM, block_k), F32)
        dk, dv = lax.fori_loop(0, query_count // block_q, query_block, (zeros, zeros))
        dkv[:HEAD_DIM, pl.ds(k_start, block_k)] = dk.astype(BF16)
        dkv[HEAD_DIM:, pl.ds(k_start, block_k)] = dv.astype(BF16)
        return 0

    lax.fori_loop(0, key_count // block_k, key_block, 0)
    for index, result_ref in enumerate(result_refs):
        lanes = slice(index * part, (index + 1) * part)
        if index < MEMBERS:
            result_ref[:HEAD_DIM, :] = (dq_acc[:, lanes] * scale).astype(BF16)
        else:
            result_ref[:HEAD_DIM, :] = jnp.zeros((HEAD_DIM, part), BF16)
        result_ref[HEAD_DIM:, :] = dkv[:, lanes]


def attention_backward(queries, keys, values, places, mask_rows, sums, outs, grads):
    query_count = queries.shape[1]
    key_count = keys.shape[1]
    part = query_count // MEMBERS
    pieces = key_count // part
    wide = HEAD_DIM + EXTRA
    return pl.pallas_call(
        functools.partial(
            backward_kernel, min(1024, query_count), min(1024, key_count), pieces
        ),
        grid=(1,),
        in_specs=head_specs((queries, keys, values), places)
        + [whole((EXTRA, key_count)), whole((1, query_count))]
        + [whole((HEAD_DIM, part))] * (2 * MEMBERS),
        out_specs=[whole((3 * HEAD_DIM, part))] * pieces,
        out_shape=[jax.ShapeDtypeStruct((3 * HEAD_DIM, part), BF16)] * pieces,
        scratch_shapes=[
            pltpu.VMEM((query_count, wide), BF16),
            pltpu.VMEM((wide, key_count), BF16),
            pltpu.VMEM((query_count, wide), BF16),
            pltpu.VMEM((wide, key_count), BF16),
            pltpu.VMEM((HEAD_DIM, query_count), BF16),
            pltpu.VMEM((HEAD_DIM, query_count), BF16),
            pltpu.VMEM((HEAD_DIM, query_count), F32),
            pltpu.VMEM((2 * HEAD_DIM, key_count), BF16),
        ],
        compiler_params=pltpu.CompilerParams(vmem_limit_bytes=VMEM_LIMIT),
        cost_estimate=pl.CostEstimate(
            flops=40 * HEAD_DIM * query_count * key_count,
            transcendentals=query_count * key_count,
            bytes_accessed=16 * HEAD_DIM * key_count,
        ),
    )(queries, keys, values, mask_rows, sums, *outs, *grads)


def project_kernel(count, weight_ref, bias_ref, *rest):
    piece_refs, (all_ref, out_ref) = rest[:count], rest[count:]
    rows = piece_refs[0].shape[0]
    for index, piece_ref in enumerate(piece_refs):
        all_ref[index * rows : (index + 1) * rows, :] = piece_ref[...]
    weight = weight_ref[...].astype(F32).T.astype(BF16)
    step = all_ref.shape[0] // MEMBERS
    for member in range(MEMBERS):
        lanes = slice(member * step, (member + 1) * step)
        out_ref[:, lanes] = (dot(weight, all_ref[lanes, :], 1, 1) + bias_ref[...]).astype(BF16)


def project(weight, bias_column, pieces):
    count, (rows, width) = len(pieces), pieces[0].shape
    columns = weight.shape[1]
    return pl.pallas_call(
        functools.partial(project_kernel, count),
        grid=(1,),
        in_specs=[whole(weight.shape), whole(bias_column.shape)] + [whole((rows, width))] * count,
        out_specs=[whole((count * rows, width)), whole((columns, count * rows))],
        out_shape=[
            jax.ShapeDtypeStruct((count * rows, width), BF16),
            jax.ShapeDtypeStruct((columns, count * rows), BF16),
        ],
        compiler_params=pltpu.CompilerParams(vmem_limit_bytes=VMEM_LIMIT),
        cost_estimate=pl.CostEstimate(
            flops=2 * count * rows * width * columns,
            transcendentals=0,
            bytes_accessed=6 * count * rows * width,
        ),
    )(weight, bias_column, *pieces)


def weight_grad_kernel(slots, chunks, chunk_rows, rows_ref, *rest):
    grad_refs, out_ref = rest[:-1], rest[-1]
    part = grad_refs[0].shape[1]
    columns = grad_refs[0].shape[0]
    ones = jnp.ones((8, part), BF16)
    for slot in range(slots):
        lanes = slice(slot * columns, (slot + 1) * columns)
        total, bias = 0.0, 0.0
        for member in range(MEMBERS):
            grad = grad_refs[slot * MEMBERS + member][...]
            total = total + dot(grad, rows_ref[member * part : (member + 1) * part, :], 1, 0)
            bias = bias + dot(ones, grad, 1, 1)
        turned = total.T.astype(BF16)
        bias = jnp.broadcast_to(bias[0:1].astype(BF16), (out_ref.shape[1] - chunk_rows, columns))
        for chunk in range(chunks):
            out_ref[chunk, :chunk_rows, lanes] = turned[chunk * chunk_rows : (chunk + 1) * chunk_rows]
            out_ref[chunk, chunk_rows:, lanes] = bias


def weight_grad(rows_all, slot_pieces, chunks, chunk_rows, block_rows):
    slots = len(slot_pieces)
    columns, part = slot_pieces[0][0].shape
    shape = (chunks, block_rows, slots * columns)
    return pl.pallas_call(
        functools.partial(weight_grad_kernel, slots, chunks, chunk_rows),
        grid=(1,),
        in_specs=[whole(rows_all.shape)] + [whole((columns, part))] * (slots * MEMBERS),
        out_specs=whole(shape),
        out_shape=jax.ShapeDtypeStruct(shape, BF16),
        compiler_params=pltpu.CompilerParams(vmem_limit_bytes=VMEM_LIMIT),
        cost_estimate=pl.CostEstimate(
            flops=2 * slots * columns * rows_all.size,
            transcendentals=0,
            bytes_accessed=2 * rows_all.size,
        ),
    )(rows_all, *[piece for pieces in slot_pieces for piece in pieces])


def input_grad_kernel(last, info_ref, acc_ref, weight_ref, *rest):
    piece_refs, out_refs, joined = rest[:MEMBERS], rest[MEMBERS:-1], rest[-1]
    columns = piece_refs[0].shape[0]
    for member in range(MEMBERS):
        start = pl.multiple_of(info_ref[member], HEAD_DIM)
        joined[pl.ds(start, columns), :] = piece_refs[member][...]
    rows = acc_ref.shape[0] // len(out_refs)
    total = acc_ref[...] + dot(joined[...], weight_ref[...], 0, 1)
    for index, out_ref in enumerate(out_refs):
        out_ref[...] = total[index * rows : (index + 1) * rows].astype(out_ref.dtype)


def input_grad_step(info, acc, weight, pieces, out_count, dtype):
    columns, part = pieces[0].shape
    rows, width = acc.shape
    out = (rows // out_count, width)
    return pl.pallas_call(
        functools.partial(input_grad_kernel, out_count),
        grid_spec=pltpu.PrefetchScalarGridSpec(
            num_scalar_prefetch=1,
            grid=(1,),
            in_specs=[whole(acc.shape), whole(weight.shape)] + [whole((columns, part))] * MEMBERS,
            out_specs=[whole(out)] * out_count,
            scratch_shapes=[pltpu.VMEM((MEMBERS * columns, part), BF16)],
        ),
        out_shape=[jax.ShapeDtypeStruct(out, dtype)] * out_count,
        compiler_params=pltpu.CompilerParams(vmem_limit_bytes=VMEM_LIMIT),
        cost_estimate=pl.CostEstimate(
            flops=2 * rows * width * MEMBERS * columns,
            transcendentals=0,
            bytes_accessed=8 * rows * width,
        ),
    )(info, acc, weight, *pieces)


def collect_kernel(count, place_ref, *rest):
    piece_refs, out_ref = rest[:count], rest[count]
    for index, piece_ref in enumerate(piece_refs):
        out_ref[lax.rem(place_ref[0] + index, count)] = piece_ref[...]


def collect(pieces, place):
    count, shape = len(pieces), pieces[0].shape
    return pl.pallas_call(
        functools.partial(collect_kernel, count),
        grid_spec=pltpu.PrefetchScalarGridSpec(
            num_scalar_prefetch=1,
            grid=(1,),
            in_specs=[whole(shape)] * count,
            out_specs=whole((count,) + shape),
        ),
        out_shape=jax.ShapeDtypeStruct((count,) + shape, pieces[0].dtype),
        compiler_params=pltpu.CompilerParams(vmem_limit_bytes=VMEM_LIMIT),
    )(place[None], *pieces)


def gelu_parts(value):
    size = jnp.abs(value) * math.sqrt(0.5)
    t = 1.0 / (1.0 + 0.3275911 * size)
    bell = jnp.exp(-0.5 * value * value)
    poly = 1.061405429 * t - 1.453152027
    poly = poly * t + 1.421413741
    poly = poly * t - 0.284496736
    poly = poly * t + 0.254829592
    tail = 0.5 * poly * t * bell
    share = jnp.where(value < 0, tail, 1.0 - tail)
    return value * share, share + value * bell * (1.0 / math.sqrt(2.0 * math.pi))


def row_mean(array):
    return jnp.mean(array, axis=-1, keepdims=True)


def column_sum(array):
    return jnp.sum(array, axis=0, keepdims=True)


def layer_kernel(blocks, planes, parts, info_ref, rows_ref, vectors_ref, inner_bias_ref, *rest):
    weight_out, weight_inner, weight_outer = rest[:3]
    att_refs, rest = rest[3 : 3 + parts], rest[3 + parts :]
    cot_refs, rest = rest[:planes], rest[planes:]
    final_refs, rest = rest[:planes], rest[planes:]
    grad_att_refs, rest = rest[:parts], rest[parts:]
    resid_ref, grad_outer_w, grad_inner_w, grad_out_w, grad_vectors, grad_inner_bias = rest[:6]
    attended, hat1, scale1, low, acc, active, slope, grad_low, grad_hidden = rest[6:]
    step = pl.program_id(0)
    row_count, width = rows_ref.shape
    piece = row_count // planes
    group = width // MEMBERS
    block = jnp.where(step < blocks, step, step - blocks)
    pieces = [slice(k * piece, (k + 1) * piece) for k in range(planes)]

    def group_rows(member):
        return pl.ds(pl.multiple_of(info_ref[member], HEAD_DIM), group)

    def vector(index):
        return vectors_ref[index : index + 1, :]

    @pl.when(step == 0)
    def _():
        for index, att_ref in enumerate(att_refs):
            attended[index * HEAD_DIM : (index + 1) * HEAD_DIM, :] = att_ref[...]
        weight = jnp.concatenate([weight_out[group_rows(m), :] for m in range(MEMBERS)])
        for k in range(planes):
            branch = dot(attended[:, pieces[k]], weight, 0, 0) + vector(0)
            value = rows_ref[pieces[k], :].astype(F32) + branch
            centred = value - row_mean(value)
            scale = lax.rsqrt(row_mean(centred * centred) + EPSILON)
            hat = centred * scale
            normed = hat * vector(1) + vector(2)
            hat1[pieces[k], :] = hat
            scale1[pieces[k], :] = scale
            low[pieces[k], :] = normed.astype(BF16)
            acc[pieces[k], :] = normed + vector(3)
        grad_vectors[...] = jnp.zeros_like(grad_vectors)
        grad_inner_bias[...] = jnp.zeros_like(grad_inner_bias)

    @pl.when(step < blocks)
    def _():
        bias = inner_bias_ref[pl.ds(block, 1), :]
        for k in range(planes):
            inner = dot(low[pieces[k], :], weight_inner[...], 1, 0) + bias
            value, derivative = gelu_parts(inner)
            value = value.astype(BF16)
            active[block, pieces[k], :] = value
            slope[block, pieces[k], :] = derivative
            acc[pieces[k], :] += dot(value, weight_outer[...], 1, 0)

    @pl.when(step == blocks)
    def _():
        gain_sum, shift_sum, bias_sum = 0.0, 0.0, 0.0
        for k in range(planes):
            value = acc[pieces[k], :]
            centred = value - row_mean(value)
            scale = lax.rsqrt(row_mean(centred * centred) + EPSILON)
            hat = centred * scale
            final_refs[k][...] = (hat * vector(4) + vector(5)).astype(BF16)
            places = lax.broadcasted_iota(jnp.int32, (piece, width), 0)
            grad = jnp.where(
                places < info_ref[MEMBERS + k], cot_refs[k][...].astype(F32), 0.0
            )
            gain_sum += column_sum(grad * hat)
            shift_sum += column_sum(grad)
            grad = grad * vector(4)
            grad = scale * (grad - row_mean(grad) - hat * row_mean(grad * hat))
            rounded = grad.astype(BF16)
            bias_sum += column_sum(rounded.astype(F32))
            grad_low[pieces[k], :] = rounded
            acc[pieces[k], :] = grad
        grad_vectors[3:4, :] = bias_sum
        grad_vectors[4:5, :] = gain_sum
        grad_vectors[5:6, :] = shift_sum

    @pl.when(step >= blocks)
    def _():
        bias_sum = 0.0
        for k in range(planes):
            moved = dot(grad_low[pieces[k], :], weight_outer[...], 1, 1)
            grad = (moved * slope[block, pieces[k], :]).astype(BF16)
            grad_hidden[pieces[k], :] = grad
            bias_sum += column_sum(grad.astype(F32))
            acc[pieces[k], :] += dot(grad, weight_inner[...], 1, 1)
        grad_inner_bias[pl.ds(block, 1), :] = bias_sum
        for m in range(MEMBERS // 2):
            lanes = slice(m * 2 * group, (m + 1) * 2 * group)
            grad_outer_w[lanes, :] = dot(active[block, :, lanes], grad_low[...], 0, 0).astype(BF16)
            grad_inner_w[lanes, :] = dot(low[:, lanes], grad_hidden[...], 0, 0).astype(BF16)

    @pl.when(step == 2 * blocks - 1)
    def _():
        gain_sum, shift_sum, bias_sum = 0.0, 0.0, 0.0
        for k in range(planes):
            grad, hat = acc[pieces[k], :], hat1[pieces[k], :]
            gain_sum += column_sum(grad * hat)
            shift_sum += column_sum(grad)
            grad = grad * vector(1)
            grad = scale1[pieces[k], :] * (grad - row_mean(grad) - hat * row_mean(grad * hat))
            resid_ref[pieces[k], :] = grad
            rounded = grad.astype(BF16)
            bias_sum += column_sum(rounded.astype(F32))
            grad_low[pieces[k], :] = rounded
        grad_vectors[0:1, :] = bias_sum
        grad_vectors[1:2, :] = gain_sum
        grad_vectors[2:3, :] = shift_sum
        heads = group // HEAD_DIM
        for m in range(MEMBERS):
            rows = slice(m * group, (m + 1) * group)
            grad_out_w[group_rows(m), :] = dot(attended[rows, :], grad_low[...], 1, 0).astype(BF16)
            moved = dot(weight_out[group_rows(m), :], grad_low[...], 1, 1).astype(BF16)
            for j in range(heads):
                grad_att_refs[m * heads + j][...] = moved[j * HEAD_DIM : (j + 1) * HEAD_DIM, :]


def layer_rows(info, rows_all, vectors, inner_bias, weights, att_parts, cot_pieces):
    weight_out, weight_inner, weight_outer = weights
    hidden, width = weight_outer.shape
    blocks, planes, parts = hidden // width, len(cot_pieces), len(att_parts)
    row_count = att_parts[0].shape[1]
    piece = row_count // planes
    once = pl.Buffered(1)

    def fixed(shape):
        return pl.BlockSpec(shape, lambda *unused: (0,) * len(shape), pipeline_mode=once)

    square = (width, width)
    weight_spec = pl.BlockSpec(square, lambda i, info: (lax.rem(i, blocks), 0))
    grad_spec = pl.BlockSpec(square, lambda i, info: (jnp.maximum(i - blocks, 0), 0))
    small = [fixed((8, width)), fixed((8, width))]

    def shape(dims, dtype):
        return jax.ShapeDtypeStruct(dims, dtype)

    result = pl.pallas_call(
        functools.partial(layer_kernel, blocks, planes, parts),
        grid_spec=pltpu.PrefetchScalarGridSpec(
            num_scalar_prefetch=1,
            grid=(2 * blocks,),
            in_specs=[fixed((row_count, width))]
            + small
            + [fixed(square), weight_spec, weight_spec]
            + [fixed((HEAD_DIM, row_count))] * parts
            + [fixed((piece, width))] * planes,
            out_specs=[fixed((piece, width))] * planes
            + [fixed((HEAD_DIM, row_count))] * parts
            + [fixed((row_count, width)), grad_spec, grad_spec, fixed(square)]
            + small,
            scratch_shapes=[
                pltpu.VMEM((width, row_count), BF16),
                pltpu.VMEM((row_count, width), F32),
                pltpu.VMEM((row_count, 1), F32),
                pltpu.VMEM((row_count, width), BF16),
                pltpu.VMEM((row_count, width), F32),
                pltpu.VMEM((blocks, row_count, width), BF16),
                pltpu.VMEM((blocks, row_count, width), F32),
                pltpu.VMEM((row_count, width), BF16),
                pltpu.VMEM((row_count, width), BF16),
            ],
        ),
        out_shape=[shape((piece, width), BF16)] * planes
        + [shape((HEAD_DIM, row_count), BF16)] * parts
        + [
            shape((row_count, width), F32),
            shape((hidden, width), BF16),
            shape((hidden, width), BF16),
            shape(square, BF16),
            shape((8, width), F32),
            shape((8, width), F32),
        ],
        compiler_params=pltpu.CompilerParams(vmem_limit_bytes=LAYER_VMEM),
        cost_estimate=pl.CostEstimate(
            flops=12 * row_count * width * hidden,
            transcendentals=row_count * hidden,
            bytes_accessed=8 * width * hidden,
        ),
    )(
        info,
        rows_all,
        vectors,
        inner_bias,
        weight_out,
        weight_inner,
        weight_outer,
        *att_parts,
        *cot_pieces,
    )
    return result[:planes], result[planes : planes + parts], result[planes + parts :]


def pad_rows(array, count):
    return jnp.concatenate([array, jnp.zeros((count,) + array.shape[1:], array.dtype)])


def local(
    layer_input,
    lengths,
    cotangent,
    w_query,
    b_query,
    w_key,
    w_value,
    b_value,
    w_attn_out,
    b_attn_out,
    norm1_gain,
    norm1_bias,
    w_inner,
    b_inner,
    w_outer,
    b_outer,
    norm2_gain,
    norm2_bias,
):
    seqs, part_rows, width = layer_input.shape
    batches = lax.axis_size("batch")
    planes = lax.axis_size("blk") // CORES
    devices = batches * planes * MEMBERS
    spread_planes = planes // seqs
    piece = part_rows // spread_planes
    row_count = planes * piece
    share = width // devices
    wide_share = w_outer.shape[0]
    hidden = wide_share * devices
    folds = hidden // width
    group = width // MEMBERS

    plane = lax.axis_index("blk") // CORES
    core = lax.axis_index("blk") % CORES
    head_place = lax.axis_index("head")
    batch_place = lax.axis_index("batch")
    device = (batch_place * planes + plane) * MEMBERS + core * 2 + head_place
    seq_length = pick(lengths, plane // spread_planes)
    part = plane % spread_planes

    def places(other_plane):
        source = (other_plane - jnp.arange(planes, dtype=jnp.int32)) % planes
        member = jnp.arange(MEMBERS, dtype=jnp.int32)
        cores = core ^ (member // 2)
        heads = head_place ^ (member % 2)
        base = (source[None, :] * CORES + cores[:, None]) * 2 + heads[:, None]
        offset = (other_plane % spread_planes) * piece + jnp.arange(piece, dtype=jnp.int32)
        return (base[:, :, None] * part_rows + offset).reshape(-1)

    def to_planes(array):
        chunks = array.reshape(planes, piece, width)
        pieces = [pick(chunks, plane)]
        for distance in range(1, planes):
            chunk = pick(chunks, (plane + distance) % planes)
            pieces.append(shift_planes(chunk, distance))
        return pieces

    def from_planes(pieces):
        back = [pieces[0]]
        for distance in range(1, planes):
            back.append(shift_planes(pieces[distance], -distance))
        return collect(back, plane).reshape(seqs, part_rows, width)

    own_group = core * 2 + head_place
    heads_here = HEADS // MEMBERS
    piece_rows = (share // 8 + 1) * 8
    kinds = jnp.stack([w_query, w_key, w_value], axis=1)
    kinds = kinds.reshape(share, 3, MEMBERS, group)
    by_group = jnp.moveaxis(kinds, 2, 0).reshape(MEMBERS, share, 3 * group)
    bias_row = jnp.pad(jnp.concatenate([b_query, b_value]), (0, 3 * group - 2 * share))
    tail_rows = jnp.pad(bias_row[None], ((0, piece_rows - share - 1), (0, 0)))
    tail_rows = jnp.broadcast_to(tail_rows, (MEMBERS,) + tail_rows.shape)
    by_group = jnp.concatenate([by_group, tail_rows], axis=1)
    by_member = reorder_members(by_group, core, head_place)
    gathered = [by_member[0]] + [
        swap_member(by_member[member], member) for member in range(1, MEMBERS)
    ]
    gathered = reorder_members(jnp.stack(gathered), core, head_place)
    gathered = in_order(
        [gathered] + [shift_planes(gathered, distance) for distance in range(1, planes)], plane
    )
    gathered = in_order(
        [gathered] + [shift_batch(gathered, distance) for distance in range(1, batches)],
        batch_place,
    )
    gathered = gathered.reshape(devices, piece_rows, 3 * group)
    own_weight = gathered[:, :share].reshape(width, 3 * group)
    bias_query = gathered[:, share, :share].reshape(MEMBERS, group)
    bias_value = gathered[:, share, share : 2 * share].reshape(MEMBERS, group)
    own_bias = jnp.concatenate(
        [
            pick(bias_query, own_group),
            jnp.zeros((group,), BF16),
            pick(bias_value, own_group),
        ]
    ).astype(F32)

    own_pieces = to_planes(layer_input)
    head_pieces = [swap_member(part_in, 1) for part_in in own_pieces]
    core_pieces = [swap_member(part_in, 2) for part_in in own_pieces]
    both_pieces = [swap_member(part_in, 2) for part_in in head_pieces]
    all_pieces = own_pieces + head_pieces + core_pieces + both_pieces
    valid_own = places(plane) < seq_length
    row_starts = (own_group ^ jnp.arange(MEMBERS, dtype=jnp.int32)) * group
    kept_rows = seq_length - places(plane)[:row_count:piece]
    info = jnp.concatenate([row_starts, kept_rows])

    def other_plane(distance):
        return (plane // spread_planes) * spread_planes + (part - distance) % spread_planes

    def shift_parts(array, distance):
        size = lax.axis_size("blk")
        route = []
        for i in range(size):
            start = i // CORES // spread_planes * spread_planes
            target = start + (i // CORES - start + distance) % spread_planes
            route.append((i, target * CORES + i % CORES))
        return lax.ppermute(array, "blk", route)

    rows_all, qkv = project(own_weight, own_bias[:, None], all_pieces)
    late_cotangent, late_out, late_inner, late_outer, qkv = lax.optimization_barrier(
        (cotangent, w_attn_out, w_inner, w_outer, qkv)
    )
    cot_pieces = to_planes(late_cotangent)

    small = jnp.concatenate(
        [b_attn_out, norm1_gain, norm1_bias, b_outer, norm2_gain, norm2_bias, b_inner]
    )
    small_row = jnp.pad(small, (0, width - small.shape[0]))[None]
    inner_rows = jnp.swapaxes(late_inner.reshape(share, folds, width), 0, 1).reshape(-1, width)
    second_pack = jnp.concatenate([late_outer, inner_rows, late_out, small_row])
    second_pack = pad_rows(second_pack, -second_pack.shape[0] % 8)
    second = lax.all_gather(second_pack, ALL_AXES, axis=0, tiled=False)
    slots = jnp.stack([w_query, w_key, w_value], axis=1)
    slots = slots.reshape(share, 3, MEMBERS, heads_here, HEAD_DIM)
    slots = jnp.transpose(slots, (3, 0, 2, 1, 4)).reshape(heads_here * share, width)
    slots, second = lax.optimization_barrier((slots, second))
    third = lax.all_gather(slots, ALL_AXES, axis=0, tiled=False)

    inner_start = wide_share
    out_start = wide_share + share * folds
    small_all = second[:, out_start + share]
    vectors = jnp.swapaxes(small_all[:, : 6 * share].reshape(devices, 6, share), 0, 1)
    vectors = pad_rows(vectors.reshape(6, width).astype(F32), 2)
    bias_inner = small_all[:, 6 * share : 6 * share + wide_share].astype(F32)
    bias_inner = pad_rows(bias_inner.reshape(folds, width), 8 - folds)
    weight_out = second[:, out_start : out_start + share].reshape(width, width)
    weight_inner = second[:, inner_start:out_start].reshape(devices, folds, share, width)
    weight_inner = jnp.swapaxes(weight_inner, 0, 1).reshape(hidden, width)
    weight_outer = second[:, :wide_share].reshape(hidden, width)

    queries = keys = values = qkv
    starts = (0, heads_here, 2 * heads_here)
    valid_keys = [valid_own]
    if spread_planes > 1:
        sides = [qkv[group:]]
        for distance in range(1, spread_planes):
            sides.append(shift_parts(qkv[group:], distance))
            valid_keys.append(places(other_plane(distance)) < seq_length)
        keys = values = jnp.concatenate(sides, axis=1)
        starts = (0, 0, heads_here)
    valid = jnp.concatenate(valid_keys)
    mask_row = jnp.where(valid, 0.0, NEG_BIG).astype(BF16)[None]
    mask_rows = pad_rows(mask_row, EXTRA - 1)

    def to_members(pieces):
        return [pieces[0]] + [
            swap_member(pieces[member], member) for member in range(1, MEMBERS)
        ]

    outs, sums, parts = [], [], []
    for slot in range(heads_here):
        slot_at = tuple(start + slot for start in starts)
        out, total = attention_forward(queries, keys, values, slot_at, mask_rows)
        outs.append(out)
        sums.append(total)
        parts.append(to_members(out))
    att_parts = [parts[slot][member] for member in range(MEMBERS) for slot in range(heads_here)]
    final_pieces, grad_att, more = layer_rows(
        info,
        rows_all,
        vectors,
        bias_inner,
        (weight_out, weight_inner, weight_outer),
        att_parts,
        cot_pieces,
    )
    output = from_planes(final_pieces)
    grad_input, grad_outer_w, grad_inner_w, grad_out_w, grad_vectors, grad_inner_bias = more

    vector_pack = jnp.swapaxes(grad_vectors[:6].reshape(6, devices, share), 0, 1)
    vector_pack = jnp.concatenate(
        [
            vector_pack.reshape(devices, 6 * share),
            grad_inner_bias[:folds].reshape(devices, wide_share),
        ],
        axis=1,
    ).astype(BF16)
    vector_pack = jnp.pad(vector_pack, ((0, 0), (0, width - vector_pack.shape[1])))
    pack_rows = out_start + share
    grad_pack = jnp.concatenate(
        [
            grad_outer_w.reshape(devices, wide_share, width),
            jnp.swapaxes(grad_inner_w.reshape(folds, devices, share, width), 0, 1).reshape(
                devices, folds * share, width
            ),
            grad_out_w.reshape(devices, share, width),
            jnp.pad(vector_pack[:, None], ((0, 0), (0, 7 - pack_rows % 8), (0, 0))),
        ],
        axis=1,
    )
    owned = lax.psum_scatter(grad_pack, ALL_AXES, scatter_dimension=0, tiled=True)[0].astype(F32)
    owned_outer = owned[:wide_share]
    owned_inner = owned[inner_start:out_start].reshape(folds, share, width)
    owned_inner = jnp.swapaxes(owned_inner, 0, 1).reshape(share, hidden)
    owned_out = owned[out_start : out_start + share]
    owned_vectors = owned[out_start + share]

    chunk_rows = width // (batches * planes)
    block_rows = chunk_rows + -chunk_rows % 16 + 16

    def reduce_weights(slot_pieces):
        chunks = weight_grad(rows_all, slot_pieces, batches * planes, chunk_rows, block_rows)
        return chunks.reshape((batches, planes) + chunks.shape[1:])

    def finish_weights(chunks):
        columns = chunks.shape[-1]
        total = pick(chunks, batch_place).astype(F32)
        for distance in range(1, batches):
            sent = pick(chunks, (batch_place + distance) % batches)
            total = total + shift_batch(sent, distance).astype(F32)
        sending = total.astype(BF16)
        total = pick(total, plane)
        for distance in range(1, planes):
            sent = pick(sending, (plane + distance) % planes)
            total = total + shift_planes(sent, distance).astype(F32)
        bias_total = total[chunk_rows]
        member_rows = total[:chunk_rows].reshape(MEMBERS, share, columns)
        member_rows = reorder_members(member_rows, core, head_place)
        tail = jnp.broadcast_to(bias_total, (MEMBERS, piece_rows - share, columns))
        sending = jnp.concatenate([member_rows, tail], axis=1)
        got = [sending[0]] + [
            swap_member(sending[member], member) for member in range(1, MEMBERS)
        ]
        got = reorder_members(jnp.stack(got), core, head_place)
        return got.reshape(MEMBERS, piece_rows, columns // (3 * HEAD_DIM), 3, HEAD_DIM)

    slot_grads = []
    early = None
    for slot in range(heads_here):
        last = slot == heads_here - 1
        sent = [grad_att[member * heads_here + slot] for member in range(MEMBERS)]
        grad_side = to_members(sent)
        if last:
            early = reduce_weights(slot_grads)
            early, grad_side = lax.optimization_barrier((early, grad_side))
        slot_at = tuple(start + slot for start in starts)
        grads = attention_backward(
            queries, keys, values, slot_at, mask_rows, sums[slot], outs[slot], grad_side
        )
        own = list(grads[:MEMBERS])
        for distance in range(1, spread_planes):
            for member in range(MEMBERS):
                moved = shift_parts(grads[distance * MEMBERS + member], -distance)
                own[member] = (own[member].astype(F32) + moved.astype(F32)).astype(BF16)
        slot_grads.append(own)
        slot_weight = third[:, slot * share : (slot + 1) * share].reshape(width, width)
        stepped = input_grad_step(
            row_starts,
            grad_input,
            slot_weight,
            to_members(own),
            planes if last else 1,
            BF16 if last else F32,
        )
        grad_input = stepped[0]
    input_grad = from_planes(stepped)

    got = jnp.concatenate(
        [finish_weights(early), finish_weights(reduce_weights(slot_grads[-1:]))], axis=2
    )
    matrices = [
        jnp.swapaxes(got[:, :share, :, i], 0, 1).reshape(share, width) for i in range(3)
    ]
    biases = [
        lax.dynamic_slice_in_dim(got[:, share, :, i].reshape(width), device * share, share)
        for i in (0, 2)
    ]

    def vector(index):
        return owned_vectors[index * share : (index + 1) * share]

    return (
        output,
        input_grad,
        matrices[0],
        biases[0],
        matrices[1],
        matrices[2],
        biases[1],
        owned_out,
        vector(0),
        vector(1),
        vector(2),
        owned_inner,
        owned_vectors[6 * share : 6 * share + wide_share],
        owned_outer,
        vector(3),
        vector(4),
        vector(5),
    )


def solution(mesh):
    rows = P("batch", ("blk", "head"), None)
    matrix = P(ALL_AXES, None)
    vector = P(ALL_AXES)
    parameters = (
        matrix,
        vector,
        matrix,
        matrix,
        vector,
        matrix,
        vector,
        vector,
        vector,
        matrix,
        vector,
        matrix,
        vector,
        vector,
        vector,
    )
    return jax.shard_map(
        local,
        mesh=mesh,
        in_specs=(rows, P("batch"), rows) + parameters,
        out_specs=(rows, rows) + parameters,
        check_vma=False,
    )
```

```python
import functools
import math

import jax
import jax.numpy as jnp
from jax import lax
from jax.experimental import pallas as pl
from jax.experimental.pallas import tpu as pltpu
from jax.sharding import PartitionSpec as P

HEADS = 12
HEAD_DIM = 64
CORES = 2
MEMBERS = 4
EXTRA = 16
NEG_BIG = -1e30
EPSILON = 1e-06
F32 = jnp.float32
BF16 = jnp.bfloat16
ALL_AXES = ("batch", "blk", "head")
VMEM_LIMIT = 56 * 2**20
LAYER_VMEM = 60 * 2**20


def dot(left_op, right_op, left_dim, right_dim):
    return lax.dot_general(
        left_op, right_op, (((left_dim,), (right_dim,)), ((), ())), preferred_element_type=F32
    )


def shift_planes(array, distance):
    size = lax.axis_size("blk")
    route = [(i, (i + CORES * distance) % size) for i in range(size)]
    return lax.ppermute(array, "blk", route)


def shift_batch(array, distance):
    size = lax.axis_size("batch")
    return lax.ppermute(array, "batch", [(i, (i + distance) % size) for i in range(size)])


def swap_member(array, member):
    size = lax.axis_size("blk")
    if member == 1:
        return lax.ppermute(array, "head", [(0, 1), (1, 0)])
    if member == 2:
        return lax.ppermute(array, "blk", [(i, i ^ 1) for i in range(size)])
    route = [(i * 2 + j, (i ^ 1) * 2 + (j ^ 1)) for i in range(size) for j in range(2)]
    return lax.ppermute(array, ("blk", "head"), route)


def pick(array, index):
    return lax.dynamic_index_in_dim(array, index, 0, keepdims=False)


def reorder_members(stack, core, head_place):
    stack = jnp.where(core == 1, jnp.concatenate([stack[2:], stack[:2]]), stack)
    swapped = jnp.stack([stack[1], stack[0], stack[3], stack[2]])
    return jnp.where(head_place == 1, swapped, stack)


def in_order(pieces, place):
    stack = jnp.stack(pieces[::-1] * 2)
    return lax.dynamic_slice_in_dim(stack, len(pieces) - 1 - place, len(pieces), 0)


def forward_kernel(block_k, members, q_ref, k_ref, v_ref, mask_ref, *rest):
    count = len(members)
    out_refs, sum_refs, (keys, values) = rest[:count], rest[count : 2 * count], rest[2 * count :]
    key_count = k_ref.shape[1]
    block_q = q_ref.shape[1] // MEMBERS
    rows = lax.broadcasted_iota(jnp.int32, (EXTRA, key_count), 0)
    joined = jnp.concatenate([k_ref[...], mask_ref[...]], axis=0)
    keys[...] = joined.astype(F32).T.astype(BF16)
    values[:HEAD_DIM, :] = v_ref[...]
    values[HEAD_DIM:, :] = jnp.where(rows == 0, 1.0, 0.0).astype(BF16)
    rows_q = lax.broadcasted_iota(jnp.int32, (EXTRA, block_q), 0)
    ones_row = jnp.where(rows_q == 0, 1.0, 0.0).astype(BF16)
    scale = 1.0 / math.sqrt(HEAD_DIM)

    for index, member in enumerate(members):
        q_places = pl.ds(member * block_q, block_q)
        scaled = (q_ref[:, q_places].astype(F32) * scale).astype(BF16)
        query = jnp.concatenate([scaled, ones_row], axis=0)

        def key_block(j, carry):
            top, acc = carry
            k_start = pl.multiple_of(j * block_k, block_k)
            scores = dot(keys[pl.ds(k_start, block_k), :], query, 1, 0)
            new_top = jnp.maximum(top, jnp.max(scores, axis=0, keepdims=True))
            probs = jnp.exp(scores - new_top)
            acc = acc * jnp.exp(top - new_top) + dot(
                values[:, pl.ds(k_start, block_k)], probs.astype(BF16), 1, 0
            )
            return new_top, acc

        top, acc = lax.fori_loop(
            0,
            key_count // block_k,
            key_block,
            (
                jnp.full((1, block_q), NEG_BIG, F32),
                jnp.zeros((HEAD_DIM + EXTRA, block_q), F32),
            ),
        )
        total = acc[HEAD_DIM : HEAD_DIM + 1, :]
        out_refs[index][...] = (acc[:HEAD_DIM, :] / total).astype(BF16)
        sum_refs[index][...] = top + jnp.log(total)


def head_specs(arrays, places):
    return [
        pl.BlockSpec((HEAD_DIM, array.shape[1]), functools.partial(lambda at, i: (at, 0), place))
        for array, place in zip(arrays, places)
    ]


def whole(shape):
    return pl.BlockSpec(shape, lambda *unused: (0,) * len(shape))


def attention_forward(queries, keys, values, places, mask_rows, members):
    part_count = queries.shape[1] // MEMBERS
    key_count = keys.shape[1]
    count = len(members)
    result = pl.pallas_call(
        functools.partial(forward_kernel, min(1024, key_count), members),
        grid=(1,),
        in_specs=head_specs((queries, keys, values), places) + [whole((EXTRA, key_count))],
        out_specs=[whole((HEAD_DIM, part_count))] * count + [whole((1, part_count))] * count,
        out_shape=[jax.ShapeDtypeStruct((HEAD_DIM, part_count), BF16)] * count
        + [jax.ShapeDtypeStruct((1, part_count), F32)] * count,
        scratch_shapes=[
            pltpu.VMEM((key_count, HEAD_DIM + EXTRA), BF16),
            pltpu.VMEM((HEAD_DIM + EXTRA, key_count), BF16),
        ],
        compiler_params=pltpu.CompilerParams(vmem_limit_bytes=VMEM_LIMIT),
        cost_estimate=pl.CostEstimate(
            flops=16 * HEAD_DIM * count * part_count * key_count,
            transcendentals=count * part_count * key_count,
            bytes_accessed=8 * HEAD_DIM * key_count,
        ),
    )(queries, keys, values, mask_rows)
    return dict(zip(members, result[:count])), dict(zip(members, result[count:]))


def split_three(row):
    high = row.astype(BF16)
    rest = row - high.astype(F32)
    middle = rest.astype(BF16)
    low = (rest - middle.astype(F32)).astype(BF16)
    return high.astype(F32), middle.astype(F32), low.astype(F32)


def backward_kernel(block_q, chosen, first, last, q_ref, k_ref, v_ref, mask_ref, *rest):
    sum_refs, rest = rest[:MEMBERS], rest[MEMBERS:]
    out_refs, rest = rest[:MEMBERS], rest[MEMBERS:]
    grad_refs, rest = rest[:MEMBERS], rest[MEMBERS:]
    if not first:
        start_ref, rest = rest[0], rest[1:]
    result_refs, rest = rest[: len(chosen)], rest[len(chosen) :]
    if not last:
        partial_ref, rest = rest[0], rest[1:]
    elif not first:
        dq_refs, rest = rest[:MEMBERS], rest[MEMBERS:]
    query_rows, keys, grad_rows, values, scaled_q, grads, dq_acc, dkv = rest
    key_count = k_ref.shape[1]
    query_count = q_ref.shape[1]
    part = query_count // MEMBERS
    scale = 1.0 / math.sqrt(HEAD_DIM)
    places_q = lax.broadcasted_iota(jnp.int32, (EXTRA, query_count), 0)
    places_k = lax.broadcasted_iota(jnp.int32, (EXTRA, key_count), 0)

    def extra_rows(row, fourth):
        high, middle, low = split_three(row)
        rows = jnp.where(
            places_q == 0, high, jnp.where(places_q == 1, middle, jnp.where(places_q == 2, low, 0.0))
        )
        return jnp.where(places_q == 3, fourth, rows).astype(BF16)

    query = (q_ref[...].astype(F32) * scale).astype(BF16)
    scaled_q[...] = query
    deltas = []
    for member in range(MEMBERS):
        grad = grad_refs[member][...]
        grads[:, member * part : (member + 1) * part] = grad
        product = grad.astype(F32) * out_refs[member][...].astype(F32)
        deltas.append(jnp.sum(product, axis=0, keepdims=True))
    deltas = jnp.concatenate(deltas, axis=1)
    sums = jnp.concatenate([sum_ref[...] for sum_ref in sum_refs], axis=1)
    joined_q = jnp.concatenate([query, extra_rows(-sums, 1.0)], axis=0)
    query_rows[...] = joined_q.astype(F32).T.astype(BF16)
    joined_g = jnp.concatenate([grads[...], extra_rows(-deltas, 0.0)], axis=0)
    grad_rows[...] = joined_g.astype(F32).T.astype(BF16)
    ones_rows = jnp.where(places_k < 3, 1.0, 0.0)
    mask_row = mask_ref[0:1, :].astype(F32)
    keys[:HEAD_DIM, :] = k_ref[...]
    keys[HEAD_DIM:, :] = jnp.where(places_k == 3, mask_row, ones_rows).astype(BF16)
    values[:HEAD_DIM, :] = v_ref[...]
    values[HEAD_DIM:, :] = ones_rows.astype(BF16)
    dq_acc[...] = jnp.zeros_like(dq_acc) if first else start_ref[...]

    def key_block(j, unused):
        k_start = pl.multiple_of((chosen.start + j * chosen.step) * part, part)
        key_part = keys[:, pl.ds(k_start, part)]
        value_part = values[:, pl.ds(k_start, part)]
        plain_keys = k_ref[:, pl.ds(k_start, part)]

        def query_block(i, carry):
            dk, dv = carry
            q_start = pl.multiple_of(i * block_q, block_q)
            probs = jnp.exp(dot(query_rows[pl.ds(q_start, block_q), :], key_part, 1, 0))
            moved = dot(grad_rows[pl.ds(q_start, block_q), :], value_part, 1, 0)
            grad_scores = (probs * moved).astype(BF16)
            dv = dv + dot(grads[:, pl.ds(q_start, block_q)], probs.astype(BF16), 1, 0)
            dk = dk + dot(scaled_q[:, pl.ds(q_start, block_q)], grad_scores, 1, 0)
            dq_acc[:, pl.ds(q_start, block_q)] += dot(plain_keys, grad_scores, 1, 1)
            return dk, dv

        zeros = jnp.zeros((HEAD_DIM, part), F32)
        dk, dv = lax.fori_loop(0, query_count // block_q, query_block, (zeros, zeros))
        place = pl.multiple_of(j * part, part)
        dkv[:HEAD_DIM, pl.ds(place, part)] = dk.astype(BF16)
        dkv[HEAD_DIM:, pl.ds(place, part)] = dv.astype(BF16)
        return 0

    lax.fori_loop(0, len(chosen), key_block, 0)

    def query_grads(member):
        return (dq_acc[:, member * part : (member + 1) * part] * scale).astype(BF16)

    together = first and last
    for index, result_ref in enumerate(result_refs):
        found = dkv[:, index * part : (index + 1) * part]
        if together:
            if chosen[index] < MEMBERS:
                result_ref[:HEAD_DIM, :] = query_grads(chosen[index])
            else:
                result_ref[:HEAD_DIM, :] = jnp.zeros((HEAD_DIM, part), BF16)
            result_ref[HEAD_DIM:, :] = found
        else:
            result_ref[...] = found
    if not last:
        partial_ref[...] = dq_acc[...]
    elif not first:
        for member in range(MEMBERS):
            dq_refs[member][...] = query_grads(member)


def attention_backward(
    queries, keys, values, places, mask_rows, sums, outs, grads, chosen, start=None, last=True
):
    query_count = queries.shape[1]
    key_count = keys.shape[1]
    part = query_count // MEMBERS
    wide = HEAD_DIM + EXTRA
    first = start is None
    height = (3 if first and last else 2) * HEAD_DIM
    count = len(chosen)
    results = [((height, part), BF16)] * count
    if not last:
        results.append(((HEAD_DIM, query_count), F32))
    elif not first:
        results += [((HEAD_DIM, part), BF16)] * MEMBERS
    extra = [] if first else [start]
    found = pl.pallas_call(
        functools.partial(backward_kernel, min(1024, query_count), chosen, first, last),
        grid=(1,),
        in_specs=head_specs((queries, keys, values), places)
        + [whole((EXTRA, key_count))]
        + [whole((1, part))] * MEMBERS
        + [whole((HEAD_DIM, part))] * (2 * MEMBERS)
        + [whole(array.shape) for array in extra],
        out_specs=[whole(dims) for dims, dtype in results],
        out_shape=[jax.ShapeDtypeStruct(dims, dtype) for dims, dtype in results],
        scratch_shapes=[
            pltpu.VMEM((query_count, wide), BF16),
            pltpu.VMEM((wide, key_count), BF16),
            pltpu.VMEM((query_count, wide), BF16),
            pltpu.VMEM((wide, key_count), BF16),
            pltpu.VMEM((HEAD_DIM, query_count), BF16),
            pltpu.VMEM((HEAD_DIM, query_count), BF16),
            pltpu.VMEM((HEAD_DIM, query_count), F32),
            pltpu.VMEM((2 * HEAD_DIM, count * part), BF16),
        ],
        compiler_params=pltpu.CompilerParams(vmem_limit_bytes=VMEM_LIMIT),
        cost_estimate=pl.CostEstimate(
            flops=40 * HEAD_DIM * query_count * count * part,
            transcendentals=query_count * count * part,
            bytes_accessed=16 * HEAD_DIM * key_count,
        ),
    )(queries, keys, values, mask_rows, *sums, *outs, *grads, *extra)
    return list(found[:count]), list(found[count:])


def joined_rows(refs, member):
    count = len(refs) // MEMBERS
    return jnp.concatenate([ref[...] for ref in refs[member * count : (member + 1) * count]])


def project_kernel(weight_ref, bias_ref, *rest):
    piece_refs, out_ref = rest[:-1], rest[-1]
    weight = weight_ref[...].astype(F32).T.astype(BF16)
    step = out_ref.shape[1] // MEMBERS
    for member in range(MEMBERS):
        lanes = slice(member * step, (member + 1) * step)
        rows = joined_rows(piece_refs, member)
        out_ref[:, lanes] = (dot(weight, rows, 1, 1) + bias_ref[...]).astype(BF16)


def project(weight, bias_column, pieces):
    count, (rows, width) = len(pieces), pieces[0].shape
    columns = weight.shape[1]
    return pl.pallas_call(
        project_kernel,
        grid=(1,),
        in_specs=[whole(weight.shape), whole(bias_column.shape)] + [whole((rows, width))] * count,
        out_specs=whole((columns, count * rows)),
        out_shape=jax.ShapeDtypeStruct((columns, count * rows), BF16),
        compiler_params=pltpu.CompilerParams(vmem_limit_bytes=VMEM_LIMIT),
        cost_estimate=pl.CostEstimate(
            flops=2 * count * rows * width * columns,
            transcendentals=0,
            bytes_accessed=4 * count * rows * width,
        ),
    )(weight, bias_column, *pieces)


def stacked(refs):
    parts = [ref[...] for ref in refs]
    return parts[0] if len(parts) == 1 else jnp.concatenate(parts)


def flatten(nested):
    return [array for slot in nested for member in slot for array in member]


def regroup(refs, counts):
    refs = list(refs)
    return [[[refs.pop(0) for _ in range(n)] for n in slot] for slot in counts]


def counts_of(nested):
    return [[len(member) for member in slot] for slot in nested]


def weight_grad_kernel(counts, pieces, chunk_rows, *rest):
    row_refs, grad_refs, out_ref = rest[:pieces], rest[pieces:-1], rest[-1]
    slots = regroup(grad_refs, counts)
    chunks = out_ref.shape[0]
    columns = out_ref.shape[2] // len(slots)
    part = slots[0][0][0].shape[1]
    ones = jnp.ones((8, part), BF16)
    totals, biases = [0.0] * len(slots), [0.0] * len(slots)
    for member in range(MEMBERS):
        rows = joined_rows(row_refs, member)
        for slot, members in enumerate(slots):
            grad = stacked(members[member])
            totals[slot] = totals[slot] + dot(grad, rows, 1, 0)
            biases[slot] = biases[slot] + dot(ones, grad, 1, 1)
    for slot in range(len(slots)):
        lanes = slice(slot * columns, (slot + 1) * columns)
        turned = totals[slot].T.astype(BF16)
        bias = biases[slot][0:1].astype(BF16)
        bias = jnp.broadcast_to(bias, (out_ref.shape[1] - chunk_rows, columns))
        for chunk in range(chunks):
            out_ref[chunk, :chunk_rows, lanes] = turned[chunk * chunk_rows : (chunk + 1) * chunk_rows]
            out_ref[chunk, chunk_rows:, lanes] = bias


def weight_grad(row_pieces, slots, chunks, chunk_rows, block_rows):
    arrays = flatten(slots)
    shape = (chunks, block_rows, len(slots) * 3 * HEAD_DIM)
    return pl.pallas_call(
        functools.partial(weight_grad_kernel, counts_of(slots), len(row_pieces), chunk_rows),
        grid=(1,),
        in_specs=[whole(array.shape) for array in list(row_pieces) + arrays],
        out_specs=whole(shape),
        out_shape=jax.ShapeDtypeStruct(shape, BF16),
        compiler_params=pltpu.CompilerParams(vmem_limit_bytes=VMEM_LIMIT),
        cost_estimate=pl.CostEstimate(
            flops=2 * shape[2] * len(row_pieces) * row_pieces[0].size,
            transcendentals=0,
            bytes_accessed=2 * len(row_pieces) * row_pieces[0].size,
        ),
    )(*row_pieces, *arrays)


def input_grad_kernel(counts, info_ref, acc_ref, *rest):
    slots = len(counts)
    weight_refs, rest = rest[:slots], rest[slots:]
    grads = regroup(rest[: sum(map(sum, counts))], counts)
    out_refs, joined = rest[sum(map(sum, counts)) : -1], rest[-1]
    total = acc_ref[...]
    width = total.shape[1]
    for slot, members in enumerate(grads):
        for member, refs in enumerate(members):
            start = info_ref[member]
            for ref in refs:
                height = ref.shape[0]
                joined[slot, pl.ds(pl.multiple_of(start, HEAD_DIM), height), :] = ref[...]
                start = start + height
        weight = weight_refs[slot][...].reshape(width, width)
        total = total + dot(joined[slot], weight, 0, 1)
    rows = acc_ref.shape[0] // len(out_refs)
    for index, out_ref in enumerate(out_refs):
        out_ref[...] = total[index * rows : (index + 1) * rows].astype(out_ref.dtype)


def input_grad_step(info, acc, weights, slots, out_count, dtype):
    arrays = flatten(slots)
    rows, width = acc.shape
    out = (rows // out_count, width)
    return pl.pallas_call(
        functools.partial(input_grad_kernel, counts_of(slots)),
        grid_spec=pltpu.PrefetchScalarGridSpec(
            num_scalar_prefetch=1,
            grid=(1,),
            in_specs=[whole(acc.shape)]
            + [pl.BlockSpec(dims, functools.partial(lambda at, i, info: at, place))
               for array, dims, place in weights]
            + [whole(array.shape) for array in arrays],
            out_specs=[whole(out)] * out_count,
            scratch_shapes=[pltpu.VMEM((len(slots), width, rows), BF16)],
        ),
        out_shape=[jax.ShapeDtypeStruct(out, dtype)] * out_count,
        compiler_params=pltpu.CompilerParams(vmem_limit_bytes=VMEM_LIMIT),
        cost_estimate=pl.CostEstimate(
            flops=2 * rows * width * width * len(slots),
            transcendentals=0,
            bytes_accessed=8 * rows * width,
        ),
    )(info, acc, *[array for array, dims, place in weights], *arrays)


def collect_kernel(count, place_ref, *rest):
    piece_refs, out_ref = rest[:count], rest[count]
    for index, piece_ref in enumerate(piece_refs):
        out_ref[lax.rem(place_ref[0] + index, count)] = piece_ref[...]


def collect(pieces, place):
    count, shape = len(pieces), pieces[0].shape
    return pl.pallas_call(
        functools.partial(collect_kernel, count),
        grid_spec=pltpu.PrefetchScalarGridSpec(
            num_scalar_prefetch=1,
            grid=(1,),
            in_specs=[whole(shape)] * count,
            out_specs=whole((count,) + shape),
        ),
        out_shape=jax.ShapeDtypeStruct((count,) + shape, pieces[0].dtype),
        compiler_params=pltpu.CompilerParams(vmem_limit_bytes=VMEM_LIMIT),
    )(place[None], *pieces)


def gelu_parts(value):
    size = jnp.abs(value) * math.sqrt(0.5)
    t = 1.0 / (1.0 + 0.3275911 * size)
    bell = jnp.exp(-0.5 * value * value)
    poly = 1.061405429 * t - 1.453152027
    poly = poly * t + 1.421413741
    poly = poly * t - 0.284496736
    poly = poly * t + 0.254829592
    tail = 0.5 * poly * t * bell
    share = jnp.where(value < 0, tail, 1.0 - tail)
    return value * share, share + value * bell * (1.0 / math.sqrt(2.0 * math.pi))


def row_mean(array):
    return jnp.mean(array, axis=-1, keepdims=True)


def column_sum(array):
    return jnp.sum(array, axis=0, keepdims=True)


def layer_kernel(blocks, planes, parts, info_ref, vectors_ref, inner_bias_ref, *rest):
    row_refs, rest = rest[:planes], rest[planes:]
    packed_out, packed_inner, packed_outer = rest[:3]
    att_refs, rest = rest[3 : 3 + parts], rest[3 + parts :]
    cot_refs, rest = rest[:planes], rest[planes:]
    final_refs, rest = rest[:planes], rest[planes:]
    grad_att_refs, rest = rest[:parts], rest[parts:]
    resid_ref, grad_outer_w, grad_inner_w, grad_out_w, grad_vectors, grad_inner_bias = rest[:6]
    attended, hat1, scale1, low, acc, active, slope, grad_low, grad_hidden, weight_out = rest[6:]
    step = pl.program_id(0)
    row_count, width = acc.shape
    piece = row_count // planes
    group = width // MEMBERS
    block = jnp.where(step < blocks, step, step - blocks)
    pieces = [slice(k * piece, (k + 1) * piece) for k in range(planes)]

    def group_rows(member):
        return pl.ds(pl.multiple_of(info_ref[member], HEAD_DIM), group)

    def vector(index):
        return vectors_ref[index : index + 1, :]

    @pl.when(step == 0)
    def _():
        for index, att_ref in enumerate(att_refs):
            attended[index * HEAD_DIM : (index + 1) * HEAD_DIM, :] = att_ref[...]
        weight_out[...] = packed_out[...].reshape(width, width)
        weight = jnp.concatenate([weight_out[group_rows(m), :] for m in range(MEMBERS)])
        for k in range(planes):
            branch = dot(attended[:, pieces[k]], weight, 0, 0) + vector(0)
            value = row_refs[k][...].astype(F32) + branch
            centred = value - row_mean(value)
            scale = lax.rsqrt(row_mean(centred * centred) + EPSILON)
            hat = centred * scale
            normed = hat * vector(1) + vector(2)
            hat1[pieces[k], :] = hat
            scale1[pieces[k], :] = scale
            low[pieces[k], :] = normed.astype(BF16)
            acc[pieces[k], :] = normed + vector(3)
        grad_vectors[...] = jnp.zeros_like(grad_vectors)
        grad_inner_bias[...] = jnp.zeros_like(grad_inner_bias)

    @pl.when(step < blocks)
    def _():
        bias = inner_bias_ref[pl.ds(block, 1), :]
        weight_inner = packed_inner[...].reshape(width, width)
        weight_outer = packed_outer[...].reshape(width, width)
        for k in range(planes):
            inner = dot(low[pieces[k], :], weight_inner, 1, 0) + bias
            value, derivative = gelu_parts(inner)
            value = value.astype(BF16)
            active[block, pieces[k], :] = value
            slope[block, pieces[k], :] = derivative
            acc[pieces[k], :] += dot(value, weight_outer, 1, 0)

    @pl.when(step == blocks)
    def _():
        gain_sum, shift_sum, bias_sum = 0.0, 0.0, 0.0
        for k in range(planes):
            value = acc[pieces[k], :]
            centred = value - row_mean(value)
            scale = lax.rsqrt(row_mean(centred * centred) + EPSILON)
            hat = centred * scale
            final_refs[k][...] = (hat * vector(4) + vector(5)).astype(BF16)
            places = lax.broadcasted_iota(jnp.int32, (piece, width), 0)
            grad = jnp.where(
                places < info_ref[MEMBERS + k], cot_refs[k][...].astype(F32), 0.0
            )
            gain_sum += column_sum(grad * hat)
            shift_sum += column_sum(grad)
            grad = grad * vector(4)
            grad = scale * (grad - row_mean(grad) - hat * row_mean(grad * hat))
            rounded = grad.astype(BF16)
            bias_sum += column_sum(rounded.astype(F32))
            grad_low[pieces[k], :] = rounded
            acc[pieces[k], :] = grad
        grad_vectors[3:4, :] = bias_sum
        grad_vectors[4:5, :] = gain_sum
        grad_vectors[5:6, :] = shift_sum

    @pl.when(step >= blocks)
    def _():
        bias_sum = 0.0
        weight_inner = packed_inner[...].reshape(width, width)
        weight_outer = packed_outer[...].reshape(width, width)
        for k in range(planes):
            moved = dot(grad_low[pieces[k], :], weight_outer, 1, 1)
            grad = (moved * slope[block, pieces[k], :]).astype(BF16)
            grad_hidden[pieces[k], :] = grad
            bias_sum += column_sum(grad.astype(F32))
            acc[pieces[k], :] += dot(grad, weight_inner, 1, 1)
        grad_inner_bias[pl.ds(block, 1), :] = bias_sum
        for m in range(MEMBERS // 2):
            lanes = slice(m * 2 * group, (m + 1) * 2 * group)
            grad_outer_w[lanes, :] = dot(active[block, :, lanes], grad_low[...], 0, 0).astype(BF16)
            grad_inner_w[lanes, :] = dot(low[:, lanes], grad_hidden[...], 0, 0).astype(BF16)

    @pl.when(step == 2 * blocks - 1)
    def _():
        gain_sum, shift_sum, bias_sum = 0.0, 0.0, 0.0
        for k in range(planes):
            grad, hat = acc[pieces[k], :], hat1[pieces[k], :]
            gain_sum += column_sum(grad * hat)
            shift_sum += column_sum(grad)
            grad = grad * vector(1)
            grad = scale1[pieces[k], :] * (grad - row_mean(grad) - hat * row_mean(grad * hat))
            resid_ref[pieces[k], :] = grad
            rounded = grad.astype(BF16)
            bias_sum += column_sum(rounded.astype(F32))
            grad_low[pieces[k], :] = rounded
        grad_vectors[0:1, :] = bias_sum
        grad_vectors[1:2, :] = gain_sum
        grad_vectors[2:3, :] = shift_sum
        heads = group // HEAD_DIM
        for m in range(MEMBERS):
            rows = slice(m * group, (m + 1) * group)
            grad_out_w[group_rows(m), :] = dot(attended[rows, :], grad_low[...], 1, 0).astype(BF16)
            moved = dot(weight_out[group_rows(m), :], grad_low[...], 1, 1).astype(BF16)
            for j in range(heads):
                grad_att_refs[m * heads + j][...] = moved[j * HEAD_DIM : (j + 1) * HEAD_DIM, :]


def layer_rows(info, row_pieces, vectors, inner_bias, weights, att_parts, cot_pieces):
    width = row_pieces[0].shape[1]
    blocks, planes, parts = weights[0], len(cot_pieces), len(att_parts)
    hidden = blocks * width
    row_count = att_parts[0].shape[1]
    piece = row_count // planes
    once = pl.Buffered(1)

    def fixed(shape):
        return pl.BlockSpec(shape, lambda *unused: (0,) * len(shape), pipeline_mode=once)

    square = (width, width)
    weight_specs = [
        pl.BlockSpec(
            dims,
            functools.partial(lambda at, i, info: at(lax.rem(i, blocks)), place),
            pipeline_mode=pl.Buffered(1 if index == 0 else 2),
        )
        for index, (array, dims, place) in enumerate(weights[1:])
    ]
    grad_spec = pl.BlockSpec(square, lambda i, info: (jnp.maximum(i - blocks, 0), 0))
    small = [fixed((8, width)), fixed((8, width))]

    def shape(dims, dtype):
        return jax.ShapeDtypeStruct(dims, dtype)

    result = pl.pallas_call(
        functools.partial(layer_kernel, blocks, planes, parts),
        grid_spec=pltpu.PrefetchScalarGridSpec(
            num_scalar_prefetch=1,
            grid=(2 * blocks,),
            in_specs=small
            + [fixed((piece, width))] * planes
            + weight_specs
            + [fixed((HEAD_DIM, row_count))] * parts
            + [fixed((piece, width))] * planes,
            out_specs=[fixed((piece, width))] * planes
            + [fixed((HEAD_DIM, row_count))] * parts
            + [fixed((row_count, width)), grad_spec, grad_spec, fixed(square)]
            + small,
            scratch_shapes=[
                pltpu.VMEM((width, row_count), BF16),
                pltpu.VMEM((row_count, width), F32),
                pltpu.VMEM((row_count, 1), F32),
                pltpu.VMEM((row_count, width), BF16),
                pltpu.VMEM((row_count, width), F32),
                pltpu.VMEM((blocks, row_count, width), BF16),
                pltpu.VMEM((blocks, row_count, width), F32),
                pltpu.VMEM((row_count, width), BF16),
                pltpu.VMEM((row_count, width), BF16),
                pltpu.VMEM(square, BF16),
            ],
        ),
        out_shape=[shape((piece, width), BF16)] * planes
        + [shape((HEAD_DIM, row_count), BF16)] * parts
        + [
            shape((row_count, width), F32),
            shape((hidden, width), BF16),
            shape((hidden, width), BF16),
            shape(square, BF16),
            shape((8, width), F32),
            shape((8, width), F32),
        ],
        compiler_params=pltpu.CompilerParams(vmem_limit_bytes=LAYER_VMEM),
        cost_estimate=pl.CostEstimate(
            flops=12 * row_count * width * hidden,
            transcendentals=row_count * hidden,
            bytes_accessed=8 * width * hidden,
        ),
    )(
        info,
        vectors,
        inner_bias,
        *row_pieces,
        *[array for array, dims, place in weights[1:]],
        *att_parts,
        *cot_pieces,
    )
    return result[:planes], result[planes : planes + parts], result[planes + parts :]


def pad_rows(array, count):
    return jnp.concatenate([array, jnp.zeros((count,) + array.shape[1:], array.dtype)])


def local(
    layer_input,
    lengths,
    cotangent,
    w_query,
    b_query,
    w_key,
    w_value,
    b_value,
    w_attn_out,
    b_attn_out,
    norm1_gain,
    norm1_bias,
    w_inner,
    b_inner,
    w_outer,
    b_outer,
    norm2_gain,
    norm2_bias,
):
    seqs, part_rows, width = layer_input.shape
    batches = lax.axis_size("batch")
    planes = lax.axis_size("blk") // CORES
    devices = batches * planes * MEMBERS
    spread_planes = planes // seqs
    piece = part_rows // spread_planes
    row_count = planes * piece
    share = width // devices
    wide_share = w_outer.shape[0]
    hidden = wide_share * devices
    folds = hidden // width
    group = width // MEMBERS

    plane = lax.axis_index("blk") // CORES
    core = lax.axis_index("blk") % CORES
    head_place = lax.axis_index("head")
    batch_place = lax.axis_index("batch")
    device = (batch_place * planes + plane) * MEMBERS + core * 2 + head_place
    seq_length = pick(lengths, plane // spread_planes)
    part = plane % spread_planes

    def places(other_plane):
        source = (other_plane - jnp.arange(planes, dtype=jnp.int32)) % planes
        member = jnp.arange(MEMBERS, dtype=jnp.int32)
        cores = core ^ (member // 2)
        heads = head_place ^ (member % 2)
        base = (source[None, :] * CORES + cores[:, None]) * 2 + heads[:, None]
        offset = (other_plane % spread_planes) * piece + jnp.arange(piece, dtype=jnp.int32)
        return (base[:, :, None] * part_rows + offset).reshape(-1)

    def to_planes(array):
        chunks = array.reshape(planes, piece, width)
        pieces = [pick(chunks, plane)]
        for distance in range(1, planes):
            chunk = pick(chunks, (plane + distance) % planes)
            pieces.append(shift_planes(chunk, distance))
        return pieces

    own_pieces = to_planes(layer_input)
    own_group = core * 2 + head_place
    heads_here = HEADS // MEMBERS
    piece_rows = (share // 8 + 1) * 8
    kinds = jnp.stack([w_query, w_key, w_value], axis=1)
    kinds = kinds.reshape(share, 3, MEMBERS, group)
    by_group = jnp.moveaxis(kinds, 2, 0).reshape(MEMBERS, share, 3 * group)
    bias_row = jnp.pad(jnp.concatenate([b_query, b_value]), (0, 3 * group - 2 * share))
    tail_rows = jnp.pad(bias_row[None], ((0, piece_rows - share - 1), (0, 0)))
    tail_rows = jnp.broadcast_to(tail_rows, (MEMBERS,) + tail_rows.shape)
    by_group = jnp.concatenate([by_group, tail_rows], axis=1)
    by_group, own_pieces[1] = lax.optimization_barrier((by_group, own_pieces[1]))
    by_member = reorder_members(by_group, core, head_place)
    gathered = [by_member[0]] + [
        swap_member(by_member[member], member) for member in range(1, MEMBERS)
    ]
    gathered = reorder_members(jnp.stack(gathered), core, head_place)
    gathered = in_order(
        [gathered] + [shift_planes(gathered, distance) for distance in range(1, planes)], plane
    )
    gathered = in_order(
        [gathered] + [shift_batch(gathered, distance) for distance in range(1, batches)],
        batch_place,
    )
    gathered = gathered.reshape(devices, piece_rows, 3 * group)
    own_weight = gathered[:, :share].reshape(width, 3 * group)
    bias_query = gathered[:, share, :share].reshape(MEMBERS, group)
    bias_value = gathered[:, share, share : 2 * share].reshape(MEMBERS, group)
    own_bias = jnp.concatenate(
        [
            pick(bias_query, own_group),
            jnp.zeros((group,), BF16),
            pick(bias_value, own_group),
        ]
    ).astype(F32)

    head_pieces = [swap_member(part_in, 1) for part_in in own_pieces]
    core_pieces = [swap_member(part_in, 2) for part_in in own_pieces]
    both_pieces = [swap_member(part_in, 2) for part_in in head_pieces]
    all_pieces = own_pieces + head_pieces + core_pieces + both_pieces
    valid_own = places(plane) < seq_length
    row_starts = (own_group ^ jnp.arange(MEMBERS, dtype=jnp.int32)) * group
    kept_rows = seq_length - places(plane)[:row_count:piece]
    info = jnp.concatenate([row_starts, kept_rows])

    def other_plane(distance):
        return (plane // spread_planes) * spread_planes + (part - distance) % spread_planes

    def shift_parts(array, distance):
        size = lax.axis_size("blk")
        route = []
        for i in range(size):
            start = i // CORES // spread_planes * spread_planes
            target = start + (i // CORES - start + distance) % spread_planes
            route.append((i, target * CORES + i % CORES))
        return lax.ppermute(array, "blk", route)

    qkv = project(own_weight, own_bias[:, None], all_pieces)
    late_cotangent, qkv = lax.optimization_barrier((cotangent, qkv))
    cot_pieces = to_planes(late_cotangent)

    small = jnp.concatenate(
        [b_attn_out, norm1_gain, norm1_bias, b_outer, norm2_gain, norm2_bias, b_inner]
    )
    small_row = jnp.pad(small, (0, width - small.shape[0]))[None]
    inner_rows = jnp.swapaxes(w_inner.reshape(share, folds, width), 0, 1).reshape(-1, width)
    second_pack = jnp.concatenate([w_outer, inner_rows, w_attn_out, small_row])
    second_pack = pad_rows(second_pack, -second_pack.shape[0] % 8)
    second_pack, gate = lax.optimization_barrier((second_pack, head_pieces[-1]))
    second = lax.all_gather(second_pack, ALL_AXES, axis=0, tiled=False)
    slots = jnp.stack([w_query, w_key, w_value], axis=1)
    slots = slots.reshape(share, 3, MEMBERS, heads_here, HEAD_DIM)
    slots = jnp.transpose(slots, (3, 0, 2, 1, 4)).reshape(heads_here * share, width)
    slots, gate = lax.optimization_barrier((slots, qkv[0, 0]))
    third = lax.all_gather(slots, ALL_AXES, axis=0, tiled=False)

    inner_start = wide_share
    out_start = wide_share + share * folds
    small_all = second[:, out_start + share]
    vectors = jnp.swapaxes(small_all[:, : 6 * share].reshape(devices, 6, share), 0, 1)
    vectors = pad_rows(vectors.reshape(6, width).astype(F32), 2)
    bias_inner = small_all[:, 6 * share : 6 * share + wide_share].astype(F32)
    bias_inner = pad_rows(bias_inner.reshape(folds, width), 8 - folds)
    square = (width, width)
    if share % 8 == 0:
        narrow = (devices, share, width)
        layer_weights = (
            folds,
            (second, narrow, lambda j: (0, out_start // share, 0)),
            (second, narrow, lambda j: (0, inner_start // share + j, 0)),
            (second, (devices // folds, wide_share, width), lambda j: (j, 0, 0)),
        )
        slot_weights = [(third, narrow, (0, slot, 0)) for slot in range(heads_here)]
    else:
        inner = second[:, inner_start:out_start].reshape(devices, folds, share, width)
        inner = jnp.swapaxes(inner, 0, 1).reshape((folds,) + square)
        outer = second[:, :wide_share].reshape((folds,) + square)
        layer_weights = (
            folds,
            (second[:, out_start : out_start + share].reshape(square), square, lambda j: (0, 0)),
            (inner, (1,) + square, lambda j: (j, 0, 0)),
            (outer, (1,) + square, lambda j: (j, 0, 0)),
        )
        slot_weights = [
            (third[:, slot * share : (slot + 1) * share].reshape(square), square, (0, 0))
            for slot in range(heads_here)
        ]

    queries = keys = values = qkv
    starts = (0, heads_here, 2 * heads_here)
    valid_keys = [valid_own]
    if spread_planes > 1:
        sides = [qkv[group:]]
        for distance in range(1, spread_planes):
            sides.append(shift_parts(qkv[group:], distance))
            valid_keys.append(places(other_plane(distance)) < seq_length)
        keys = values = jnp.concatenate(sides, axis=1)
        starts = (0, 0, heads_here)
    valid = jnp.concatenate(valid_keys)
    mask_row = jnp.where(valid, 0.0, NEG_BIG).astype(BF16)[None]
    mask_rows = pad_rows(mask_row, EXTRA - 1)

    def to_members(pieces):
        return [pieces[0]] + [
            swap_member(pieces[member], member) for member in range(1, MEMBERS)
        ]

    far, near = range(1, MEMBERS, 2), range(0, MEMBERS, 2)
    outs, sums, parts = [], [], []
    for slot in range(heads_here):
        slot_at = tuple(start + slot for start in starts)
        chosen = [range(MEMBERS)] if slot < heads_here - 1 else [far, near]
        out, total, moved = {}, {}, {}
        for members in chosen:
            found = attention_forward(queries, keys, values, slot_at, mask_rows, members)
            out.update(found[0])
            total.update(found[1])
            for member in members:
                piece_out = found[0][member]
                moved[member] = swap_member(piece_out, member) if member else piece_out
        outs.append([out[member] for member in range(MEMBERS)])
        sums.append([total[member] for member in range(MEMBERS)])
        parts.append(moved)
    att_parts = [parts[slot][member] for member in range(MEMBERS) for slot in range(heads_here)]
    final_pieces, grad_att, more = layer_rows(
        info, own_pieces, vectors, bias_inner, layer_weights, att_parts, cot_pieces
    )
    output_pieces = [final_pieces[0]] + [
        shift_planes(final_pieces[distance], -distance) for distance in range(1, planes)
    ]
    grad_input, grad_outer_w, grad_inner_w, grad_out_w, grad_vectors, grad_inner_bias = more

    vector_pack = jnp.swapaxes(grad_vectors[:6].reshape(6, devices, share), 0, 1)
    vector_pack = jnp.concatenate(
        [
            vector_pack.reshape(devices, 6 * share),
            grad_inner_bias[:folds].reshape(devices, wide_share),
        ],
        axis=1,
    ).astype(BF16)
    vector_pack = jnp.pad(vector_pack, ((0, 0), (0, width - vector_pack.shape[1])))
    pack_rows = out_start + share
    grad_pack = jnp.concatenate(
        [
            grad_outer_w.reshape(devices, wide_share, width),
            jnp.swapaxes(grad_inner_w.reshape(folds, devices, share, width), 0, 1).reshape(
                devices, folds * share, width
            ),
            grad_out_w.reshape(devices, share, width),
            jnp.pad(vector_pack[:, None], ((0, 0), (0, 7 - pack_rows % 8), (0, 0))),
        ],
        axis=1,
    )
    owned = lax.psum_scatter(grad_pack, ALL_AXES, scatter_dimension=0, tiled=True)[0].astype(F32)
    owned_outer = owned[:wide_share]
    owned_inner = owned[inner_start:out_start].reshape(folds, share, width)
    owned_inner = jnp.swapaxes(owned_inner, 0, 1).reshape(share, hidden)
    owned_out = owned[out_start : out_start + share]
    owned_vectors = owned[out_start + share]

    chunk_rows = width // (batches * planes)
    block_rows = chunk_rows + -chunk_rows % 16 + 16

    def finish_weights(chunks):
        columns = chunks.shape[-1]
        total = pick(chunks, batch_place).astype(F32)
        for distance in range(1, batches):
            sent = pick(chunks, (batch_place + distance) % batches)
            total = total + shift_batch(sent, distance).astype(F32)
        sending = total.astype(BF16)
        total = pick(total, plane)
        for distance in range(1, planes):
            sent = pick(sending, (plane + distance) % planes)
            total = total + shift_planes(sent, distance).astype(F32)
        bias_total = total[chunk_rows]
        member_rows = total[:chunk_rows].reshape(MEMBERS, share, columns)
        member_rows = reorder_members(member_rows, core, head_place)
        tail = jnp.broadcast_to(bias_total, (MEMBERS, piece_rows - share, columns))
        sending = jnp.concatenate([member_rows, tail], axis=1)
        got = [sending[0]] + [
            swap_member(sending[member], member) for member in range(1, MEMBERS)
        ]
        got = reorder_members(jnp.stack(got), core, head_place)
        return got.reshape(MEMBERS, piece_rows, columns // (3 * HEAD_DIM), 3, HEAD_DIM)

    def own_places(found):
        own = {index: array for index, array in found.items() if index < MEMBERS}
        for index, array in found.items():
            if index >= MEMBERS:
                moved = shift_parts(array, -(index // MEMBERS)).astype(F32)
                kept = own[index % MEMBERS]
                own[index % MEMBERS] = (kept.astype(F32) + moved).astype(BF16)
        return own

    def send(member, array):
        return swap_member(array, member) if member else array

    pieces_here = MEMBERS * spread_planes
    kept_slots, sent_slots = [], []
    for slot in range(heads_here):
        grad_side = [
            send(member, grad_att[member * heads_here + slot]) for member in range(MEMBERS)
        ]
        slot_at = tuple(start + slot for start in starts)
        given = (queries, keys, values, slot_at, mask_rows, sums[slot], outs[slot])
        if slot == 1:
            output_pieces, grad_side = lax.optimization_barrier((output_pieces, grad_side))
        if slot < heads_here - 1:
            chosen = range(pieces_here)
            found, unused = attention_backward(*given, grad_side, chosen)
            own = own_places(dict(zip(chosen, found)))
            kept_slots.append([[own[member]] for member in range(MEMBERS)])
            sent_slots.append([[send(member, own[member])] for member in range(MEMBERS)])
            continue
        sent_slots[:-1], grad_side = lax.optimization_barrier((sent_slots[:-1], grad_side))
        chosen = range(1, pieces_here, 2)
        found, (partial,) = attention_backward(*given, grad_side, chosen, last=False)
        own = own_places(dict(zip(chosen, found)))
        sent = {member: send(member, own[member]) for member in far}
        grad_input = input_grad_step(
            row_starts, grad_input, slot_weights[:-1], sent_slots, 1, F32
        )[0]
        partial, grad_input = lax.optimization_barrier((partial, grad_input))
        chosen = range(0, pieces_here, 2)
        found, query_grads = attention_backward(*given, grad_side, chosen, start=partial)
        own.update(own_places(dict(zip(chosen, found))))
        sent.update({member: send(member, own[member]) for member in near})
        kept_slots.append([[query_grads[member], own[member]] for member in range(MEMBERS)])
        last_sent = [
            [send(member, query_grads[member]), sent[member]] for member in range(MEMBERS)
        ]
    input_pieces = input_grad_step(
        row_starts, grad_input, slot_weights[-1:], [last_sent], planes, BF16
    )
    input_pieces = [input_pieces[0]] + [
        shift_planes(input_pieces[distance], -distance) for distance in range(1, planes)
    ]
    input_grad = collect(input_pieces, plane).reshape(seqs, part_rows, width)
    output = collect(output_pieces, plane).reshape(seqs, part_rows, width)

    chunks = weight_grad(all_pieces, kept_slots, batches * planes, chunk_rows, block_rows)
    got = finish_weights(chunks.reshape((batches, planes) + chunks.shape[1:]))
    matrices = [
        jnp.swapaxes(got[:, :share, :, i], 0, 1).reshape(share, width) for i in range(3)
    ]
    biases = [
        lax.dynamic_slice_in_dim(got[:, share, :, i].reshape(width), device * share, share)
        for i in (0, 2)
    ]

    def vector(index):
        return owned_vectors[index * share : (index + 1) * share]

    return (
        output,
        input_grad,
        matrices[0],
        biases[0],
        matrices[1],
        matrices[2],
        biases[1],
        owned_out,
        vector(0),
        vector(1),
        vector(2),
        owned_inner,
        owned_vectors[6 * share : 6 * share + wide_share],
        owned_outer,
        vector(3),
        vector(4),
        vector(5),
    )


def solution(mesh):
    rows = P("batch", ("blk", "head"), None)
    matrix = P(ALL_AXES, None)
    vector = P(ALL_AXES)
    parameters = (
        matrix,
        vector,
        matrix,
        matrix,
        vector,
        matrix,
        vector,
        vector,
        vector,
        matrix,
        vector,
        matrix,
        vector,
        vector,
        vector,
    )
    return jax.shard_map(
        local,
        mesh=mesh,
        in_specs=(rows, P("batch"), rows) + parameters,
        out_specs=(rows, rows) + parameters,
        check_vma=False,
    )
```

```python
import functools
import math

import jax
import jax.numpy as jnp
from jax import lax
from jax.experimental import pallas as pl
from jax.experimental.pallas import tpu as pltpu
from jax.sharding import PartitionSpec as P

HEADS = 12
HEAD_DIM = 64
CORES = 2
MEMBERS = 4
EXTRA = 16
NEG_BIG = -1e30
EPSILON = 1e-06
F32 = jnp.float32
BF16 = jnp.bfloat16
ALL_AXES = ("batch", "blk", "head")
VMEM_LIMIT = 56 * 2**20
LAYER_VMEM = 60 * 2**20


def dot(left_op, right_op, left_dim, right_dim):
    return lax.dot_general(
        left_op, right_op, (((left_dim,), (right_dim,)), ((), ())), preferred_element_type=F32
    )


def shift_planes(array, distance):
    size = lax.axis_size("blk")
    route = [(i, (i + CORES * distance) % size) for i in range(size)]
    return lax.ppermute(array, "blk", route)


def shift_batch(array, distance):
    size = lax.axis_size("batch")
    return lax.ppermute(array, "batch", [(i, (i + distance) % size) for i in range(size)])


def swap_member(array, member):
    size = lax.axis_size("blk")
    if member == 1:
        return lax.ppermute(array, "head", [(0, 1), (1, 0)])
    if member == 2:
        return lax.ppermute(array, "blk", [(i, i ^ 1) for i in range(size)])
    route = [(i * 2 + j, (i ^ 1) * 2 + (j ^ 1)) for i in range(size) for j in range(2)]
    return lax.ppermute(array, ("blk", "head"), route)


def pick(array, index):
    return lax.dynamic_index_in_dim(array, index, 0, keepdims=False)


def reorder_members(stack, core, head_place):
    stack = jnp.where(core == 1, jnp.concatenate([stack[2:], stack[:2]]), stack)
    swapped = jnp.stack([stack[1], stack[0], stack[3], stack[2]])
    return jnp.where(head_place == 1, swapped, stack)


def in_order(pieces, place):
    stack = jnp.stack(pieces[::-1] * 2)
    return lax.dynamic_slice_in_dim(stack, len(pieces) - 1 - place, len(pieces), 0)


def split_three(row):
    high = row.astype(BF16)
    rest = row - high.astype(F32)
    middle = rest.astype(BF16)
    low = (rest - middle.astype(F32)).astype(BF16)
    return high, middle, low


def forward_kernel(block_k, members, q_ref, k_ref, v_ref, mask_ref, *rest):
    count = len(members)
    out_refs, sum_refs, (keys, values) = rest[:count], rest[count : 2 * count], rest[2 * count :]
    key_count = k_ref.shape[1]
    block_q = q_ref.shape[1] // MEMBERS
    rows = lax.broadcasted_iota(jnp.int32, (EXTRA, key_count), 0)
    joined = jnp.concatenate([k_ref[...]] * 3 + [mask_ref[...]], axis=0)
    keys[...] = joined.astype(F32).T.astype(BF16)
    values[:HEAD_DIM, :] = v_ref[...]
    values[HEAD_DIM:, :] = jnp.where(rows == 0, 1.0, 0.0).astype(BF16)
    rows_q = lax.broadcasted_iota(jnp.int32, (EXTRA, block_q), 0)
    ones_row = jnp.where(rows_q == 0, 1.0, 0.0).astype(BF16)
    scale = math.log2(math.e) / math.sqrt(HEAD_DIM)

    def prepared(member):
        scaled = q_ref[:, pl.ds(member * block_q, block_q)].astype(F32) * scale
        return jnp.concatenate(list(split_three(scaled)) + [ones_row], axis=0)

    def advance(state, scores, value_part):
        top, acc = state
        new_top = jnp.maximum(top, jnp.max(scores, axis=0, keepdims=True))
        probs = jnp.exp2(scores - new_top).astype(BF16)
        return new_top, acc * jnp.exp2(top - new_top) + dot(value_part, probs, 1, 0)

    for start in range(0, count, 2):
        queries = [prepared(member) for member in members[start : start + 2]]

        def key_block(j, states):
            k_start = pl.multiple_of(j * block_k, block_k)
            key_part = keys[pl.ds(k_start, block_k), :]
            value_part = values[:, pl.ds(k_start, block_k)]
            scores = [dot(key_part, query, 1, 0) for query in queries]
            return tuple(
                advance(state, score, value_part) for state, score in zip(states, scores)
            )

        begin = (jnp.full((1, block_q), NEG_BIG, F32), jnp.zeros((HEAD_DIM + EXTRA, block_q), F32))
        states = lax.fori_loop(0, key_count // block_k, key_block, (begin,) * len(queries))
        for index, (top, acc) in enumerate(states):
            total = acc[HEAD_DIM : HEAD_DIM + 1, :]
            out_refs[start + index][...] = (acc[:HEAD_DIM, :] / total).astype(BF16)
            sum_refs[start + index][...] = top * math.log(2.0) + jnp.log(total)


def head_specs(arrays, places):
    return [
        pl.BlockSpec((HEAD_DIM, array.shape[1]), functools.partial(lambda at, i: (at, 0), place))
        for array, place in zip(arrays, places)
    ]


def whole(shape):
    return pl.BlockSpec(shape, lambda *unused: (0,) * len(shape))


def attention_forward(queries, keys, values, places, mask_rows, members):
    part_count = queries.shape[1] // MEMBERS
    key_count = keys.shape[1]
    count = len(members)
    result = pl.pallas_call(
        functools.partial(forward_kernel, min(512, key_count), members),
        grid=(1,),
        in_specs=head_specs((queries, keys, values), places) + [whole((EXTRA, key_count))],
        out_specs=[whole((HEAD_DIM, part_count))] * count + [whole((1, part_count))] * count,
        out_shape=[jax.ShapeDtypeStruct((HEAD_DIM, part_count), BF16)] * count
        + [jax.ShapeDtypeStruct((1, part_count), F32)] * count,
        scratch_shapes=[
            pltpu.VMEM((key_count, 3 * HEAD_DIM + EXTRA), BF16),
            pltpu.VMEM((HEAD_DIM + EXTRA, key_count), BF16),
        ],
        compiler_params=pltpu.CompilerParams(vmem_limit_bytes=VMEM_LIMIT),
        cost_estimate=pl.CostEstimate(
            flops=16 * HEAD_DIM * count * part_count * key_count,
            transcendentals=count * part_count * key_count,
            bytes_accessed=8 * HEAD_DIM * key_count,
        ),
    )(queries, keys, values, mask_rows)
    return dict(zip(members, result[:count])), dict(zip(members, result[count:]))


def backward_kernel(block_q, chosen, first, last, q_ref, k_ref, v_ref, mask_ref, *rest):
    sum_refs, rest = rest[:MEMBERS], rest[MEMBERS:]
    out_refs, rest = rest[:MEMBERS], rest[MEMBERS:]
    grad_refs, rest = rest[:MEMBERS], rest[MEMBERS:]
    if not first:
        start_ref, rest = rest[0], rest[1:]
    result_refs, rest = rest[: len(chosen)], rest[len(chosen) :]
    if not last:
        partial_ref, rest = rest[0], rest[1:]
    elif not first:
        dq_refs, rest = rest[:MEMBERS], rest[MEMBERS:]
    query_rows, keys, grad_rows, values, scaled_q, grads, dq_acc, dkv = rest
    key_count = k_ref.shape[1]
    query_count = q_ref.shape[1]
    part = query_count // MEMBERS
    scale = 1.0 / math.sqrt(HEAD_DIM)
    places_q = lax.broadcasted_iota(jnp.int32, (EXTRA, query_count), 0)
    places_k = lax.broadcasted_iota(jnp.int32, (EXTRA, key_count), 0)

    def extra_rows(row, fourth):
        high, middle, low = [piece.astype(F32) for piece in split_three(row)]
        rows = jnp.where(
            places_q == 0, high, jnp.where(places_q == 1, middle, jnp.where(places_q == 2, low, 0.0))
        )
        return jnp.where(places_q == 3, fourth, rows).astype(BF16)

    query = (q_ref[...].astype(F32) * scale).astype(BF16)
    scaled_q[...] = query
    deltas = []
    for member in range(MEMBERS):
        grad = grad_refs[member][...]
        grads[:, member * part : (member + 1) * part] = grad
        product = grad.astype(F32) * out_refs[member][...].astype(F32)
        deltas.append(jnp.sum(product, axis=0, keepdims=True))
    deltas = jnp.concatenate(deltas, axis=1)
    sums = jnp.concatenate([sum_ref[...] for sum_ref in sum_refs], axis=1)
    joined_q = jnp.concatenate([query, extra_rows(-sums, 1.0)], axis=0)
    query_rows[...] = joined_q.astype(F32).T.astype(BF16)
    joined_g = jnp.concatenate([grads[...], extra_rows(-deltas, 0.0)], axis=0)
    grad_rows[...] = joined_g.astype(F32).T.astype(BF16)
    ones_rows = jnp.where(places_k < 3, 1.0, 0.0)
    mask_row = mask_ref[0:1, :].astype(F32)
    keys[:HEAD_DIM, :] = k_ref[...]
    keys[HEAD_DIM:, :] = jnp.where(places_k == 3, mask_row, ones_rows).astype(BF16)
    values[:HEAD_DIM, :] = v_ref[...]
    values[HEAD_DIM:, :] = ones_rows.astype(BF16)
    dq_acc[...] = jnp.zeros_like(dq_acc) if first else start_ref[...]

    def key_block(j, unused):
        k_start = pl.multiple_of((chosen.start + j * chosen.step) * part, part)
        key_part = keys[:, pl.ds(k_start, part)]
        value_part = values[:, pl.ds(k_start, part)]
        plain_keys = k_ref[:, pl.ds(k_start, part)]

        def query_block(i, carry):
            dk, dv = carry
            q_start = pl.multiple_of(i * block_q, block_q)
            probs = jnp.exp(dot(query_rows[pl.ds(q_start, block_q), :], key_part, 1, 0))
            moved = dot(grad_rows[pl.ds(q_start, block_q), :], value_part, 1, 0)
            grad_scores = (probs * moved).astype(BF16)
            dv = dv + dot(grads[:, pl.ds(q_start, block_q)], probs.astype(BF16), 1, 0)
            dk = dk + dot(scaled_q[:, pl.ds(q_start, block_q)], grad_scores, 1, 0)
            dq_acc[:, pl.ds(q_start, block_q)] += dot(plain_keys, grad_scores, 1, 1)
            return dk, dv

        zeros = jnp.zeros((HEAD_DIM, part), F32)
        dk, dv = lax.fori_loop(0, query_count // block_q, query_block, (zeros, zeros))
        place = pl.multiple_of(j * part, part)
        dkv[:HEAD_DIM, pl.ds(place, part)] = dk.astype(BF16)
        dkv[HEAD_DIM:, pl.ds(place, part)] = dv.astype(BF16)
        return 0

    lax.fori_loop(0, len(chosen), key_block, 0)

    def query_grads(member):
        return (dq_acc[:, member * part : (member + 1) * part] * scale).astype(BF16)

    together = first and last
    for index, result_ref in enumerate(result_refs):
        found = dkv[:, index * part : (index + 1) * part]
        if together:
            if chosen[index] < MEMBERS:
                result_ref[:HEAD_DIM, :] = query_grads(chosen[index])
            else:
                result_ref[:HEAD_DIM, :] = jnp.zeros((HEAD_DIM, part), BF16)
            result_ref[HEAD_DIM:, :] = found
        else:
            result_ref[...] = found
    if not last:
        partial_ref[...] = dq_acc[...]
    elif not first:
        for member in range(MEMBERS):
            dq_refs[member][...] = query_grads(member)


def attention_backward(
    queries, keys, values, places, mask_rows, sums, outs, grads, chosen, start=None, last=True
):
    query_count = queries.shape[1]
    key_count = keys.shape[1]
    part = query_count // MEMBERS
    wide = HEAD_DIM + EXTRA
    first = start is None
    height = (3 if first and last else 2) * HEAD_DIM
    count = len(chosen)
    results = [((height, part), BF16)] * count
    if not last:
        results.append(((HEAD_DIM, query_count), F32))
    elif not first:
        results += [((HEAD_DIM, part), BF16)] * MEMBERS
    extra = [] if first else [start]
    found = pl.pallas_call(
        functools.partial(backward_kernel, min(1024, query_count), chosen, first, last),
        grid=(1,),
        in_specs=head_specs((queries, keys, values), places)
        + [whole((EXTRA, key_count))]
        + [whole((1, part))] * MEMBERS
        + [whole((HEAD_DIM, part))] * MEMBERS
        + head_specs([grad for grad, place in grads], [place for grad, place in grads])
        + [whole(array.shape) for array in extra],
        out_specs=[whole(dims) for dims, dtype in results],
        out_shape=[jax.ShapeDtypeStruct(dims, dtype) for dims, dtype in results],
        scratch_shapes=[
            pltpu.VMEM((query_count, wide), BF16),
            pltpu.VMEM((wide, key_count), BF16),
            pltpu.VMEM((query_count, wide), BF16),
            pltpu.VMEM((wide, key_count), BF16),
            pltpu.VMEM((HEAD_DIM, query_count), BF16),
            pltpu.VMEM((HEAD_DIM, query_count), BF16),
            pltpu.VMEM((HEAD_DIM, query_count), F32),
            pltpu.VMEM((2 * HEAD_DIM, count * part), BF16),
        ],
        compiler_params=pltpu.CompilerParams(vmem_limit_bytes=VMEM_LIMIT),
        cost_estimate=pl.CostEstimate(
            flops=40 * HEAD_DIM * query_count * count * part,
            transcendentals=query_count * count * part,
            bytes_accessed=16 * HEAD_DIM * key_count,
        ),
    )(queries, keys, values, mask_rows, *sums, *outs, *[grad for grad, place in grads], *extra)
    return list(found[:count]), list(found[count:])


def joined_rows(refs, member):
    count = len(refs) // MEMBERS
    return jnp.concatenate([ref[...] for ref in refs[member * count : (member + 1) * count]])


def project_kernel(weight_ref, bias_ref, *rest):
    piece_refs, out_ref = rest[:-1], rest[-1]
    weight = weight_ref[...].astype(F32).T.astype(BF16)
    step = out_ref.shape[1] // MEMBERS
    for member in range(MEMBERS):
        lanes = slice(member * step, (member + 1) * step)
        rows = joined_rows(piece_refs, member)
        out_ref[:, lanes] = (dot(weight, rows, 1, 1) + bias_ref[...]).astype(BF16)


def project(weight, bias_column, pieces):
    count, (rows, width) = len(pieces), pieces[0].shape
    columns = weight.shape[1]
    return pl.pallas_call(
        project_kernel,
        grid=(1,),
        in_specs=[whole(weight.shape), whole(bias_column.shape)] + [whole((rows, width))] * count,
        out_specs=whole((columns, count * rows)),
        out_shape=jax.ShapeDtypeStruct((columns, count * rows), BF16),
        compiler_params=pltpu.CompilerParams(vmem_limit_bytes=VMEM_LIMIT),
        cost_estimate=pl.CostEstimate(
            flops=2 * count * rows * width * columns,
            transcendentals=0,
            bytes_accessed=4 * count * rows * width,
        ),
    )(weight, bias_column, *pieces)


def stacked(refs):
    parts = [ref[...] for ref in refs]
    return parts[0] if len(parts) == 1 else jnp.concatenate(parts)


def flatten(nested):
    return [array for slot in nested for member in slot for array in member]


def regroup(refs, counts):
    refs = list(refs)
    return [[[refs.pop(0) for _ in range(n)] for n in slot] for slot in counts]


def counts_of(nested):
    return [[len(member) for member in slot] for slot in nested]


def weight_grad_kernel(counts, pieces, chunk_rows, *rest):
    row_refs, grad_refs, out_ref = rest[:pieces], rest[pieces:-1], rest[-1]
    slots = regroup(grad_refs, counts)
    chunks = out_ref.shape[0]
    columns = out_ref.shape[2] // len(slots)
    part = slots[0][0][0].shape[1]
    ones = jnp.ones((8, part), BF16)
    totals, biases = [0.0] * len(slots), [0.0] * len(slots)
    for member in range(MEMBERS):
        rows = joined_rows(row_refs, member)
        for slot, members in enumerate(slots):
            grad = stacked(members[member])
            totals[slot] = totals[slot] + dot(grad, rows, 1, 0)
            biases[slot] = biases[slot] + dot(ones, grad, 1, 1)
    for slot in range(len(slots)):
        lanes = slice(slot * columns, (slot + 1) * columns)
        turned = totals[slot].T.astype(BF16)
        bias = biases[slot][0:1].astype(BF16)
        bias = jnp.broadcast_to(bias, (out_ref.shape[1] - chunk_rows, columns))
        for chunk in range(chunks):
            out_ref[chunk, :chunk_rows, lanes] = turned[chunk * chunk_rows : (chunk + 1) * chunk_rows]
            out_ref[chunk, chunk_rows:, lanes] = bias


def weight_grad(row_pieces, slots, chunks, chunk_rows, block_rows):
    arrays = flatten(slots)
    shape = (chunks, block_rows, len(slots) * 3 * HEAD_DIM)
    return pl.pallas_call(
        functools.partial(weight_grad_kernel, counts_of(slots), len(row_pieces), chunk_rows),
        grid=(1,),
        in_specs=[whole(array.shape) for array in list(row_pieces) + arrays],
        out_specs=whole(shape),
        out_shape=jax.ShapeDtypeStruct(shape, BF16),
        compiler_params=pltpu.CompilerParams(vmem_limit_bytes=VMEM_LIMIT),
        cost_estimate=pl.CostEstimate(
            flops=2 * shape[2] * len(row_pieces) * row_pieces[0].size,
            transcendentals=0,
            bytes_accessed=2 * len(row_pieces) * row_pieces[0].size,
        ),
    )(*row_pieces, *arrays)


def input_grad_kernel(counts, info_ref, acc_ref, *rest):
    slots = len(counts)
    weight_refs, rest = rest[:slots], rest[slots:]
    grads = regroup(rest[: sum(map(sum, counts))], counts)
    out_refs, joined = rest[sum(map(sum, counts)) : -1], rest[-1]
    total = acc_ref[...]
    width = total.shape[1]
    for slot, members in enumerate(grads):
        for member, refs in enumerate(members):
            start = info_ref[member]
            for ref in refs:
                height = ref.shape[0]
                joined[slot, pl.ds(pl.multiple_of(start, HEAD_DIM), height), :] = ref[...]
                start = start + height
        weight = weight_refs[slot][...].reshape(width, width)
        total = total + dot(joined[slot], weight, 0, 1)
    rows = acc_ref.shape[0] // len(out_refs)
    for index, out_ref in enumerate(out_refs):
        out_ref[...] = total[index * rows : (index + 1) * rows].astype(out_ref.dtype)


def input_grad_step(info, acc, weights, slots, out_count, dtype):
    arrays = flatten(slots)
    rows, width = acc.shape
    out = (rows // out_count, width)
    return pl.pallas_call(
        functools.partial(input_grad_kernel, counts_of(slots)),
        grid_spec=pltpu.PrefetchScalarGridSpec(
            num_scalar_prefetch=1,
            grid=(1,),
            in_specs=[whole(acc.shape)]
            + [pl.BlockSpec(dims, functools.partial(lambda at, i, info: at, place))
               for array, dims, place in weights]
            + [whole(array.shape) for array in arrays],
            out_specs=[whole(out)] * out_count,
            scratch_shapes=[pltpu.VMEM((len(slots), width, rows), BF16)],
        ),
        out_shape=[jax.ShapeDtypeStruct(out, dtype)] * out_count,
        compiler_params=pltpu.CompilerParams(vmem_limit_bytes=VMEM_LIMIT),
        cost_estimate=pl.CostEstimate(
            flops=2 * rows * width * width * len(slots),
            transcendentals=0,
            bytes_accessed=8 * rows * width,
        ),
    )(info, acc, *[array for array, dims, place in weights], *arrays)


def collect_kernel(count, place_ref, *rest):
    piece_refs, out_ref = rest[:count], rest[count]
    for index, piece_ref in enumerate(piece_refs):
        out_ref[lax.rem(place_ref[0] + index, count)] = piece_ref[...]


def collect(pieces, place):
    count, shape = len(pieces), pieces[0].shape
    return pl.pallas_call(
        functools.partial(collect_kernel, count),
        grid_spec=pltpu.PrefetchScalarGridSpec(
            num_scalar_prefetch=1,
            grid=(1,),
            in_specs=[whole(shape)] * count,
            out_specs=whole((count,) + shape),
        ),
        out_shape=jax.ShapeDtypeStruct((count,) + shape, pieces[0].dtype),
        compiler_params=pltpu.CompilerParams(vmem_limit_bytes=VMEM_LIMIT),
    )(place[None], *pieces)


def gelu_parts(value):
    size = jnp.abs(value) * math.sqrt(0.5)
    t = 1.0 / (1.0 + 0.3275911 * size)
    bell = jnp.exp(-0.5 * value * value)
    poly = 1.061405429 * t - 1.453152027
    poly = poly * t + 1.421413741
    poly = poly * t - 0.284496736
    poly = poly * t + 0.254829592
    tail = 0.5 * poly * t * bell
    share = jnp.where(value < 0, tail, 1.0 - tail)
    return value * share, share + value * bell * (1.0 / math.sqrt(2.0 * math.pi))


def row_mean(array):
    return jnp.mean(array, axis=-1, keepdims=True)


def column_sum(array):
    return jnp.sum(array, axis=0, keepdims=True)


def layer_kernel(blocks, planes, parts, info_ref, vectors_ref, inner_bias_ref, *rest):
    row_refs, rest = rest[:planes], rest[planes:]
    packed_out, packed_inner, packed_outer = rest[:3]
    att_refs, rest = rest[3 : 3 + parts], rest[3 + parts :]
    cot_refs, rest = rest[:planes], rest[planes:]
    final_refs, rest = rest[:planes], rest[planes:]
    grad_att_refs, rest = rest[: 2 * MEMBERS], rest[2 * MEMBERS :]
    resid_ref, grad_outer_w, grad_inner_w, grad_out_w, grad_vectors, grad_inner_bias = rest[:6]
    attended, hat1, scale1, low, acc, active, slope, grad_low, grad_hidden, weight_out = rest[6:]
    step = pl.program_id(0)
    row_count, width = acc.shape
    piece = row_count // planes
    group = width // MEMBERS
    block = jnp.where(step < blocks, step, step - blocks)
    pieces = [slice(k * piece, (k + 1) * piece) for k in range(planes)]

    def group_rows(member):
        return pl.ds(pl.multiple_of(info_ref[member], HEAD_DIM), group)

    def vector(index):
        return vectors_ref[index : index + 1, :]

    @pl.when(step == 0)
    def _():
        for index, att_ref in enumerate(att_refs):
            attended[index * HEAD_DIM : (index + 1) * HEAD_DIM, :] = att_ref[...]
        weight_out[...] = packed_out[...].reshape(width, width)
        weight = jnp.concatenate([weight_out[group_rows(m), :] for m in range(MEMBERS)])
        for k in range(planes):
            branch = dot(attended[:, pieces[k]], weight, 0, 0) + vector(0)
            value = row_refs[k][...].astype(F32) + branch
            centred = value - row_mean(value)
            scale = lax.rsqrt(row_mean(centred * centred) + EPSILON)
            hat = centred * scale
            normed = hat * vector(1) + vector(2)
            hat1[pieces[k], :] = hat
            scale1[pieces[k], :] = scale
            low[pieces[k], :] = normed.astype(BF16)
            acc[pieces[k], :] = normed + vector(3)
        grad_vectors[...] = jnp.zeros_like(grad_vectors)
        grad_inner_bias[...] = jnp.zeros_like(grad_inner_bias)

    @pl.when(step < blocks)
    def _():
        bias = inner_bias_ref[pl.ds(block, 1), :]
        weight_inner = packed_inner[...].reshape(width, width)
        weight_outer = packed_outer[...].reshape(width, width)
        for k in range(planes):
            inner = dot(low[pieces[k], :], weight_inner, 1, 0) + bias
            value, derivative = gelu_parts(inner)
            value = value.astype(BF16)
            active[block, pieces[k], :] = value
            slope[block, pieces[k], :] = derivative
            acc[pieces[k], :] += dot(value, weight_outer, 1, 0)

    @pl.when(step == blocks)
    def _():
        gain_sum, shift_sum, bias_sum = 0.0, 0.0, 0.0
        for k in range(planes):
            value = acc[pieces[k], :]
            centred = value - row_mean(value)
            scale = lax.rsqrt(row_mean(centred * centred) + EPSILON)
            hat = centred * scale
            final_refs[k][...] = (hat * vector(4) + vector(5)).astype(BF16)
            places = lax.broadcasted_iota(jnp.int32, (piece, width), 0)
            grad = jnp.where(
                places < info_ref[MEMBERS + k], cot_refs[k][...].astype(F32), 0.0
            )
            gain_sum += column_sum(grad * hat)
            shift_sum += column_sum(grad)
            grad = grad * vector(4)
            grad = scale * (grad - row_mean(grad) - hat * row_mean(grad * hat))
            rounded = grad.astype(BF16)
            bias_sum += column_sum(rounded.astype(F32))
            grad_low[pieces[k], :] = rounded
            acc[pieces[k], :] = grad
        grad_vectors[3:4, :] = bias_sum
        grad_vectors[4:5, :] = gain_sum
        grad_vectors[5:6, :] = shift_sum

    @pl.when(step >= blocks)
    def _():
        bias_sum = 0.0
        weight_inner = packed_inner[...].reshape(width, width)
        weight_outer = packed_outer[...].reshape(width, width)
        for k in range(planes):
            moved = dot(grad_low[pieces[k], :], weight_outer, 1, 1)
            grad = (moved * slope[block, pieces[k], :]).astype(BF16)
            grad_hidden[pieces[k], :] = grad
            bias_sum += column_sum(grad.astype(F32))
            acc[pieces[k], :] += dot(grad, weight_inner, 1, 1)
        grad_inner_bias[pl.ds(block, 1), :] = bias_sum
        for m in range(MEMBERS // 2):
            lanes = slice(m * 2 * group, (m + 1) * 2 * group)
            grad_outer_w[lanes, :] = dot(active[block, :, lanes], grad_low[...], 0, 0).astype(BF16)
            grad_inner_w[lanes, :] = dot(low[:, lanes], grad_hidden[...], 0, 0).astype(BF16)

    @pl.when(step == 2 * blocks - 1)
    def _():
        gain_sum, shift_sum, bias_sum = 0.0, 0.0, 0.0
        for k in range(planes):
            grad, hat = acc[pieces[k], :], hat1[pieces[k], :]
            gain_sum += column_sum(grad * hat)
            shift_sum += column_sum(grad)
            grad = grad * vector(1)
            grad = scale1[pieces[k], :] * (grad - row_mean(grad) - hat * row_mean(grad * hat))
            resid_ref[pieces[k], :] = grad
            rounded = grad.astype(BF16)
            bias_sum += column_sum(rounded.astype(F32))
            grad_low[pieces[k], :] = rounded
        grad_vectors[0:1, :] = bias_sum
        grad_vectors[1:2, :] = gain_sum
        grad_vectors[2:3, :] = shift_sum
        for m in range(MEMBERS):
            rows = slice(m * group, (m + 1) * group)
            grad_out_w[group_rows(m), :] = dot(attended[rows, :], grad_low[...], 1, 0).astype(BF16)
            moved = dot(weight_out[group_rows(m), :], grad_low[...], 1, 1).astype(BF16)
            grad_att_refs[2 * m][...] = moved[:HEAD_DIM, :]
            grad_att_refs[2 * m + 1][...] = moved[HEAD_DIM:, :]


def layer_rows(info, row_pieces, vectors, inner_bias, weights, att_parts, cot_pieces):
    width = row_pieces[0].shape[1]
    blocks, planes, parts = weights[0], len(cot_pieces), len(att_parts)
    hidden = blocks * width
    row_count = att_parts[0].shape[1]
    piece = row_count // planes
    group = width // MEMBERS
    once = pl.Buffered(1)

    def fixed(shape):
        return pl.BlockSpec(shape, lambda *unused: (0,) * len(shape), pipeline_mode=once)

    square = (width, width)
    weight_specs = [
        pl.BlockSpec(
            dims,
            functools.partial(lambda at, i, info: at(lax.rem(i, blocks)), place),
            pipeline_mode=pl.Buffered(1 if index == 0 else 2),
        )
        for index, (array, dims, place) in enumerate(weights[1:])
    ]
    grad_spec = pl.BlockSpec(square, lambda i, info: (jnp.maximum(i - blocks, 0), 0))
    small = [fixed((8, width)), fixed((8, width))]

    def shape(dims, dtype):
        return jax.ShapeDtypeStruct(dims, dtype)

    result = pl.pallas_call(
        functools.partial(layer_kernel, blocks, planes, parts),
        grid_spec=pltpu.PrefetchScalarGridSpec(
            num_scalar_prefetch=1,
            grid=(2 * blocks,),
            in_specs=small
            + [fixed((piece, width))] * planes
            + weight_specs
            + [fixed((HEAD_DIM, row_count))] * parts
            + [fixed((piece, width))] * planes,
            out_specs=[fixed((piece, width))] * planes
            + [fixed((HEAD_DIM, row_count)), fixed((group - HEAD_DIM, row_count))] * MEMBERS
            + [fixed((row_count, width)), grad_spec, grad_spec, fixed(square)]
            + small,
            scratch_shapes=[
                pltpu.VMEM((width, row_count), BF16),
                pltpu.VMEM((row_count, width), F32),
                pltpu.VMEM((row_count, 1), F32),
                pltpu.VMEM((row_count, width), BF16),
                pltpu.VMEM((row_count, width), F32),
                pltpu.VMEM((blocks, row_count, width), BF16),
                pltpu.VMEM((blocks, row_count, width), F32),
                pltpu.VMEM((row_count, width), BF16),
                pltpu.VMEM((row_count, width), BF16),
                pltpu.VMEM(square, BF16),
            ],
        ),
        out_shape=[shape((piece, width), BF16)] * planes
        + [shape((HEAD_DIM, row_count), BF16), shape((group - HEAD_DIM, row_count), BF16)] * MEMBERS
        + [
            shape((row_count, width), F32),
            shape((hidden, width), BF16),
            shape((hidden, width), BF16),
            shape(square, BF16),
            shape((8, width), F32),
            shape((8, width), F32),
        ],
        compiler_params=pltpu.CompilerParams(vmem_limit_bytes=LAYER_VMEM),
        cost_estimate=pl.CostEstimate(
            flops=12 * row_count * width * hidden,
            transcendentals=row_count * hidden,
            bytes_accessed=8 * width * hidden,
        ),
    )(
        info,
        vectors,
        inner_bias,
        *row_pieces,
        *[array for array, dims, place in weights[1:]],
        *att_parts,
        *cot_pieces,
    )
    return result[:planes], result[planes : planes + 2 * MEMBERS], result[planes + 2 * MEMBERS :]


def pad_rows(array, count):
    return jnp.concatenate([array, jnp.zeros((count,) + array.shape[1:], array.dtype)])


def local(
    layer_input,
    lengths,
    cotangent,
    w_query,
    b_query,
    w_key,
    w_value,
    b_value,
    w_attn_out,
    b_attn_out,
    norm1_gain,
    norm1_bias,
    w_inner,
    b_inner,
    w_outer,
    b_outer,
    norm2_gain,
    norm2_bias,
):
    seqs, part_rows, width = layer_input.shape
    batches = lax.axis_size("batch")
    planes = lax.axis_size("blk") // CORES
    devices = batches * planes * MEMBERS
    spread_planes = planes // seqs
    piece = part_rows // spread_planes
    row_count = planes * piece
    share = width // devices
    wide_share = w_outer.shape[0]
    hidden = wide_share * devices
    folds = hidden // width
    group = width // MEMBERS

    plane = lax.axis_index("blk") // CORES
    core = lax.axis_index("blk") % CORES
    head_place = lax.axis_index("head")
    batch_place = lax.axis_index("batch")
    device = (batch_place * planes + plane) * MEMBERS + core * 2 + head_place
    seq_length = pick(lengths, plane // spread_planes)
    part = plane % spread_planes

    def places(other_plane):
        source = (other_plane - jnp.arange(planes, dtype=jnp.int32)) % planes
        member = jnp.arange(MEMBERS, dtype=jnp.int32)
        cores = core ^ (member // 2)
        heads = head_place ^ (member % 2)
        base = (source[None, :] * CORES + cores[:, None]) * 2 + heads[:, None]
        offset = (other_plane % spread_planes) * piece + jnp.arange(piece, dtype=jnp.int32)
        return (base[:, :, None] * part_rows + offset).reshape(-1)

    def chunks_for_planes(array):
        chunks = array.reshape(planes, piece, width)
        return [pick(chunks, (plane + distance) % planes) for distance in range(planes)]

    def to_planes(array):
        chunks = chunks_for_planes(array)
        return [chunks[0]] + [shift_planes(chunks[k], k) for k in range(1, planes)]

    stage = lax.optimization_barrier

    own_group = core * 2 + head_place
    heads_here = HEADS // MEMBERS
    piece_rows = (share // 8 + 1) * 8
    kinds = jnp.stack([w_query, w_key, w_value], axis=1)
    kinds = kinds.reshape(share, 3, MEMBERS, group)
    by_group = jnp.moveaxis(kinds, 2, 0).reshape(MEMBERS, share, 3 * group)
    bias_row = jnp.pad(jnp.concatenate([b_query, b_value]), (0, 3 * group - 2 * share))
    tail_rows = jnp.pad(bias_row[None], ((0, piece_rows - share - 1), (0, 0)))
    tail_rows = jnp.broadcast_to(tail_rows, (MEMBERS,) + tail_rows.shape)
    by_group = jnp.concatenate([by_group, tail_rows], axis=1)
    by_member = reorder_members(by_group, core, head_place)

    chunks = chunks_for_planes(layer_input)
    own_pieces = chunks[:1] + [shift_planes(chunks[k], k) for k in range(1, planes - 1)]
    head_pieces = [swap_member(own_pieces[0], 1)]
    gathered = [by_member[0]] + [
        swap_member(by_member[member], member) for member in range(1, MEMBERS)
    ]
    own_pieces, head_pieces, gathered, chunks = stage((own_pieces, head_pieces, gathered, chunks))
    own_pieces = own_pieces + [shift_planes(chunks[-1], planes - 1)]
    head_pieces = head_pieces + [swap_member(own_pieces[k], 1) for k in range(1, planes - 1)]
    core_pieces = [swap_member(own_pieces[0], 2)]
    both_pieces = [swap_member(head_pieces[0], 2)]
    gathered = reorder_members(jnp.stack(gathered), core, head_place)
    gathered = [gathered] + [shift_planes(gathered, distance) for distance in range(1, planes)]
    own_pieces, head_pieces, core_pieces, both_pieces, gathered = stage(
        (own_pieces, head_pieces, core_pieces, both_pieces, gathered)
    )
    core_pieces = core_pieces + [swap_member(own_pieces[k], 2) for k in range(1, planes)]
    both_pieces = both_pieces + [swap_member(head_pieces[k], 2) for k in range(1, planes - 1)]
    head_pieces = head_pieces + [swap_member(own_pieces[-1], 1)]
    gathered = in_order(gathered, plane)
    gathered = [gathered] + [shift_batch(gathered, distance) for distance in range(1, batches)]
    core_pieces, both_pieces, head_pieces, gathered = stage(
        (core_pieces, both_pieces, head_pieces, gathered)
    )
    both_pieces = both_pieces + [swap_member(head_pieces[-1], 2)]
    gathered = in_order(gathered, batch_place)
    gathered = gathered.reshape(devices, piece_rows, 3 * group)
    own_weight = gathered[:, :share].reshape(width, 3 * group)
    bias_query = gathered[:, share, :share].reshape(MEMBERS, group)
    bias_value = gathered[:, share, share : 2 * share].reshape(MEMBERS, group)
    own_bias = jnp.concatenate(
        [
            pick(bias_query, own_group),
            jnp.zeros((group,), BF16),
            pick(bias_value, own_group),
        ]
    ).astype(F32)

    all_pieces = own_pieces + head_pieces + core_pieces + both_pieces
    valid_own = places(plane) < seq_length
    row_starts = (own_group ^ jnp.arange(MEMBERS, dtype=jnp.int32)) * group
    kept_rows = seq_length - places(plane)[:row_count:piece]
    info = jnp.concatenate([row_starts, kept_rows])

    def other_plane(distance):
        return (plane // spread_planes) * spread_planes + (part - distance) % spread_planes

    def shift_parts(array, distance):
        size = lax.axis_size("blk")
        route = []
        for i in range(size):
            start = i // CORES // spread_planes * spread_planes
            target = start + (i // CORES - start + distance) % spread_planes
            route.append((i, target * CORES + i % CORES))
        return lax.ppermute(array, "blk", route)

    qkv = project(own_weight, own_bias[:, None], all_pieces)
    late_cotangent, qkv = lax.optimization_barrier((cotangent, qkv))
    cot_pieces = to_planes(late_cotangent)

    small = jnp.concatenate(
        [b_attn_out, norm1_gain, norm1_bias, b_outer, norm2_gain, norm2_bias, b_inner]
    )
    small_row = jnp.pad(small, (0, width - small.shape[0]))[None]
    inner_rows = jnp.swapaxes(w_inner.reshape(share, folds, width), 0, 1).reshape(-1, width)
    second_pack = jnp.concatenate([w_outer, inner_rows, w_attn_out, small_row])
    second_pack = pad_rows(second_pack, -second_pack.shape[0] % 8)
    second_pack, gate = lax.optimization_barrier((second_pack, head_pieces[-1]))
    second = lax.all_gather(second_pack, ALL_AXES, axis=0, tiled=False)
    slots = jnp.stack([w_query, w_key, w_value], axis=1)
    slots = slots.reshape(share, 3, MEMBERS, heads_here, HEAD_DIM)
    slots = jnp.transpose(slots, (3, 0, 2, 1, 4)).reshape(heads_here * share, width)
    slots, gate = lax.optimization_barrier((slots, qkv[0, 0]))
    third = lax.all_gather(slots, ALL_AXES, axis=0, tiled=False)

    inner_start = wide_share
    out_start = wide_share + share * folds
    small_all = second[:, out_start + share]
    vectors = jnp.swapaxes(small_all[:, : 6 * share].reshape(devices, 6, share), 0, 1)
    vectors = pad_rows(vectors.reshape(6, width).astype(F32), 2)
    bias_inner = small_all[:, 6 * share : 6 * share + wide_share].astype(F32)
    bias_inner = pad_rows(bias_inner.reshape(folds, width), 8 - folds)
    square = (width, width)
    if share % 8 == 0:
        narrow = (devices, share, width)
        layer_weights = (
            folds,
            (second, narrow, lambda j: (0, out_start // share, 0)),
            (second, narrow, lambda j: (0, inner_start // share + j, 0)),
            (second, (devices // folds, wide_share, width), lambda j: (j, 0, 0)),
        )
        slot_weights = [(third, narrow, (0, slot, 0)) for slot in range(heads_here)]
    else:
        inner = second[:, inner_start:out_start].reshape(devices, folds, share, width)
        inner = jnp.swapaxes(inner, 0, 1).reshape((folds,) + square)
        outer = second[:, :wide_share].reshape((folds,) + square)
        layer_weights = (
            folds,
            (second[:, out_start : out_start + share].reshape(square), square, lambda j: (0, 0)),
            (inner, (1,) + square, lambda j: (j, 0, 0)),
            (outer, (1,) + square, lambda j: (j, 0, 0)),
        )
        slot_weights = [
            (third[:, slot * share : (slot + 1) * share].reshape(square), square, (0, 0))
            for slot in range(heads_here)
        ]

    queries = keys = values = qkv
    starts = (0, heads_here, 2 * heads_here)
    valid_keys = [valid_own]
    if spread_planes > 1:
        sides = [qkv[group:]]
        for distance in range(1, spread_planes):
            sides.append(shift_parts(qkv[group:], distance))
            valid_keys.append(places(other_plane(distance)) < seq_length)
        keys = values = jnp.concatenate(sides, axis=1)
        starts = (0, 0, heads_here)
    valid = jnp.concatenate(valid_keys)
    mask_row = jnp.where(valid, 0.0, NEG_BIG).astype(BF16)[None]
    mask_rows = pad_rows(mask_row, EXTRA - 1)

    def to_members(pieces):
        return [pieces[0]] + [
            swap_member(pieces[member], member) for member in range(1, MEMBERS)
        ]

    far, near = range(1, MEMBERS, 2), range(0, MEMBERS, 2)
    outs, sums, parts = [], [], []
    for slot in range(heads_here):
        slot_at = tuple(start + slot for start in starts)
        chosen = [range(MEMBERS)] if slot < heads_here - 1 else [far, near]
        out, total, moved = {}, {}, {}
        for members in chosen:
            found = attention_forward(queries, keys, values, slot_at, mask_rows, members)
            out.update(found[0])
            total.update(found[1])
            for member in members:
                piece_out = found[0][member]
                moved[member] = swap_member(piece_out, member) if member else piece_out
        outs.append([out[member] for member in range(MEMBERS)])
        sums.append([total[member] for member in range(MEMBERS)])
        parts.append(moved)
    att_parts = [parts[slot][member] for member in range(MEMBERS) for slot in range(heads_here)]
    final_pieces, grad_att, more = layer_rows(
        info, own_pieces, vectors, bias_inner, layer_weights, att_parts, cot_pieces
    )
    output_pieces = [final_pieces[0]] + [
        shift_planes(final_pieces[distance], -distance) for distance in range(1, planes)
    ]
    grad_input, grad_outer_w, grad_inner_w, grad_out_w, grad_vectors, grad_inner_bias = more

    vector_pack = jnp.swapaxes(grad_vectors[:6].reshape(6, devices, share), 0, 1)
    vector_pack = jnp.concatenate(
        [
            vector_pack.reshape(devices, 6 * share),
            grad_inner_bias[:folds].reshape(devices, wide_share),
        ],
        axis=1,
    ).astype(BF16)
    vector_pack = jnp.pad(vector_pack, ((0, 0), (0, width - vector_pack.shape[1])))
    pack_rows = out_start + share
    grad_pack = jnp.concatenate(
        [
            grad_outer_w.reshape(devices, wide_share, width),
            jnp.swapaxes(grad_inner_w.reshape(folds, devices, share, width), 0, 1).reshape(
                devices, folds * share, width
            ),
            grad_out_w.reshape(devices, share, width),
            jnp.pad(vector_pack[:, None], ((0, 0), (0, 7 - pack_rows % 8), (0, 0))),
        ],
        axis=1,
    )
    owned = lax.psum_scatter(grad_pack, ALL_AXES, scatter_dimension=0, tiled=True)[0].astype(F32)
    owned_outer = owned[:wide_share]
    owned_inner = owned[inner_start:out_start].reshape(folds, share, width)
    owned_inner = jnp.swapaxes(owned_inner, 0, 1).reshape(share, hidden)
    owned_out = owned[out_start : out_start + share]
    owned_vectors = owned[out_start + share]

    chunk_rows = width // (batches * planes)
    block_rows = chunk_rows + -chunk_rows % 16 + 16

    def own_places(found):
        own = {index: array for index, array in found.items() if index < MEMBERS}
        for index, array in found.items():
            if index >= MEMBERS:
                moved = shift_parts(array, -(index // MEMBERS)).astype(F32)
                kept = own[index % MEMBERS]
                own[index % MEMBERS] = (kept.astype(F32) + moved).astype(BF16)
        return own

    def send(member, array):
        return swap_member(array, member) if member else array

    pieces_here = MEMBERS * spread_planes
    kept_slots, sent_slots = [], []
    for slot in range(heads_here):
        if slot < 2:
            grad_sent = [send(member, grad_att[2 * member + slot]) for member in range(MEMBERS)]
        slot_at = tuple(start + slot for start in starts)
        given = (queries, keys, values, slot_at, mask_rows, sums[slot], outs[slot])
        place = max(slot - 1, 0)
        if slot == 1:
            output_pieces, grad_sent = lax.optimization_barrier((output_pieces, grad_sent))
        if slot < heads_here - 1:
            chosen = range(pieces_here)
            grad_side = [(array, place) for array in grad_sent]
            found, unused = attention_backward(*given, grad_side, chosen)
            own = own_places(dict(zip(chosen, found)))
            kept_slots.append([[own[member]] for member in range(MEMBERS)])
            sent_slots.append([[send(member, own[member])] for member in range(MEMBERS)])
            continue
        sent_slots[:-1], grad_sent = lax.optimization_barrier((sent_slots[:-1], grad_sent))
        grad_side = [(array, place) for array in grad_sent]
        chosen = range(1, pieces_here, 2)
        found, (partial,) = attention_backward(*given, grad_side, chosen, last=False)
        own = own_places(dict(zip(chosen, found)))
        sent = {member: send(member, own[member]) for member in far}
        grad_input = input_grad_step(
            row_starts, grad_input, slot_weights[:-1], sent_slots, 1, F32
        )[0]
        partial, grad_input = lax.optimization_barrier((partial, grad_input))
        chosen = range(0, pieces_here, 2)
        found, query_grads = attention_backward(*given, grad_side, chosen, start=partial)
        own.update(own_places(dict(zip(chosen, found))))
        sent.update({member: send(member, own[member]) for member in near})
        kept_slots.append([[query_grads[member], own[member]] for member in range(MEMBERS)])
        last_sent = [
            [send(member, query_grads[member]), sent[member]] for member in range(MEMBERS)
        ]
    input_pieces = input_grad_step(
        row_starts, grad_input, slot_weights[-1:], [last_sent], planes, BF16
    )
    chunks = weight_grad(all_pieces, kept_slots, batches * planes, chunk_rows, block_rows)
    chunks = chunks.reshape((batches, planes) + chunks.shape[1:])
    parts = [pick(chunks, (batch_place + distance) % batches) for distance in range(batches)]

    def move(first, last):
        return [shift_planes(input_pieces[k], -k) for k in range(first, last)]

    parts, input_pieces = stage((parts, input_pieces))
    arrived = move(1, 2)
    moved = [shift_batch(parts[distance], distance) for distance in range(1, batches)]
    arrived, moved = stage((arrived, moved))
    total = sum([part_in.astype(F32) for part_in in [parts[0]] + moved])
    sending = total.astype(BF16)
    sending = [pick(sending, (plane + distance) % planes) for distance in range(1, planes)]
    arrived = arrived + move(2, planes - 1)
    moved = [shift_planes(sending[k - 1], k) for k in range(1, planes)]
    arrived, moved, total = stage((arrived, moved, total))
    total = pick(total, plane) + sum([part_in.astype(F32) for part_in in moved])
    columns = total.shape[-1]
    member_rows = total[:chunk_rows].reshape(MEMBERS, share, columns)
    member_rows = reorder_members(member_rows, core, head_place)
    tail = jnp.broadcast_to(total[chunk_rows], (MEMBERS, piece_rows - share, columns))
    sending = jnp.concatenate([member_rows, tail], axis=1)
    arrived = arrived + move(planes - 1, planes)
    got = [sending[0]] + [
        swap_member(sending[member], member) for member in range(1, MEMBERS)
    ]
    got = reorder_members(jnp.stack(got), core, head_place)
    got = got.reshape(MEMBERS, piece_rows, heads_here, 3, HEAD_DIM)
    input_grad = collect([input_pieces[0]] + arrived, plane).reshape(seqs, part_rows, width)
    output = collect(output_pieces, plane).reshape(seqs, part_rows, width)
    matrices = [
        jnp.swapaxes(got[:, :share, :, i], 0, 1).reshape(share, width) for i in range(3)
    ]
    biases = [
        lax.dynamic_slice_in_dim(got[:, share, :, i].reshape(width), device * share, share)
        for i in (0, 2)
    ]

    def vector(index):
        return owned_vectors[index * share : (index + 1) * share]

    return (
        output,
        input_grad,
        matrices[0],
        biases[0],
        matrices[1],
        matrices[2],
        biases[1],
        owned_out,
        vector(0),
        vector(1),
        vector(2),
        owned_inner,
        owned_vectors[6 * share : 6 * share + wide_share],
        owned_outer,
        vector(3),
        vector(4),
        vector(5),
    )


def solution(mesh):
    rows = P("batch", ("blk", "head"), None)
    matrix = P(ALL_AXES, None)
    vector = P(ALL_AXES)
    parameters = (
        matrix,
        vector,
        matrix,
        matrix,
        vector,
        matrix,
        vector,
        vector,
        vector,
        matrix,
        vector,
        matrix,
        vector,
        vector,
        vector,
    )
    return jax.shard_map(
        local,
        mesh=mesh,
        in_specs=(rows, P("batch"), rows) + parameters,
        out_specs=(rows, rows) + parameters,
        check_vma=False,
    )
```

```python
import functools
import math

import jax
import jax.numpy as jnp
from jax import lax
from jax.experimental import pallas as pl
from jax.experimental.pallas import tpu as pltpu
from jax.sharding import PartitionSpec as P

HEADS = 12
HEAD_DIM = 64
CORES = 2
MEMBERS = 4
EXTRA = 16
NEG_BIG = -1e30
EPSILON = 1e-06
F32 = jnp.float32
BF16 = jnp.bfloat16
ALL_AXES = ("batch", "blk", "head")
VMEM_LIMIT = 56 * 2**20
LAYER_VMEM = 60 * 2**20


def dot(left_op, right_op, left_dim, right_dim):
    return lax.dot_general(
        left_op, right_op, (((left_dim,), (right_dim,)), ((), ())), preferred_element_type=F32
    )


def shift_planes(array, distance):
    size = lax.axis_size("blk")
    route = [(i, (i + CORES * distance) % size) for i in range(size)]
    return lax.ppermute(array, "blk", route)


def exchange_planes(stack):
    size = lax.axis_size("blk")
    groups = [list(range(core, size, CORES)) for core in range(CORES)]
    return lax.all_to_all(stack, "blk", 0, 0, axis_index_groups=groups, tiled=True)


def shift_batch(array, distance):
    size = lax.axis_size("batch")
    return lax.ppermute(array, "batch", [(i, (i + distance) % size) for i in range(size)])


def swap_member(array, member):
    size = lax.axis_size("blk")
    if member == 1:
        return lax.ppermute(array, "head", [(0, 1), (1, 0)])
    if member == 2:
        return lax.ppermute(array, "blk", [(i, i ^ 1) for i in range(size)])
    route = [(i * 2 + j, (i ^ 1) * 2 + (j ^ 1)) for i in range(size) for j in range(2)]
    return lax.ppermute(array, ("blk", "head"), route)


def pick(array, index):
    return lax.dynamic_index_in_dim(array, index, 0, keepdims=False)


def reorder_members(stack, core, head_place):
    stack = jnp.where(core == 1, jnp.concatenate([stack[2:], stack[:2]]), stack)
    swapped = jnp.stack([stack[1], stack[0], stack[3], stack[2]])
    return jnp.where(head_place == 1, swapped, stack)


def in_order(pieces, place):
    stack = jnp.stack(pieces[::-1] * 2)
    return lax.dynamic_slice_in_dim(stack, len(pieces) - 1 - place, len(pieces), 0)


def split_three(row):
    high = row.astype(BF16)
    rest = row - high.astype(F32)
    middle = rest.astype(BF16)
    low = (rest - middle.astype(F32)).astype(BF16)
    return high, middle, low


def forward_kernel(block_k, members, q_ref, k_ref, v_ref, mask_ref, *rest):
    count = len(members)
    out_refs, sum_refs, (keys, values) = rest[:count], rest[count : 2 * count], rest[2 * count :]
    key_count = k_ref.shape[1]
    block_q = q_ref.shape[1] // MEMBERS
    rows = lax.broadcasted_iota(jnp.int32, (EXTRA, key_count), 0)
    joined = jnp.concatenate([k_ref[...]] * 3 + [mask_ref[...]], axis=0)
    keys[...] = joined.astype(F32).T.astype(BF16)
    values[:HEAD_DIM, :] = v_ref[...]
    values[HEAD_DIM:, :] = jnp.where(rows == 0, 1.0, 0.0).astype(BF16)
    rows_q = lax.broadcasted_iota(jnp.int32, (EXTRA, block_q), 0)
    ones_row = jnp.where(rows_q == 0, 1.0, 0.0).astype(BF16)
    scale = math.log2(math.e) / math.sqrt(HEAD_DIM)

    def prepared(member):
        scaled = q_ref[:, pl.ds(member * block_q, block_q)].astype(F32) * scale
        return jnp.concatenate(list(split_three(scaled)) + [ones_row], axis=0)

    def advance(state, scores, value_part):
        top, acc = state
        new_top = jnp.maximum(top, jnp.max(scores, axis=0, keepdims=True))
        probs = jnp.exp2(scores - new_top).astype(BF16)
        return new_top, acc * jnp.exp2(top - new_top) + dot(value_part, probs, 1, 0)

    for start in range(0, count, 2):
        queries = [prepared(member) for member in members[start : start + 2]]

        def key_block(j, states):
            k_start = pl.multiple_of(j * block_k, block_k)
            key_part = keys[pl.ds(k_start, block_k), :]
            value_part = values[:, pl.ds(k_start, block_k)]
            scores = [dot(key_part, query, 1, 0) for query in queries]
            return tuple(
                advance(state, score, value_part) for state, score in zip(states, scores)
            )

        begin = (jnp.full((1, block_q), NEG_BIG, F32), jnp.zeros((HEAD_DIM + EXTRA, block_q), F32))
        states = lax.fori_loop(0, key_count // block_k, key_block, (begin,) * len(queries))
        for index, (top, acc) in enumerate(states):
            total = acc[HEAD_DIM : HEAD_DIM + 1, :]
            out_refs[start + index][...] = (acc[:HEAD_DIM, :] / total).astype(BF16)
            sum_refs[start + index][...] = top * math.log(2.0) + jnp.log(total)


def head_specs(arrays, places):
    return [
        pl.BlockSpec((HEAD_DIM, array.shape[1]), functools.partial(lambda at, i: (at, 0), place))
        for array, place in zip(arrays, places)
    ]


def whole(shape):
    return pl.BlockSpec(shape, lambda *unused: (0,) * len(shape))


def attention_forward(queries, keys, values, places, mask_rows, members):
    part_count = queries.shape[1] // MEMBERS
    key_count = keys.shape[1]
    count = len(members)
    result = pl.pallas_call(
        functools.partial(forward_kernel, min(512, key_count), members),
        grid=(1,),
        in_specs=head_specs((queries, keys, values), places) + [whole((EXTRA, key_count))],
        out_specs=[whole((HEAD_DIM, part_count))] * count + [whole((1, part_count))] * count,
        out_shape=[jax.ShapeDtypeStruct((HEAD_DIM, part_count), BF16)] * count
        + [jax.ShapeDtypeStruct((1, part_count), F32)] * count,
        scratch_shapes=[
            pltpu.VMEM((key_count, 3 * HEAD_DIM + EXTRA), BF16),
            pltpu.VMEM((HEAD_DIM + EXTRA, key_count), BF16),
        ],
        compiler_params=pltpu.CompilerParams(vmem_limit_bytes=VMEM_LIMIT),
        cost_estimate=pl.CostEstimate(
            flops=16 * HEAD_DIM * count * part_count * key_count,
            transcendentals=count * part_count * key_count,
            bytes_accessed=8 * HEAD_DIM * key_count,
        ),
    )(queries, keys, values, mask_rows)
    return dict(zip(members, result[:count])), dict(zip(members, result[count:]))


def backward_kernel(block_q, chosen, first, last, q_ref, k_ref, v_ref, mask_ref, *rest):
    sum_refs, rest = rest[:MEMBERS], rest[MEMBERS:]
    out_refs, rest = rest[:MEMBERS], rest[MEMBERS:]
    grad_refs, rest = rest[:MEMBERS], rest[MEMBERS:]
    if not first:
        start_ref, rest = rest[0], rest[1:]
    result_refs, rest = rest[: len(chosen)], rest[len(chosen) :]
    if not last:
        partial_ref, rest = rest[0], rest[1:]
    elif not first:
        dq_refs, rest = rest[:MEMBERS], rest[MEMBERS:]
    query_rows, keys, grad_rows, values, scaled_q, grads, dq_acc, dkv = rest
    key_count = k_ref.shape[1]
    query_count = q_ref.shape[1]
    part = query_count // MEMBERS
    scale = 1.0 / math.sqrt(HEAD_DIM)
    places_q = lax.broadcasted_iota(jnp.int32, (EXTRA, query_count), 0)
    places_k = lax.broadcasted_iota(jnp.int32, (EXTRA, key_count), 0)

    def extra_rows(row, fourth):
        high, middle, low = [piece.astype(F32) for piece in split_three(row)]
        rows = jnp.where(
            places_q == 0, high, jnp.where(places_q == 1, middle, jnp.where(places_q == 2, low, 0.0))
        )
        return jnp.where(places_q == 3, fourth, rows).astype(BF16)

    query = (q_ref[...].astype(F32) * scale).astype(BF16)
    scaled_q[...] = query
    deltas = []
    for member in range(MEMBERS):
        grad = grad_refs[member][...]
        grads[:, member * part : (member + 1) * part] = grad
        product = grad.astype(F32) * out_refs[member][...].astype(F32)
        deltas.append(jnp.sum(product, axis=0, keepdims=True))
    deltas = jnp.concatenate(deltas, axis=1)
    sums = jnp.concatenate([sum_ref[...] for sum_ref in sum_refs], axis=1)
    joined_q = jnp.concatenate([query, extra_rows(-sums, 1.0)], axis=0)
    query_rows[...] = joined_q.astype(F32).T.astype(BF16)
    joined_g = jnp.concatenate([grads[...], extra_rows(-deltas, 0.0)], axis=0)
    grad_rows[...] = joined_g.astype(F32).T.astype(BF16)
    ones_rows = jnp.where(places_k < 3, 1.0, 0.0)
    mask_row = mask_ref[0:1, :].astype(F32)
    keys[:HEAD_DIM, :] = k_ref[...]
    keys[HEAD_DIM:, :] = jnp.where(places_k == 3, mask_row, ones_rows).astype(BF16)
    values[:HEAD_DIM, :] = v_ref[...]
    values[HEAD_DIM:, :] = ones_rows.astype(BF16)
    dq_acc[...] = jnp.zeros_like(dq_acc) if first else start_ref[...]

    def key_block(j, unused):
        k_start = pl.multiple_of((chosen.start + j * chosen.step) * part, part)
        key_part = keys[:, pl.ds(k_start, part)]
        value_part = values[:, pl.ds(k_start, part)]
        plain_keys = k_ref[:, pl.ds(k_start, part)]

        def query_block(i, carry):
            dk, dv = carry
            q_start = pl.multiple_of(i * block_q, block_q)
            probs = jnp.exp(dot(query_rows[pl.ds(q_start, block_q), :], key_part, 1, 0))
            moved = dot(grad_rows[pl.ds(q_start, block_q), :], value_part, 1, 0)
            grad_scores = (probs * moved).astype(BF16)
            dv = dv + dot(grads[:, pl.ds(q_start, block_q)], probs.astype(BF16), 1, 0)
            dk = dk + dot(scaled_q[:, pl.ds(q_start, block_q)], grad_scores, 1, 0)
            dq_acc[:, pl.ds(q_start, block_q)] += dot(plain_keys, grad_scores, 1, 1)
            return dk, dv

        zeros = jnp.zeros((HEAD_DIM, part), F32)
        dk, dv = lax.fori_loop(0, query_count // block_q, query_block, (zeros, zeros))
        place = pl.multiple_of(j * part, part)
        dkv[:HEAD_DIM, pl.ds(place, part)] = dk.astype(BF16)
        dkv[HEAD_DIM:, pl.ds(place, part)] = dv.astype(BF16)
        return 0

    lax.fori_loop(0, len(chosen), key_block, 0)

    def query_grads(member):
        return (dq_acc[:, member * part : (member + 1) * part] * scale).astype(BF16)

    together = first and last
    for index, result_ref in enumerate(result_refs):
        found = dkv[:, index * part : (index + 1) * part]
        if together:
            if chosen[index] < MEMBERS:
                result_ref[:HEAD_DIM, :] = query_grads(chosen[index])
            else:
                result_ref[:HEAD_DIM, :] = jnp.zeros((HEAD_DIM, part), BF16)
            result_ref[HEAD_DIM:, :] = found
        else:
            result_ref[...] = found
    if not last:
        partial_ref[...] = dq_acc[...]
    elif not first:
        for member in range(MEMBERS):
            dq_refs[member][...] = query_grads(member)


def attention_backward(
    queries, keys, values, places, mask_rows, sums, outs, grads, chosen, start=None, last=True
):
    query_count = queries.shape[1]
    key_count = keys.shape[1]
    part = query_count // MEMBERS
    wide = HEAD_DIM + EXTRA
    first = start is None
    height = (3 if first and last else 2) * HEAD_DIM
    count = len(chosen)
    results = [((height, part), BF16)] * count
    if not last:
        results.append(((HEAD_DIM, query_count), F32))
    elif not first:
        results += [((HEAD_DIM, part), BF16)] * MEMBERS
    extra = [] if first else [start]
    found = pl.pallas_call(
        functools.partial(backward_kernel, min(1024, query_count), chosen, first, last),
        grid=(1,),
        in_specs=head_specs((queries, keys, values), places)
        + [whole((EXTRA, key_count))]
        + [whole((1, part))] * MEMBERS
        + [whole((HEAD_DIM, part))] * MEMBERS
        + head_specs([grad for grad, place in grads], [place for grad, place in grads])
        + [whole(array.shape) for array in extra],
        out_specs=[whole(dims) for dims, dtype in results],
        out_shape=[jax.ShapeDtypeStruct(dims, dtype) for dims, dtype in results],
        scratch_shapes=[
            pltpu.VMEM((query_count, wide), BF16),
            pltpu.VMEM((wide, key_count), BF16),
            pltpu.VMEM((query_count, wide), BF16),
            pltpu.VMEM((wide, key_count), BF16),
            pltpu.VMEM((HEAD_DIM, query_count), BF16),
            pltpu.VMEM((HEAD_DIM, query_count), BF16),
            pltpu.VMEM((HEAD_DIM, query_count), F32),
            pltpu.VMEM((2 * HEAD_DIM, count * part), BF16),
        ],
        compiler_params=pltpu.CompilerParams(vmem_limit_bytes=VMEM_LIMIT),
        cost_estimate=pl.CostEstimate(
            flops=40 * HEAD_DIM * query_count * count * part,
            transcendentals=query_count * count * part,
            bytes_accessed=16 * HEAD_DIM * key_count,
        ),
    )(queries, keys, values, mask_rows, *sums, *outs, *[grad for grad, place in grads], *extra)
    return list(found[:count]), list(found[count:])


def joined_rows(refs, member):
    count = len(refs) // MEMBERS
    return jnp.concatenate([ref[...] for ref in refs[member * count : (member + 1) * count]])


def project_kernel(weight_ref, bias_ref, *rest):
    piece_refs, (out_ref, weight) = rest[:-2], rest[-2:]
    step = pl.program_id(0)

    @pl.when(step == 0)
    def _():
        weight[...] = weight_ref[...].astype(F32).T.astype(BF16)

    for member in range(MEMBERS):

        @pl.when(step == member)
        def _(member=member):
            rows = joined_rows(piece_refs, member)
            out_ref[...] = (dot(weight[...], rows, 1, 1) + bias_ref[...]).astype(BF16)


def project(weight, bias_column, pieces):
    count, (rows, width) = len(pieces), pieces[0].shape
    columns = weight.shape[1]
    return pl.pallas_call(
        project_kernel,
        grid=(MEMBERS,),
        in_specs=[whole(weight.shape), whole(bias_column.shape)] + [whole((rows, width))] * count,
        out_specs=pl.BlockSpec((columns, count * rows // MEMBERS), lambda i: (0, i)),
        out_shape=jax.ShapeDtypeStruct((columns, count * rows), BF16),
        scratch_shapes=[pltpu.VMEM((columns, width), BF16)],
        compiler_params=pltpu.CompilerParams(vmem_limit_bytes=VMEM_LIMIT),
        cost_estimate=pl.CostEstimate(
            flops=2 * count * rows * width * columns,
            transcendentals=0,
            bytes_accessed=4 * count * rows * width,
        ),
    )(weight, bias_column, *pieces)


def stacked(refs):
    parts = [ref[...] for ref in refs]
    return parts[0] if len(parts) == 1 else jnp.concatenate(parts)


def flatten(nested):
    return [array for slot in nested for member in slot for array in member]


def regroup(refs, counts):
    refs = list(refs)
    return [[[refs.pop(0) for _ in range(n)] for n in slot] for slot in counts]


def counts_of(nested):
    return [[len(member) for member in slot] for slot in nested]


def weight_grad_kernel(counts, pieces, chunk_rows, *rest):
    row_refs, grad_refs, out_ref = rest[:pieces], rest[pieces:-1], rest[-1]
    slots = regroup(grad_refs, counts)
    chunks = out_ref.shape[0]
    columns = out_ref.shape[2] // len(slots)
    part = slots[0][0][0].shape[1]
    ones = jnp.ones((8, part), BF16)
    totals, biases = [0.0] * len(slots), [0.0] * len(slots)
    for member in range(MEMBERS):
        rows = joined_rows(row_refs, member)
        for slot, members in enumerate(slots):
            grad = stacked(members[member])
            totals[slot] = totals[slot] + dot(grad, rows, 1, 0)
            biases[slot] = biases[slot] + dot(ones, grad, 1, 1)
    for slot in range(len(slots)):
        lanes = slice(slot * columns, (slot + 1) * columns)
        turned = totals[slot].T.astype(BF16)
        bias = biases[slot][0:1].astype(BF16)
        bias = jnp.broadcast_to(bias, (out_ref.shape[1] - chunk_rows, columns))
        for chunk in range(chunks):
            out_ref[chunk, :chunk_rows, lanes] = turned[chunk * chunk_rows : (chunk + 1) * chunk_rows]
            out_ref[chunk, chunk_rows:, lanes] = bias


def weight_grad(row_pieces, slots, chunks, chunk_rows, block_rows):
    arrays = flatten(slots)
    shape = (chunks, block_rows, len(slots) * 3 * HEAD_DIM)
    return pl.pallas_call(
        functools.partial(weight_grad_kernel, counts_of(slots), len(row_pieces), chunk_rows),
        grid=(1,),
        in_specs=[whole(array.shape) for array in list(row_pieces) + arrays],
        out_specs=whole(shape),
        out_shape=jax.ShapeDtypeStruct(shape, BF16),
        compiler_params=pltpu.CompilerParams(vmem_limit_bytes=VMEM_LIMIT),
        cost_estimate=pl.CostEstimate(
            flops=2 * shape[2] * len(row_pieces) * row_pieces[0].size,
            transcendentals=0,
            bytes_accessed=2 * len(row_pieces) * row_pieces[0].size,
        ),
    )(*row_pieces, *arrays)


def input_grad_kernel(counts, info_ref, acc_ref, *rest):
    slots = len(counts)
    weight_refs, rest = rest[:slots], rest[slots:]
    grads = regroup(rest[: sum(map(sum, counts))], counts)
    out_refs, (joined, weights) = rest[sum(map(sum, counts)) : -2], rest[-2:]
    width = acc_ref.shape[1]
    step = pl.program_id(0)

    @pl.when(step == 0)
    def _():
        for slot in range(slots):
            weights[slot] = weight_refs[slot][...].reshape(width, width)

    total = acc_ref[...]
    for slot, members in enumerate(grads):
        for member, refs in enumerate(members):
            start = info_ref[member]
            for ref in refs:
                height = ref.shape[0]
                joined[slot, pl.ds(pl.multiple_of(start, HEAD_DIM), height), :] = ref[...]
                start = start + height
        total = total + dot(joined[slot], weights[slot], 0, 1)
    if len(out_refs) == 1:
        out_refs[0][...] = total
        return
    each = len(out_refs) // MEMBERS
    rows = acc_ref.shape[0] // each
    for index, out_ref in enumerate(out_refs):

        @pl.when(step == index // each)
        def _(index=index, out_ref=out_ref):
            start = index % each * rows
            out_ref[...] = total[start : start + rows].astype(out_ref.dtype)


def input_grad_step(info, acc, weights, slots, out_count, dtype):
    arrays = flatten(slots)
    rows, width = acc.shape
    block = rows // MEMBERS
    out = (rows // out_count, width)
    row_spec = pl.BlockSpec((block, width), lambda i, info: (i, 0))
    return pl.pallas_call(
        functools.partial(input_grad_kernel, counts_of(slots)),
        grid_spec=pltpu.PrefetchScalarGridSpec(
            num_scalar_prefetch=1,
            grid=(MEMBERS,),
            in_specs=[row_spec]
            + [pl.BlockSpec(dims, functools.partial(lambda at, i, info: at, place))
               for array, dims, place in weights]
            + [pl.BlockSpec((array.shape[0], block), lambda i, info: (0, i)) for array in arrays],
            out_specs=[row_spec] if out_count == 1 else [whole(out)] * out_count,
            scratch_shapes=[
                pltpu.VMEM((len(slots), width, block), BF16),
                pltpu.VMEM((len(slots), width, width), BF16),
            ],
        ),
        out_shape=[jax.ShapeDtypeStruct(out, dtype)] * out_count,
        compiler_params=pltpu.CompilerParams(vmem_limit_bytes=VMEM_LIMIT),
        cost_estimate=pl.CostEstimate(
            flops=2 * rows * width * width * len(slots),
            transcendentals=0,
            bytes_accessed=8 * rows * width,
        ),
    )(info, acc, *[array for array, dims, place in weights], *arrays)


def collect_kernel(count, place_ref, *rest):
    piece_refs, out_ref = rest[:count], rest[count]
    for index, piece_ref in enumerate(piece_refs):
        out_ref[lax.rem(place_ref[0] + index, count)] = piece_ref[...]


def collect(pieces, place):
    count, shape = len(pieces), pieces[0].shape
    return pl.pallas_call(
        functools.partial(collect_kernel, count),
        grid_spec=pltpu.PrefetchScalarGridSpec(
            num_scalar_prefetch=1,
            grid=(1,),
            in_specs=[whole(shape)] * count,
            out_specs=whole((count,) + shape),
        ),
        out_shape=jax.ShapeDtypeStruct((count,) + shape, pieces[0].dtype),
        compiler_params=pltpu.CompilerParams(vmem_limit_bytes=VMEM_LIMIT),
    )(place[None], *pieces)


def gelu_parts(value):
    t = 1.0 / (1.0 + (0.3275911 * math.sqrt(0.5)) * jnp.abs(value))
    bell = jnp.exp2(value * value * (-0.5 * math.log2(math.e)))
    poly = (0.5 * 1.061405429) * t - 0.5 * 1.453152027
    poly = poly * t + 0.5 * 1.421413741
    poly = poly * t - 0.5 * 0.284496736
    poly = poly * t + 0.5 * 0.254829592
    tail = poly * t * bell
    share = jnp.where(value < 0, tail, 1.0 - tail)
    return value * share, share + value * (bell * (1.0 / math.sqrt(2.0 * math.pi)))


def row_mean(array):
    return jnp.mean(array, axis=-1, keepdims=True)


def column_sum(array):
    return jnp.sum(array, axis=0, keepdims=True)


def layer_kernel(blocks, planes, parts, info_ref, vectors_ref, inner_bias_ref, *rest):
    row_refs, rest = rest[:planes], rest[planes:]
    packed_out, packed_inner, packed_outer = rest[:3]
    att_refs, rest = rest[3 : 3 + parts], rest[3 + parts :]
    cot_refs, rest = rest[:planes], rest[planes:]
    final_refs, rest = rest[:planes], rest[planes:]
    grad_att_refs, rest = rest[: 2 * MEMBERS], rest[2 * MEMBERS :]
    resid_ref, grad_outer_w, grad_inner_w, grad_out_w, grad_vectors, grad_inner_bias = rest[:6]
    attended, hat1, scale1, low, acc, active, slope, grad_low, grad_hidden, weight_out = rest[6:]
    step = pl.program_id(0)
    row_count, width = acc.shape
    piece = row_count // planes
    group = width // MEMBERS
    block = jnp.where(step < blocks, step, step - blocks)
    pieces = [slice(k * piece, (k + 1) * piece) for k in range(planes)]

    def group_rows(member):
        return pl.ds(pl.multiple_of(info_ref[member], HEAD_DIM), group)

    def vector(index):
        return vectors_ref[index : index + 1, :]

    @pl.when(step == 0)
    def _():
        for index, att_ref in enumerate(att_refs):
            attended[index * HEAD_DIM : (index + 1) * HEAD_DIM, :] = att_ref[...]
        weight_out[...] = packed_out[...].reshape(width, width)
        weight = jnp.concatenate([weight_out[group_rows(m), :] for m in range(MEMBERS)])
        for k in range(planes):
            branch = dot(attended[:, pieces[k]], weight, 0, 0) + vector(0)
            value = row_refs[k][...].astype(F32) + branch
            centred = value - row_mean(value)
            scale = lax.rsqrt(row_mean(centred * centred) + EPSILON)
            hat = centred * scale
            normed = hat * vector(1) + vector(2)
            hat1[pieces[k], :] = hat
            scale1[pieces[k], :] = scale
            low[pieces[k], :] = normed.astype(BF16)
            acc[pieces[k], :] = normed + vector(3)
        grad_vectors[...] = jnp.zeros_like(grad_vectors)
        grad_inner_bias[...] = jnp.zeros_like(grad_inner_bias)

    @pl.when(step < blocks)
    def _():
        bias = inner_bias_ref[pl.ds(block, 1), :]
        weight_inner = packed_inner[...].reshape(width, width)
        weight_outer = packed_outer[...].reshape(width, width)
        ahead = dot(low[pieces[0], :], weight_inner, 1, 0)
        for k in range(planes):
            inner = ahead + bias
            if k + 1 < planes:
                ahead = dot(low[pieces[k + 1], :], weight_inner, 1, 0)
            value, derivative = gelu_parts(inner)
            value = value.astype(BF16)
            active[block, pieces[k], :] = value
            slope[block, pieces[k], :] = derivative
            acc[pieces[k], :] += dot(value, weight_outer, 1, 0)

    @pl.when(step == blocks)
    def _():
        gain_sum, shift_sum, bias_sum = 0.0, 0.0, 0.0
        for k in range(planes):
            value = acc[pieces[k], :]
            centred = value - row_mean(value)
            scale = lax.rsqrt(row_mean(centred * centred) + EPSILON)
            hat = centred * scale
            final_refs[k][...] = (hat * vector(4) + vector(5)).astype(BF16)
            places = lax.broadcasted_iota(jnp.int32, (piece, width), 0)
            grad = jnp.where(
                places < info_ref[MEMBERS + k], cot_refs[k][...].astype(F32), 0.0
            )
            gain_sum += column_sum(grad * hat)
            shift_sum += column_sum(grad)
            grad = grad * vector(4)
            grad = scale * (grad - row_mean(grad) - hat * row_mean(grad * hat))
            rounded = grad.astype(BF16)
            bias_sum += column_sum(rounded.astype(F32))
            grad_low[pieces[k], :] = rounded
            acc[pieces[k], :] = grad
        grad_vectors[3:4, :] = bias_sum
        grad_vectors[4:5, :] = gain_sum
        grad_vectors[5:6, :] = shift_sum

    @pl.when(step >= blocks)
    def _():
        bias_sum = 0.0
        weight_inner = packed_inner[...].reshape(width, width)
        weight_outer = packed_outer[...].reshape(width, width)
        ahead = dot(grad_low[pieces[0], :], weight_outer, 1, 1)
        for k in range(planes):
            moved = ahead
            if k + 1 < planes:
                ahead = dot(grad_low[pieces[k + 1], :], weight_outer, 1, 1)
            grad = (moved * slope[block, pieces[k], :]).astype(BF16)
            grad_hidden[pieces[k], :] = grad
            bias_sum += column_sum(grad.astype(F32))
            acc[pieces[k], :] += dot(grad, weight_inner, 1, 1)
        grad_inner_bias[pl.ds(block, 1), :] = bias_sum
        for m in range(MEMBERS // 2):
            lanes = slice(m * 2 * group, (m + 1) * 2 * group)
            grad_outer_w[lanes, :] = dot(active[block, :, lanes], grad_low[...], 0, 0).astype(BF16)
            grad_inner_w[lanes, :] = dot(low[:, lanes], grad_hidden[...], 0, 0).astype(BF16)

    @pl.when(step == 2 * blocks - 1)
    def _():
        gain_sum, shift_sum, bias_sum = 0.0, 0.0, 0.0
        for k in range(planes):
            grad, hat = acc[pieces[k], :], hat1[pieces[k], :]
            gain_sum += column_sum(grad * hat)
            shift_sum += column_sum(grad)
            grad = grad * vector(1)
            grad = scale1[pieces[k], :] * (grad - row_mean(grad) - hat * row_mean(grad * hat))
            resid_ref[pieces[k], :] = grad
            rounded = grad.astype(BF16)
            bias_sum += column_sum(rounded.astype(F32))
            grad_low[pieces[k], :] = rounded
        grad_vectors[0:1, :] = bias_sum
        grad_vectors[1:2, :] = gain_sum
        grad_vectors[2:3, :] = shift_sum
        for m in range(MEMBERS):
            rows = slice(m * group, (m + 1) * group)
            grad_out_w[group_rows(m), :] = dot(attended[rows, :], grad_low[...], 1, 0).astype(BF16)
            moved = dot(weight_out[group_rows(m), :], grad_low[...], 1, 1).astype(BF16)
            grad_att_refs[2 * m][...] = moved[:HEAD_DIM, :]
            grad_att_refs[2 * m + 1][...] = moved[HEAD_DIM:, :]


def layer_rows(info, row_pieces, vectors, inner_bias, weights, att_parts, cot_pieces):
    width = row_pieces[0].shape[1]
    blocks, planes, parts = weights[0], len(cot_pieces), len(att_parts)
    hidden = blocks * width
    row_count = att_parts[0].shape[1]
    piece = row_count // planes
    group = width // MEMBERS
    once = pl.Buffered(1)

    def fixed(shape):
        return pl.BlockSpec(shape, lambda *unused: (0,) * len(shape), pipeline_mode=once)

    square = (width, width)
    weight_specs = [
        pl.BlockSpec(
            dims,
            functools.partial(lambda at, i, info: at(lax.rem(i, blocks)), place),
            pipeline_mode=pl.Buffered(1 if index == 0 else 2),
        )
        for index, (array, dims, place) in enumerate(weights[1:])
    ]
    grad_spec = pl.BlockSpec(square, lambda i, info: (jnp.maximum(i - blocks, 0), 0))
    small = [fixed((8, width)), fixed((8, width))]

    def shape(dims, dtype):
        return jax.ShapeDtypeStruct(dims, dtype)

    result = pl.pallas_call(
        functools.partial(layer_kernel, blocks, planes, parts),
        grid_spec=pltpu.PrefetchScalarGridSpec(
            num_scalar_prefetch=1,
            grid=(2 * blocks,),
            in_specs=small
            + [fixed((piece, width))] * planes
            + weight_specs
            + [fixed((HEAD_DIM, row_count))] * parts
            + [fixed((piece, width))] * planes,
            out_specs=[fixed((piece, width))] * planes
            + [fixed((HEAD_DIM, row_count)), fixed((group - HEAD_DIM, row_count))] * MEMBERS
            + [fixed((row_count, width)), grad_spec, grad_spec, fixed(square)]
            + small,
            scratch_shapes=[
                pltpu.VMEM((width, row_count), BF16),
                pltpu.VMEM((row_count, width), F32),
                pltpu.VMEM((row_count, 1), F32),
                pltpu.VMEM((row_count, width), BF16),
                pltpu.VMEM((row_count, width), F32),
                pltpu.VMEM((blocks, row_count, width), BF16),
                pltpu.VMEM((blocks, row_count, width), F32),
                pltpu.VMEM((row_count, width), BF16),
                pltpu.VMEM((row_count, width), BF16),
                pltpu.VMEM(square, BF16),
            ],
        ),
        out_shape=[shape((piece, width), BF16)] * planes
        + [shape((HEAD_DIM, row_count), BF16), shape((group - HEAD_DIM, row_count), BF16)] * MEMBERS
        + [
            shape((row_count, width), F32),
            shape((hidden, width), BF16),
            shape((hidden, width), BF16),
            shape(square, BF16),
            shape((8, width), F32),
            shape((8, width), F32),
        ],
        compiler_params=pltpu.CompilerParams(vmem_limit_bytes=LAYER_VMEM),
        cost_estimate=pl.CostEstimate(
            flops=12 * row_count * width * hidden,
            transcendentals=row_count * hidden,
            bytes_accessed=8 * width * hidden,
        ),
    )(
        info,
        vectors,
        inner_bias,
        *row_pieces,
        *[array for array, dims, place in weights[1:]],
        *att_parts,
        *cot_pieces,
    )
    return result[:planes], result[planes : planes + 2 * MEMBERS], result[planes + 2 * MEMBERS :]


def pad_rows(array, count):
    return jnp.concatenate([array, jnp.zeros((count,) + array.shape[1:], array.dtype)])


def local(
    layer_input,
    lengths,
    cotangent,
    w_query,
    b_query,
    w_key,
    w_value,
    b_value,
    w_attn_out,
    b_attn_out,
    norm1_gain,
    norm1_bias,
    w_inner,
    b_inner,
    w_outer,
    b_outer,
    norm2_gain,
    norm2_bias,
):
    seqs, part_rows, width = layer_input.shape
    batches = lax.axis_size("batch")
    planes = lax.axis_size("blk") // CORES
    devices = batches * planes * MEMBERS
    spread_planes = planes // seqs
    piece = part_rows // spread_planes
    row_count = planes * piece
    share = width // devices
    wide_share = w_outer.shape[0]
    hidden = wide_share * devices
    folds = hidden // width
    group = width // MEMBERS

    plane = lax.axis_index("blk") // CORES
    core = lax.axis_index("blk") % CORES
    head_place = lax.axis_index("head")
    batch_place = lax.axis_index("batch")
    device = (batch_place * planes + plane) * MEMBERS + core * 2 + head_place
    seq_length = pick(lengths, plane // spread_planes)
    part = plane % spread_planes

    def places(other_plane):
        source = (other_plane - jnp.arange(planes, dtype=jnp.int32)) % planes
        member = jnp.arange(MEMBERS, dtype=jnp.int32)
        cores = core ^ (member // 2)
        heads = head_place ^ (member % 2)
        base = (source[None, :] * CORES + cores[:, None]) * 2 + heads[:, None]
        offset = (other_plane % spread_planes) * piece + jnp.arange(piece, dtype=jnp.int32)
        return (base[:, :, None] * part_rows + offset).reshape(-1)

    def chunks_for_planes(array):
        chunks = array.reshape(planes, piece, width)
        return [pick(chunks, (plane + distance) % planes) for distance in range(planes)]

    def to_planes(array):
        chunks = chunks_for_planes(array)
        return [chunks[0]] + [shift_planes(chunks[k], k) for k in range(1, planes)]

    stage = lax.optimization_barrier

    own_group = core * 2 + head_place
    heads_here = HEADS // MEMBERS
    piece_rows = (share // 8 + 1) * 8
    kinds = jnp.stack([w_query, w_key, w_value], axis=1)
    kinds = kinds.reshape(share, 3, MEMBERS, group)
    by_group = jnp.moveaxis(kinds, 2, 0).reshape(MEMBERS, share, 3 * group)
    bias_row = jnp.pad(jnp.concatenate([b_query, b_value]), (0, 3 * group - 2 * share))
    tail_rows = jnp.pad(bias_row[None], ((0, piece_rows - share - 1), (0, 0)))
    tail_rows = jnp.broadcast_to(tail_rows, (MEMBERS,) + tail_rows.shape)
    by_group = jnp.concatenate([by_group, tail_rows], axis=1)
    by_member = reorder_members(by_group, core, head_place)

    valid_own = places(plane) < seq_length
    row_starts = (own_group ^ jnp.arange(MEMBERS, dtype=jnp.int32)) * group
    kept_rows = seq_length - places(plane)[:row_count:piece]
    info = jnp.concatenate([row_starts, kept_rows])

    def other_plane(distance):
        return (plane // spread_planes) * spread_planes + (part - distance) % spread_planes

    small = jnp.concatenate(
        [b_attn_out, norm1_gain, norm1_bias, b_outer, norm2_gain, norm2_bias, b_inner]
    )
    small_row = jnp.pad(small, (0, width - small.shape[0]))[None]
    inner_rows = jnp.swapaxes(w_inner.reshape(share, folds, width), 0, 1).reshape(-1, width)
    second_pack = jnp.concatenate([w_outer, inner_rows, w_attn_out, small_row])
    second_pack = pad_rows(second_pack, -second_pack.shape[0] % 8)
    valid = [valid_own]
    for distance in range(1, spread_planes):
        valid.append(places(other_plane(distance)) < seq_length)
    mask_row = jnp.where(jnp.concatenate(valid), 0.0, NEG_BIG).astype(BF16)[None]
    mask_rows = pad_rows(mask_row, EXTRA - 1)

    chunks = chunks_for_planes(layer_input)
    own_pieces = chunks[:1] + [shift_planes(chunks[k], k) for k in range(1, planes - 1)]
    head_pieces = [swap_member(own_pieces[0], 1)]
    gathered = [by_member[0]] + [
        swap_member(by_member[member], member) for member in range(1, MEMBERS)
    ]
    own_pieces, head_pieces, gathered, chunks, info, mask_rows, row_starts = stage(
        (own_pieces, head_pieces, gathered, chunks, info, mask_rows, row_starts)
    )
    own_pieces = own_pieces + [shift_planes(chunks[-1], planes - 1)]
    head_pieces = head_pieces + [swap_member(own_pieces[k], 1) for k in range(1, planes - 1)]
    core_pieces = [swap_member(own_pieces[0], 2)]
    both_pieces = [swap_member(head_pieces[0], 2)]
    gathered = reorder_members(jnp.stack(gathered), core, head_place)
    gathered = exchange_planes(jnp.broadcast_to(gathered[None], (planes,) + gathered.shape))
    own_pieces, head_pieces, core_pieces, both_pieces, gathered, second_pack = stage(
        (own_pieces, head_pieces, core_pieces, both_pieces, gathered, second_pack)
    )
    second = lax.all_gather(second_pack, ALL_AXES, axis=0, tiled=False)
    core_pieces = core_pieces + [swap_member(own_pieces[k], 2) for k in range(1, planes)]
    both_pieces = both_pieces + [swap_member(head_pieces[k], 2) for k in range(1, planes - 1)]
    head_pieces = head_pieces + [swap_member(own_pieces[-1], 1)]
    gathered = [gathered] + [shift_batch(gathered, distance) for distance in range(1, batches)]
    core_pieces, both_pieces, head_pieces, gathered = stage(
        (core_pieces, both_pieces, head_pieces, gathered)
    )
    both_pieces = both_pieces + [swap_member(head_pieces[-1], 2)]
    gathered = in_order(gathered, batch_place)
    gathered = gathered.reshape(devices, piece_rows, 3 * group)
    own_weight = gathered[:, :share].reshape(width, 3 * group)
    bias_query = gathered[:, share, :share].reshape(MEMBERS, group)
    bias_value = gathered[:, share, share : 2 * share].reshape(MEMBERS, group)
    own_bias = jnp.concatenate(
        [
            pick(bias_query, own_group),
            jnp.zeros((group,), BF16),
            pick(bias_value, own_group),
        ]
    ).astype(F32)

    all_pieces = own_pieces + head_pieces + core_pieces + both_pieces
    def shift_parts(array, distance):
        size = lax.axis_size("blk")
        route = []
        for i in range(size):
            start = i // CORES // spread_planes * spread_planes
            target = start + (i // CORES - start + distance) % spread_planes
            route.append((i, target * CORES + i % CORES))
        return lax.ppermute(array, "blk", route)

    qkv = project(own_weight, own_bias[:, None], all_pieces)
    late_cotangent, qkv = lax.optimization_barrier((cotangent, qkv))
    cot_pieces = to_planes(late_cotangent)

    slots = jnp.stack([w_query, w_key, w_value], axis=1)
    slots = slots.reshape(share, 3, MEMBERS, heads_here, HEAD_DIM)
    slots = jnp.transpose(slots, (3, 0, 2, 1, 4)).reshape(heads_here * share, width)
    slots, gate = lax.optimization_barrier((slots, qkv[0, 0]))
    third = lax.all_gather(slots, ALL_AXES, axis=0, tiled=False)

    inner_start = wide_share
    out_start = wide_share + share * folds
    small_all = second[:, out_start + share]
    vectors = jnp.swapaxes(small_all[:, : 6 * share].reshape(devices, 6, share), 0, 1)
    vectors = pad_rows(vectors.reshape(6, width).astype(F32), 2)
    bias_inner = small_all[:, 6 * share : 6 * share + wide_share].astype(F32)
    bias_inner = pad_rows(bias_inner.reshape(folds, width), 8 - folds)
    square = (width, width)
    if share % 8 == 0:
        narrow = (devices, share, width)
        layer_weights = (
            folds,
            (second, narrow, lambda j: (0, out_start // share, 0)),
            (second, narrow, lambda j: (0, inner_start // share + j, 0)),
            (second, (devices // folds, wide_share, width), lambda j: (j, 0, 0)),
        )
        slot_weights = [(third, narrow, (0, slot, 0)) for slot in range(heads_here)]
    else:
        inner = second[:, inner_start:out_start].reshape(devices, folds, share, width)
        inner = jnp.swapaxes(inner, 0, 1).reshape((folds,) + square)
        outer = second[:, :wide_share].reshape((folds,) + square)
        layer_weights = (
            folds,
            (second[:, out_start : out_start + share].reshape(square), square, lambda j: (0, 0)),
            (inner, (1,) + square, lambda j: (j, 0, 0)),
            (outer, (1,) + square, lambda j: (j, 0, 0)),
        )
        slot_weights = [
            (third[:, slot * share : (slot + 1) * share].reshape(square), square, (0, 0))
            for slot in range(heads_here)
        ]

    queries = keys = values = qkv
    starts = (0, heads_here, 2 * heads_here)
    if spread_planes > 1:
        sides = [qkv[group:]]
        for distance in range(1, spread_planes):
            sides.append(shift_parts(qkv[group:], distance))
        keys = values = jnp.concatenate(sides, axis=1)
        starts = (0, 0, heads_here)

    def to_members(pieces):
        return [pieces[0]] + [
            swap_member(pieces[member], member) for member in range(1, MEMBERS)
        ]

    far, near = range(1, MEMBERS, 2), range(0, MEMBERS, 2)
    outs, sums, parts = [], [], []
    for slot in range(heads_here):
        slot_at = tuple(start + slot for start in starts)
        chosen = [range(MEMBERS)] if slot < heads_here - 1 else [far, near]
        if slot == heads_here - 1:
            cot_pieces, mask_rows = stage((cot_pieces, mask_rows))
        out, total, moved = {}, {}, {}
        for members in chosen:
            found = attention_forward(queries, keys, values, slot_at, mask_rows, members)
            out.update(found[0])
            total.update(found[1])
            for member in members:
                piece_out = found[0][member]
                moved[member] = swap_member(piece_out, member) if member else piece_out
        outs.append([out[member] for member in range(MEMBERS)])
        sums.append([total[member] for member in range(MEMBERS)])
        parts.append(moved)
    att_parts = [parts[slot][member] for member in range(MEMBERS) for slot in range(heads_here)]
    final_pieces, grad_att, more = layer_rows(
        info, own_pieces, vectors, bias_inner, layer_weights, att_parts, cot_pieces
    )
    output_pieces = [final_pieces[0]] + [
        shift_planes(final_pieces[distance], -distance) for distance in range(1, planes)
    ]
    grad_input, grad_outer_w, grad_inner_w, grad_out_w, grad_vectors, grad_inner_bias = more

    vector_pack = jnp.swapaxes(grad_vectors[:6].reshape(6, devices, share), 0, 1)
    vector_pack = jnp.concatenate(
        [
            vector_pack.reshape(devices, 6 * share),
            grad_inner_bias[:folds].reshape(devices, wide_share),
        ],
        axis=1,
    ).astype(BF16)
    vector_pack = jnp.pad(vector_pack, ((0, 0), (0, width - vector_pack.shape[1])))
    pack_rows = out_start + share
    grad_pack = jnp.concatenate(
        [
            grad_outer_w.reshape(devices, wide_share, width),
            jnp.swapaxes(grad_inner_w.reshape(folds, devices, share, width), 0, 1).reshape(
                devices, folds * share, width
            ),
            grad_out_w.reshape(devices, share, width),
            jnp.pad(vector_pack[:, None], ((0, 0), (0, 7 - pack_rows % 8), (0, 0))),
        ],
        axis=1,
    )
    owned = lax.psum_scatter(grad_pack, ALL_AXES, scatter_dimension=0, tiled=True)[0].astype(F32)
    owned_outer = owned[:wide_share]
    owned_inner = owned[inner_start:out_start].reshape(folds, share, width)
    owned_inner = jnp.swapaxes(owned_inner, 0, 1).reshape(share, hidden)
    owned_out = owned[out_start : out_start + share]
    owned_vectors = owned[out_start + share]

    chunk_rows = width // (batches * planes)
    block_rows = chunk_rows + -chunk_rows % 16 + 16

    def own_places(found):
        own = {index: array for index, array in found.items() if index < MEMBERS}
        for index, array in found.items():
            if index >= MEMBERS:
                moved = shift_parts(array, -(index // MEMBERS)).astype(F32)
                kept = own[index % MEMBERS]
                own[index % MEMBERS] = (kept.astype(F32) + moved).astype(BF16)
        return own

    def send(member, array):
        return swap_member(array, member) if member else array

    pieces_here = MEMBERS * spread_planes
    kept_slots, sent_slots = [], []
    for slot in range(heads_here):
        if slot < 2:
            grad_sent = [send(member, grad_att[2 * member + slot]) for member in range(MEMBERS)]
        slot_at = tuple(start + slot for start in starts)
        given = (queries, keys, values, slot_at, mask_rows, sums[slot], outs[slot])
        place = max(slot - 1, 0)
        if slot == 1:
            output_pieces, grad_sent = lax.optimization_barrier((output_pieces, grad_sent))
        if slot < heads_here - 1:
            chosen = range(pieces_here)
            grad_side = [(array, place) for array in grad_sent]
            found, unused = attention_backward(*given, grad_side, chosen)
            own = own_places(dict(zip(chosen, found)))
            kept_slots.append([[own[member]] for member in range(MEMBERS)])
            sent_slots.append([[send(member, own[member])] for member in range(MEMBERS)])
            continue
        output = collect(output_pieces, plane)
        sent_slots[:-1], grad_sent, output = stage((sent_slots[:-1], grad_sent, output))
        grad_side = [(array, place) for array in grad_sent]
        chosen = range(1, pieces_here, 2)
        found, (partial,) = attention_backward(*given, grad_side, chosen, last=False)
        own = own_places(dict(zip(chosen, found)))
        sent = {member: send(member, own[member]) for member in far}
        grad_input = input_grad_step(
            row_starts, grad_input, slot_weights[:-1], sent_slots, 1, F32
        )[0]
        partial, grad_input = lax.optimization_barrier((partial, grad_input))
        chosen = range(0, pieces_here, 2)
        found, query_grads = attention_backward(*given, grad_side, chosen, start=partial)
        own.update(own_places(dict(zip(chosen, found))))
        sent.update({member: send(member, own[member]) for member in near})
        kept_slots.append([[query_grads[member], own[member]] for member in range(MEMBERS)])
        last_sent = [
            [send(member, query_grads[member]), sent[member]] for member in range(MEMBERS)
        ]
    input_pieces = input_grad_step(
        row_starts, grad_input, slot_weights[-1:], [last_sent], planes, BF16
    )
    chunks = weight_grad(all_pieces, kept_slots, batches * planes, chunk_rows, block_rows)
    chunks = chunks.reshape((batches, planes) + chunks.shape[1:])
    parts = [pick(chunks, (batch_place + distance) % batches) for distance in range(batches)]

    def move(first, last):
        return [shift_planes(input_pieces[k], -k) for k in range(first, last)]

    parts, input_pieces = stage((parts, input_pieces))
    arrived = move(1, 2)
    moved = [shift_batch(parts[distance], distance) for distance in range(1, batches)]
    arrived, moved = stage((arrived, moved))
    total = sum([part_in.astype(F32) for part_in in [parts[0]] + moved])
    sending = total.astype(BF16)
    sending = [pick(sending, (plane + distance) % planes) for distance in range(1, planes)]
    arrived = arrived + move(2, planes - 1)
    moved = [shift_planes(sending[k - 1], k) for k in range(1, planes)]
    arrived, moved, total = stage((arrived, moved, total))
    arrived = arrived + move(planes - 1, planes)
    total = pick(total, plane) + sum([part_in.astype(F32) for part_in in moved])
    columns = total.shape[-1]
    member_rows = total[:chunk_rows].reshape(MEMBERS, share, columns)
    member_rows = reorder_members(member_rows, core, head_place)
    tail = jnp.broadcast_to(total[chunk_rows], (MEMBERS, piece_rows - share, columns))
    sending = jnp.concatenate([member_rows, tail], axis=1)
    got = [sending[0]] + [
        swap_member(sending[member], member) for member in range(1, MEMBERS)
    ]
    got = reorder_members(jnp.stack(got), core, head_place)
    got = got.reshape(MEMBERS, piece_rows, heads_here, 3, HEAD_DIM)
    output = output.reshape(seqs, part_rows, width)
    matrices = [
        jnp.swapaxes(got[:, :share, :, i], 0, 1).reshape(share, width) for i in range(3)
    ]
    biases = [
        lax.dynamic_slice_in_dim(got[:, share, :, i].reshape(width), device * share, share)
        for i in (0, 2)
    ]

    arrived, matrices, biases = stage((arrived, matrices, biases))
    input_grad = collect([input_pieces[0]] + arrived, plane).reshape(seqs, part_rows, width)

    def vector(index):
        return owned_vectors[index * share : (index + 1) * share]

    return (
        output,
        input_grad,
        matrices[0],
        biases[0],
        matrices[1],
        matrices[2],
        biases[1],
        owned_out,
        vector(0),
        vector(1),
        vector(2),
        owned_inner,
        owned_vectors[6 * share : 6 * share + wide_share],
        owned_outer,
        vector(3),
        vector(4),
        vector(5),
    )


def solution(mesh):
    rows = P("batch", ("blk", "head"), None)
    matrix = P(ALL_AXES, None)
    vector = P(ALL_AXES)
    parameters = (
        matrix,
        vector,
        matrix,
        matrix,
        vector,
        matrix,
        vector,
        vector,
        vector,
        matrix,
        vector,
        matrix,
        vector,
        vector,
        vector,
    )
    return jax.shard_map(
        local,
        mesh=mesh,
        in_specs=(rows, P("batch"), rows) + parameters,
        out_specs=(rows, rows) + parameters,
        check_vma=False,
    )
```

```python
import functools
import math

import jax
import jax.numpy as jnp
from jax import lax
from jax.experimental import pallas as pl
from jax.experimental.pallas import tpu as pltpu
from jax.sharding import PartitionSpec as P

HEADS = 12
HEAD_DIM = 64
CORES = 2
MEMBERS = 4
EXTRA = 16
NEG_BIG = -1e30
EPSILON = 1e-06
F32 = jnp.float32
BF16 = jnp.bfloat16
ALL_AXES = ("batch", "blk", "head")
VMEM_LIMIT = 56 * 2**20
LAYER_VMEM = 60 * 2**20


def dot(left_op, right_op, left_dim, right_dim):
    return lax.dot_general(
        left_op, right_op, (((left_dim,), (right_dim,)), ((), ())), preferred_element_type=F32
    )


def shift_planes(array, distance):
    size = lax.axis_size("blk")
    route = [(i, (i + CORES * distance) % size) for i in range(size)]
    return lax.ppermute(array, "blk", route)


def exchange_planes(stack):
    size = lax.axis_size("blk")
    groups = [list(range(core, size, CORES)) for core in range(CORES)]
    return lax.all_to_all(stack, "blk", 0, 0, axis_index_groups=groups, tiled=True)


def shift_batch(array, distance):
    size = lax.axis_size("batch")
    return lax.ppermute(array, "batch", [(i, (i + distance) % size) for i in range(size)])


def swap_member(array, member):
    size = lax.axis_size("blk")
    if member == 1:
        return lax.ppermute(array, "head", [(0, 1), (1, 0)])
    if member == 2:
        return lax.ppermute(array, "blk", [(i, i ^ 1) for i in range(size)])
    route = [(i * 2 + j, (i ^ 1) * 2 + (j ^ 1)) for i in range(size) for j in range(2)]
    return lax.ppermute(array, ("blk", "head"), route)


def pick(array, index):
    return lax.dynamic_index_in_dim(array, index, 0, keepdims=False)


def reorder_members(stack, core, head_place):
    stack = jnp.where(core == 1, jnp.concatenate([stack[2:], stack[:2]]), stack)
    swapped = jnp.stack([stack[1], stack[0], stack[3], stack[2]])
    return jnp.where(head_place == 1, swapped, stack)


def in_order(pieces, place):
    stack = jnp.stack(pieces[::-1] * 2)
    return lax.dynamic_slice_in_dim(stack, len(pieces) - 1 - place, len(pieces), 0)


def split_three(row):
    high = row.astype(BF16)
    rest = row - high.astype(F32)
    middle = rest.astype(BF16)
    low = (rest - middle.astype(F32)).astype(BF16)
    return high, middle, low


def forward_kernel(block_k, members, q_ref, k_ref, v_ref, mask_ref, *rest):
    count = len(members)
    out_refs, sum_refs, (keys, values) = rest[:count], rest[count : 2 * count], rest[2 * count :]
    key_count = k_ref.shape[1]
    block_q = q_ref.shape[1] // MEMBERS
    rows = lax.broadcasted_iota(jnp.int32, (EXTRA, key_count), 0)
    joined = jnp.concatenate([k_ref[...]] * 3 + [mask_ref[...]], axis=0)
    keys[...] = joined.astype(F32).T.astype(BF16)
    values[:HEAD_DIM, :] = v_ref[...]
    values[HEAD_DIM:, :] = jnp.where(rows == 0, 1.0, 0.0).astype(BF16)
    rows_q = lax.broadcasted_iota(jnp.int32, (EXTRA, block_q), 0)
    ones_row = jnp.where(rows_q == 0, 1.0, 0.0).astype(BF16)
    scale = math.log2(math.e) / math.sqrt(HEAD_DIM)

    def prepared(member):
        scaled = q_ref[:, pl.ds(member * block_q, block_q)].astype(F32) * scale
        return jnp.concatenate(list(split_three(scaled)) + [ones_row], axis=0)

    def advance(state, scores, value_part):
        top, acc = state
        new_top = jnp.maximum(top, jnp.max(scores, axis=0, keepdims=True))
        probs = jnp.exp2(scores - new_top).astype(BF16)
        return new_top, acc * jnp.exp2(top - new_top) + dot(value_part, probs, 1, 0)

    for start in range(0, count, 2):
        queries = [prepared(member) for member in members[start : start + 2]]

        def key_block(j, states):
            k_start = pl.multiple_of(j * block_k, block_k)
            key_part = keys[pl.ds(k_start, block_k), :]
            value_part = values[:, pl.ds(k_start, block_k)]
            scores = [dot(key_part, query, 1, 0) for query in queries]
            return tuple(
                advance(state, score, value_part) for state, score in zip(states, scores)
            )

        begin = (jnp.full((1, block_q), NEG_BIG, F32), jnp.zeros((HEAD_DIM + EXTRA, block_q), F32))
        states = lax.fori_loop(0, key_count // block_k, key_block, (begin,) * len(queries))
        for index, (top, acc) in enumerate(states):
            total = acc[HEAD_DIM : HEAD_DIM + 1, :]
            out_refs[start + index][...] = (acc[:HEAD_DIM, :] / total).astype(BF16)
            sum_refs[start + index][...] = top * math.log(2.0) + jnp.log(total)


def head_specs(arrays, places):
    return [
        pl.BlockSpec((HEAD_DIM, array.shape[1]), functools.partial(lambda at, i: (at, 0), place))
        for array, place in zip(arrays, places)
    ]


def whole(shape):
    return pl.BlockSpec(shape, lambda *unused: (0,) * len(shape))


def attention_forward(queries, keys, values, places, mask_rows, members):
    part_count = queries.shape[1] // MEMBERS
    key_count = keys.shape[1]
    count = len(members)
    result = pl.pallas_call(
        functools.partial(forward_kernel, min(512, key_count), members),
        grid=(1,),
        in_specs=head_specs((queries, keys, values), places) + [whole((EXTRA, key_count))],
        out_specs=[whole((HEAD_DIM, part_count))] * count + [whole((1, part_count))] * count,
        out_shape=[jax.ShapeDtypeStruct((HEAD_DIM, part_count), BF16)] * count
        + [jax.ShapeDtypeStruct((1, part_count), F32)] * count,
        scratch_shapes=[
            pltpu.VMEM((key_count, 3 * HEAD_DIM + EXTRA), BF16),
            pltpu.VMEM((HEAD_DIM + EXTRA, key_count), BF16),
        ],
        compiler_params=pltpu.CompilerParams(vmem_limit_bytes=VMEM_LIMIT),
        cost_estimate=pl.CostEstimate(
            flops=16 * HEAD_DIM * count * part_count * key_count,
            transcendentals=count * part_count * key_count,
            bytes_accessed=8 * HEAD_DIM * key_count,
        ),
    )(queries, keys, values, mask_rows)
    return dict(zip(members, result[:count])), dict(zip(members, result[count:]))


def backward_kernel(block_q, chosen, first, last, q_ref, k_ref, v_ref, mask_ref, *rest):
    sum_refs, rest = rest[:MEMBERS], rest[MEMBERS:]
    out_refs, rest = rest[:MEMBERS], rest[MEMBERS:]
    grad_refs, rest = rest[:MEMBERS], rest[MEMBERS:]
    if not first:
        start_ref, rest = rest[0], rest[1:]
    result_refs, rest = rest[: len(chosen)], rest[len(chosen) :]
    if not last:
        partial_ref, rest = rest[0], rest[1:]
    elif not first:
        dq_refs, rest = rest[:MEMBERS], rest[MEMBERS:]
    query_rows, keys, grad_rows, values, scaled_q, grads, dq_acc, dkv = rest
    key_count = k_ref.shape[1]
    query_count = q_ref.shape[1]
    part = query_count // MEMBERS
    scale = 1.0 / math.sqrt(HEAD_DIM)
    places_q = lax.broadcasted_iota(jnp.int32, (EXTRA, query_count), 0)
    places_k = lax.broadcasted_iota(jnp.int32, (EXTRA, key_count), 0)

    def extra_rows(row, fourth):
        high, middle, low = [piece.astype(F32) for piece in split_three(row)]
        rows = jnp.where(
            places_q == 0, high, jnp.where(places_q == 1, middle, jnp.where(places_q == 2, low, 0.0))
        )
        return jnp.where(places_q == 3, fourth, rows).astype(BF16)

    query = (q_ref[...].astype(F32) * scale).astype(BF16)
    scaled_q[...] = query
    deltas = []
    for member in range(MEMBERS):
        grad = grad_refs[member][...]
        grads[:, member * part : (member + 1) * part] = grad
        product = grad.astype(F32) * out_refs[member][...].astype(F32)
        deltas.append(jnp.sum(product, axis=0, keepdims=True))
    deltas = jnp.concatenate(deltas, axis=1)
    sums = jnp.concatenate([sum_ref[...] for sum_ref in sum_refs], axis=1)
    joined_q = jnp.concatenate([query, extra_rows(-sums, 1.0)], axis=0)
    query_rows[...] = joined_q.astype(F32).T.astype(BF16)
    joined_g = jnp.concatenate([grads[...], extra_rows(-deltas, 0.0)], axis=0)
    grad_rows[...] = joined_g.astype(F32).T.astype(BF16)
    ones_rows = jnp.where(places_k < 3, 1.0, 0.0)
    mask_row = mask_ref[0:1, :].astype(F32)
    keys[:HEAD_DIM, :] = k_ref[...]
    keys[HEAD_DIM:, :] = jnp.where(places_k == 3, mask_row, ones_rows).astype(BF16)
    values[:HEAD_DIM, :] = v_ref[...]
    values[HEAD_DIM:, :] = ones_rows.astype(BF16)
    dq_acc[...] = jnp.zeros_like(dq_acc) if first else start_ref[...]

    def key_block(j, unused):
        k_start = pl.multiple_of((chosen.start + j * chosen.step) * part, part)
        key_part = keys[:, pl.ds(k_start, part)]
        value_part = values[:, pl.ds(k_start, part)]
        plain_keys = k_ref[:, pl.ds(k_start, part)]

        def query_block(i, carry):
            dk, dv = carry
            q_start = pl.multiple_of(i * block_q, block_q)
            probs = jnp.exp(dot(query_rows[pl.ds(q_start, block_q), :], key_part, 1, 0))
            moved = dot(grad_rows[pl.ds(q_start, block_q), :], value_part, 1, 0)
            grad_scores = (probs * moved).astype(BF16)
            dv = dv + dot(grads[:, pl.ds(q_start, block_q)], probs.astype(BF16), 1, 0)
            dk = dk + dot(scaled_q[:, pl.ds(q_start, block_q)], grad_scores, 1, 0)
            dq_acc[:, pl.ds(q_start, block_q)] += dot(plain_keys, grad_scores, 1, 1)
            return dk, dv

        zeros = jnp.zeros((HEAD_DIM, part), F32)
        dk, dv = lax.fori_loop(0, query_count // block_q, query_block, (zeros, zeros))
        place = pl.multiple_of(j * part, part)
        dkv[:HEAD_DIM, pl.ds(place, part)] = dk.astype(BF16)
        dkv[HEAD_DIM:, pl.ds(place, part)] = dv.astype(BF16)
        return 0

    lax.fori_loop(0, len(chosen), key_block, 0)

    def query_grads(member):
        return (dq_acc[:, member * part : (member + 1) * part] * scale).astype(BF16)

    together = first and last
    for index, result_ref in enumerate(result_refs):
        found = dkv[:, index * part : (index + 1) * part]
        if together:
            if chosen[index] < MEMBERS:
                result_ref[:HEAD_DIM, :] = query_grads(chosen[index])
            else:
                result_ref[:HEAD_DIM, :] = jnp.zeros((HEAD_DIM, part), BF16)
            result_ref[HEAD_DIM:, :] = found
        else:
            result_ref[...] = found
    if not last:
        partial_ref[...] = dq_acc[...]
    elif not first:
        for member in range(MEMBERS):
            dq_refs[member][...] = query_grads(member)


def attention_backward(
    queries, keys, values, places, mask_rows, sums, outs, grads, chosen, start=None, last=True
):
    query_count = queries.shape[1]
    key_count = keys.shape[1]
    part = query_count // MEMBERS
    wide = HEAD_DIM + EXTRA
    first = start is None
    height = (3 if first and last else 2) * HEAD_DIM
    count = len(chosen)
    results = [((height, part), BF16)] * count
    if not last:
        results.append(((HEAD_DIM, query_count), F32))
    elif not first:
        results += [((HEAD_DIM, part), BF16)] * MEMBERS
    extra = [] if first else [start]
    found = pl.pallas_call(
        functools.partial(backward_kernel, min(2048, query_count), chosen, first, last),
        grid=(1,),
        in_specs=head_specs((queries, keys, values), places)
        + [whole((EXTRA, key_count))]
        + [whole((1, part))] * MEMBERS
        + [whole((HEAD_DIM, part))] * MEMBERS
        + head_specs([grad for grad, place in grads], [place for grad, place in grads])
        + [whole(array.shape) for array in extra],
        out_specs=[whole(dims) for dims, dtype in results],
        out_shape=[jax.ShapeDtypeStruct(dims, dtype) for dims, dtype in results],
        scratch_shapes=[
            pltpu.VMEM((query_count, wide), BF16),
            pltpu.VMEM((wide, key_count), BF16),
            pltpu.VMEM((query_count, wide), BF16),
            pltpu.VMEM((wide, key_count), BF16),
            pltpu.VMEM((HEAD_DIM, query_count), BF16),
            pltpu.VMEM((HEAD_DIM, query_count), BF16),
            pltpu.VMEM((HEAD_DIM, query_count), F32),
            pltpu.VMEM((2 * HEAD_DIM, count * part), BF16),
        ],
        compiler_params=pltpu.CompilerParams(vmem_limit_bytes=VMEM_LIMIT),
        cost_estimate=pl.CostEstimate(
            flops=40 * HEAD_DIM * query_count * count * part,
            transcendentals=query_count * count * part,
            bytes_accessed=16 * HEAD_DIM * key_count,
        ),
    )(queries, keys, values, mask_rows, *sums, *outs, *[grad for grad, place in grads], *extra)
    return list(found[:count]), list(found[count:])


def joined_rows(refs, member):
    count = len(refs) // MEMBERS
    return jnp.concatenate([ref[...] for ref in refs[member * count : (member + 1) * count]])


def project_kernel(weight_ref, bias_ref, *rest):
    piece_refs, (out_ref, weight) = rest[:-2], rest[-2:]
    step = pl.program_id(0)

    @pl.when(step == 0)
    def _():
        weight[...] = weight_ref[...].astype(F32).T.astype(BF16)

    for member in range(MEMBERS):

        @pl.when(step == member)
        def _(member=member):
            rows = joined_rows(piece_refs, member)
            out_ref[...] = (dot(weight[...], rows, 1, 1) + bias_ref[...]).astype(BF16)


def project(weight, bias_column, pieces):
    count, (rows, width) = len(pieces), pieces[0].shape
    columns = weight.shape[1]
    return pl.pallas_call(
        project_kernel,
        grid=(MEMBERS,),
        in_specs=[whole(weight.shape), whole(bias_column.shape)] + [whole((rows, width))] * count,
        out_specs=pl.BlockSpec((columns, count * rows // MEMBERS), lambda i: (0, i)),
        out_shape=jax.ShapeDtypeStruct((columns, count * rows), BF16),
        scratch_shapes=[pltpu.VMEM((columns, width), BF16)],
        compiler_params=pltpu.CompilerParams(vmem_limit_bytes=VMEM_LIMIT),
        cost_estimate=pl.CostEstimate(
            flops=2 * count * rows * width * columns,
            transcendentals=0,
            bytes_accessed=4 * count * rows * width,
        ),
    )(weight, bias_column, *pieces)


def stacked(refs):
    parts = [ref[...] for ref in refs]
    return parts[0] if len(parts) == 1 else jnp.concatenate(parts)


def flatten(nested):
    return [array for slot in nested for member in slot for array in member]


def regroup(refs, counts):
    refs = list(refs)
    return [[[refs.pop(0) for _ in range(n)] for n in slot] for slot in counts]


def counts_of(nested):
    return [[len(member) for member in slot] for slot in nested]


def weight_grad_kernel(counts, pieces, chunk_rows, *rest):
    row_refs, grad_refs, out_ref = rest[:pieces], rest[pieces:-1], rest[-1]
    slots = regroup(grad_refs, counts)
    chunks = out_ref.shape[0]
    columns = out_ref.shape[2] // len(slots)
    part = slots[0][0][0].shape[1]
    ones = jnp.ones((8, part), BF16)
    totals, biases = [0.0] * len(slots), [0.0] * len(slots)
    for member in range(MEMBERS):
        rows = joined_rows(row_refs, member)
        for slot, members in enumerate(slots):
            grad = stacked(members[member])
            totals[slot] = totals[slot] + dot(grad, rows, 1, 0)
            biases[slot] = biases[slot] + dot(ones, grad, 1, 1)
    for slot in range(len(slots)):
        lanes = slice(slot * columns, (slot + 1) * columns)
        turned = totals[slot].T.astype(BF16)
        bias = biases[slot][0:1].astype(BF16)
        bias = jnp.broadcast_to(bias, (out_ref.shape[1] - chunk_rows, columns))
        for chunk in range(chunks):
            out_ref[chunk, :chunk_rows, lanes] = turned[chunk * chunk_rows : (chunk + 1) * chunk_rows]
            out_ref[chunk, chunk_rows:, lanes] = bias


def weight_grad(row_pieces, slots, chunks, chunk_rows, block_rows):
    arrays = flatten(slots)
    shape = (chunks, block_rows, len(slots) * 3 * HEAD_DIM)
    return pl.pallas_call(
        functools.partial(weight_grad_kernel, counts_of(slots), len(row_pieces), chunk_rows),
        grid=(1,),
        in_specs=[whole(array.shape) for array in list(row_pieces) + arrays],
        out_specs=whole(shape),
        out_shape=jax.ShapeDtypeStruct(shape, BF16),
        compiler_params=pltpu.CompilerParams(vmem_limit_bytes=VMEM_LIMIT),
        cost_estimate=pl.CostEstimate(
            flops=2 * shape[2] * len(row_pieces) * row_pieces[0].size,
            transcendentals=0,
            bytes_accessed=2 * len(row_pieces) * row_pieces[0].size,
        ),
    )(*row_pieces, *arrays)


def input_grad_kernel(counts, info_ref, acc_ref, *rest):
    slots = len(counts)
    weight_refs, rest = rest[:slots], rest[slots:]
    grads = regroup(rest[: sum(map(sum, counts))], counts)
    out_refs, (joined, weights) = rest[sum(map(sum, counts)) : -2], rest[-2:]
    width = acc_ref.shape[1]
    step = pl.program_id(0)

    @pl.when(step == 0)
    def _():
        for slot in range(slots):
            weights[slot] = weight_refs[slot][...].reshape(width, width)

    total = acc_ref[...]
    for slot, members in enumerate(grads):
        for member, refs in enumerate(members):
            start = info_ref[member]
            for ref in refs:
                height = ref.shape[0]
                joined[slot, pl.ds(pl.multiple_of(start, HEAD_DIM), height), :] = ref[...]
                start = start + height
        total = total + dot(joined[slot], weights[slot], 0, 1)
    each = len(out_refs) // MEMBERS
    rows = acc_ref.shape[0] // each
    for index, out_ref in enumerate(out_refs):

        @pl.when(step == index // each)
        def _(index=index, out_ref=out_ref):
            start = index % each * rows
            out_ref[...] = total[start : start + rows].astype(out_ref.dtype)


def input_grad_step(info, acc, weights, slots, out_count):
    arrays = flatten(slots)
    rows, width = acc.shape
    block = rows // MEMBERS
    out = (rows // out_count, width)
    row_spec = pl.BlockSpec((block, width), lambda i, info: (i, 0))
    return pl.pallas_call(
        functools.partial(input_grad_kernel, counts_of(slots)),
        grid_spec=pltpu.PrefetchScalarGridSpec(
            num_scalar_prefetch=1,
            grid=(MEMBERS,),
            in_specs=[row_spec]
            + [pl.BlockSpec(dims, functools.partial(lambda at, i, info: at, place))
               for array, dims, place in weights]
            + [pl.BlockSpec((array.shape[0], block), lambda i, info: (0, i)) for array in arrays],
            out_specs=[whole(out)] * out_count,
            scratch_shapes=[
                pltpu.VMEM((len(slots), width, block), BF16),
                pltpu.VMEM((len(slots), width, width), BF16),
            ],
        ),
        out_shape=[jax.ShapeDtypeStruct(out, BF16)] * out_count,
        compiler_params=pltpu.CompilerParams(vmem_limit_bytes=VMEM_LIMIT),
        cost_estimate=pl.CostEstimate(
            flops=2 * rows * width * width * len(slots),
            transcendentals=0,
            bytes_accessed=8 * rows * width,
        ),
    )(info, acc, *[array for array, dims, place in weights], *arrays)


def collect_kernel(count, place_ref, *rest):
    piece_refs, out_ref = rest[:count], rest[count]
    for index, piece_ref in enumerate(piece_refs):
        out_ref[lax.rem(place_ref[0] + index, count)] = piece_ref[...]


def collect(pieces, place):
    count, shape = len(pieces), pieces[0].shape
    return pl.pallas_call(
        functools.partial(collect_kernel, count),
        grid_spec=pltpu.PrefetchScalarGridSpec(
            num_scalar_prefetch=1,
            grid=(1,),
            in_specs=[whole(shape)] * count,
            out_specs=whole((count,) + shape),
        ),
        out_shape=jax.ShapeDtypeStruct((count,) + shape, pieces[0].dtype),
        compiler_params=pltpu.CompilerParams(vmem_limit_bytes=VMEM_LIMIT),
    )(place[None], *pieces)


def gelu_parts(value):
    t = 1.0 / (1.0 + (0.3275911 * math.sqrt(0.5)) * jnp.abs(value))
    bell = jnp.exp2(value * value * (-0.5 * math.log2(math.e)))
    poly = (0.5 * 1.061405429) * t - 0.5 * 1.453152027
    poly = poly * t + 0.5 * 1.421413741
    poly = poly * t - 0.5 * 0.284496736
    poly = poly * t + 0.5 * 0.254829592
    tail = poly * t * bell
    share = jnp.where(value < 0, tail, 1.0 - tail)
    return value * share, share + value * (bell * (1.0 / math.sqrt(2.0 * math.pi)))


def row_mean(array):
    return jnp.mean(array, axis=-1, keepdims=True)


def column_sum(array):
    return jnp.sum(array, axis=0, keepdims=True)


def layer_kernel(blocks, planes, parts, info_ref, vectors_ref, inner_bias_ref, *rest):
    row_refs, rest = rest[:planes], rest[planes:]
    packed_out, packed_inner, packed_outer = rest[:3]
    att_refs, rest = rest[3 : 3 + parts], rest[3 + parts :]
    cot_refs, rest = rest[:planes], rest[planes:]
    final_refs, rest = rest[:planes], rest[planes:]
    grad_att_refs, rest = rest[: 2 * MEMBERS], rest[2 * MEMBERS :]
    resid_ref, grad_outer_w, grad_inner_w, grad_out_w, grad_vectors, grad_inner_bias = rest[:6]
    attended, hat1, scale1, low, acc, active, slope, grad_low, grad_hidden, weight_out = rest[6:]
    step = pl.program_id(0)
    row_count, width = acc.shape
    piece = row_count // planes
    group = width // MEMBERS
    block = jnp.where(step < blocks, step, step - blocks)
    pieces = [slice(k * piece, (k + 1) * piece) for k in range(planes)]

    def group_rows(member):
        return pl.ds(pl.multiple_of(info_ref[member], HEAD_DIM), group)

    def vector(index):
        return vectors_ref[index : index + 1, :]

    @pl.when(step == 0)
    def _():
        for index, att_ref in enumerate(att_refs):
            attended[index * HEAD_DIM : (index + 1) * HEAD_DIM, :] = att_ref[...]
        weight_out[...] = packed_out[...].reshape(width, width)
        weight = jnp.concatenate([weight_out[group_rows(m), :] for m in range(MEMBERS)])
        for k in range(planes):
            branch = dot(attended[:, pieces[k]], weight, 0, 0) + vector(0)
            value = row_refs[k][...].astype(F32) + branch
            centred = value - row_mean(value)
            scale = lax.rsqrt(row_mean(centred * centred) + EPSILON)
            hat = centred * scale
            normed = hat * vector(1) + vector(2)
            hat1[pieces[k], :] = hat
            scale1[pieces[k], :] = scale
            low[pieces[k], :] = normed.astype(BF16)
            acc[pieces[k], :] = normed + vector(3)
        grad_vectors[...] = jnp.zeros_like(grad_vectors)
        grad_inner_bias[...] = jnp.zeros_like(grad_inner_bias)

    @pl.when(step < blocks)
    def _():
        bias = inner_bias_ref[pl.ds(block, 1), :]
        weight_inner = packed_inner[...].reshape(width, width)
        weight_outer = packed_outer[...].reshape(width, width)
        ahead = dot(low[pieces[0], :], weight_inner, 1, 0)
        for k in range(planes):
            inner = ahead + bias
            if k + 1 < planes:
                ahead = dot(low[pieces[k + 1], :], weight_inner, 1, 0)
            value, derivative = gelu_parts(inner)
            value = value.astype(BF16)
            active[block, pieces[k], :] = value
            slope[block, pieces[k], :] = derivative
            acc[pieces[k], :] += dot(value, weight_outer, 1, 0)

    @pl.when(step == blocks)
    def _():
        gain_sum, shift_sum, bias_sum = 0.0, 0.0, 0.0
        for k in range(planes):
            value = acc[pieces[k], :]
            centred = value - row_mean(value)
            scale = lax.rsqrt(row_mean(centred * centred) + EPSILON)
            hat = centred * scale
            final_refs[k][...] = (hat * vector(4) + vector(5)).astype(BF16)
            places = lax.broadcasted_iota(jnp.int32, (piece, width), 0)
            grad = jnp.where(
                places < info_ref[MEMBERS + k], cot_refs[k][...].astype(F32), 0.0
            )
            gain_sum += column_sum(grad * hat)
            shift_sum += column_sum(grad)
            grad = grad * vector(4)
            grad = scale * (grad - row_mean(grad) - hat * row_mean(grad * hat))
            rounded = grad.astype(BF16)
            bias_sum += column_sum(rounded.astype(F32))
            grad_low[pieces[k], :] = rounded
            acc[pieces[k], :] = grad
        grad_vectors[3:4, :] = bias_sum
        grad_vectors[4:5, :] = gain_sum
        grad_vectors[5:6, :] = shift_sum

    @pl.when(step >= blocks)
    def _():
        bias_sum = 0.0
        weight_inner = packed_inner[...].reshape(width, width)
        weight_outer = packed_outer[...].reshape(width, width)
        ahead = dot(grad_low[pieces[0], :], weight_outer, 1, 1)
        for k in range(planes):
            moved = ahead
            if k + 1 < planes:
                ahead = dot(grad_low[pieces[k + 1], :], weight_outer, 1, 1)
            grad = (moved * slope[block, pieces[k], :]).astype(BF16)
            grad_hidden[pieces[k], :] = grad
            bias_sum += column_sum(grad.astype(F32))
            acc[pieces[k], :] += dot(grad, weight_inner, 1, 1)
        grad_inner_bias[pl.ds(block, 1), :] = bias_sum
        for m in range(MEMBERS // 2):
            lanes = slice(m * 2 * group, (m + 1) * 2 * group)
            grad_outer_w[lanes, :] = dot(active[block, :, lanes], grad_low[...], 0, 0).astype(BF16)
            grad_inner_w[lanes, :] = dot(low[:, lanes], grad_hidden[...], 0, 0).astype(BF16)

    @pl.when(step == 2 * blocks - 1)
    def _():
        gain_sum, shift_sum, bias_sum = 0.0, 0.0, 0.0
        for k in range(planes):
            grad, hat = acc[pieces[k], :], hat1[pieces[k], :]
            gain_sum += column_sum(grad * hat)
            shift_sum += column_sum(grad)
            grad = grad * vector(1)
            grad = scale1[pieces[k], :] * (grad - row_mean(grad) - hat * row_mean(grad * hat))
            resid_ref[pieces[k], :] = grad
            rounded = grad.astype(BF16)
            bias_sum += column_sum(rounded.astype(F32))
            grad_low[pieces[k], :] = rounded
        grad_vectors[0:1, :] = bias_sum
        grad_vectors[1:2, :] = gain_sum
        grad_vectors[2:3, :] = shift_sum
        for m in range(MEMBERS):
            rows = slice(m * group, (m + 1) * group)
            grad_out_w[group_rows(m), :] = dot(attended[rows, :], grad_low[...], 1, 0).astype(BF16)
            moved = dot(weight_out[group_rows(m), :], grad_low[...], 1, 1).astype(BF16)
            grad_att_refs[2 * m][...] = moved[:HEAD_DIM, :]
            grad_att_refs[2 * m + 1][...] = moved[HEAD_DIM:, :]


def layer_rows(info, row_pieces, vectors, inner_bias, weights, att_parts, cot_pieces):
    width = row_pieces[0].shape[1]
    blocks, planes, parts = weights[0], len(cot_pieces), len(att_parts)
    hidden = blocks * width
    row_count = att_parts[0].shape[1]
    piece = row_count // planes
    group = width // MEMBERS
    once = pl.Buffered(1)

    def fixed(shape):
        return pl.BlockSpec(shape, lambda *unused: (0,) * len(shape), pipeline_mode=once)

    square = (width, width)
    weight_specs = [
        pl.BlockSpec(
            dims,
            functools.partial(lambda at, i, info: at(lax.rem(i, blocks)), place),
            pipeline_mode=pl.Buffered(1 if index == 0 else 2),
        )
        for index, (array, dims, place) in enumerate(weights[1:])
    ]
    grad_spec = pl.BlockSpec(square, lambda i, info: (jnp.maximum(i - blocks, 0), 0))
    small = [fixed((8, width)), fixed((8, width))]

    def shape(dims, dtype):
        return jax.ShapeDtypeStruct(dims, dtype)

    result = pl.pallas_call(
        functools.partial(layer_kernel, blocks, planes, parts),
        grid_spec=pltpu.PrefetchScalarGridSpec(
            num_scalar_prefetch=1,
            grid=(2 * blocks,),
            in_specs=small
            + [fixed((piece, width))] * planes
            + weight_specs
            + [fixed((HEAD_DIM, row_count))] * parts
            + [fixed((piece, width))] * planes,
            out_specs=[fixed((piece, width))] * planes
            + [fixed((HEAD_DIM, row_count)), fixed((group - HEAD_DIM, row_count))] * MEMBERS
            + [fixed((row_count, width)), grad_spec, grad_spec, fixed(square)]
            + small,
            scratch_shapes=[
                pltpu.VMEM((width, row_count), BF16),
                pltpu.VMEM((row_count, width), F32),
                pltpu.VMEM((row_count, 1), F32),
                pltpu.VMEM((row_count, width), BF16),
                pltpu.VMEM((row_count, width), F32),
                pltpu.VMEM((blocks, row_count, width), BF16),
                pltpu.VMEM((blocks, row_count, width), F32),
                pltpu.VMEM((row_count, width), BF16),
                pltpu.VMEM((row_count, width), BF16),
                pltpu.VMEM(square, BF16),
            ],
        ),
        out_shape=[shape((piece, width), BF16)] * planes
        + [shape((HEAD_DIM, row_count), BF16), shape((group - HEAD_DIM, row_count), BF16)] * MEMBERS
        + [
            shape((row_count, width), F32),
            shape((hidden, width), BF16),
            shape((hidden, width), BF16),
            shape(square, BF16),
            shape((8, width), F32),
            shape((8, width), F32),
        ],
        compiler_params=pltpu.CompilerParams(vmem_limit_bytes=LAYER_VMEM),
        cost_estimate=pl.CostEstimate(
            flops=12 * row_count * width * hidden,
            transcendentals=row_count * hidden,
            bytes_accessed=8 * width * hidden,
        ),
    )(
        info,
        vectors,
        inner_bias,
        *row_pieces,
        *[array for array, dims, place in weights[1:]],
        *att_parts,
        *cot_pieces,
    )
    return result[:planes], result[planes : planes + 2 * MEMBERS], result[planes + 2 * MEMBERS :]


def pad_rows(array, count):
    return jnp.concatenate([array, jnp.zeros((count,) + array.shape[1:], array.dtype)])


def local(
    layer_input,
    lengths,
    cotangent,
    w_query,
    b_query,
    w_key,
    w_value,
    b_value,
    w_attn_out,
    b_attn_out,
    norm1_gain,
    norm1_bias,
    w_inner,
    b_inner,
    w_outer,
    b_outer,
    norm2_gain,
    norm2_bias,
):
    seqs, part_rows, width = layer_input.shape
    batches = lax.axis_size("batch")
    planes = lax.axis_size("blk") // CORES
    devices = batches * planes * MEMBERS
    spread_planes = planes // seqs
    piece = part_rows // spread_planes
    row_count = planes * piece
    share = width // devices
    wide_share = w_outer.shape[0]
    hidden = wide_share * devices
    folds = hidden // width
    group = width // MEMBERS

    plane = lax.axis_index("blk") // CORES
    core = lax.axis_index("blk") % CORES
    head_place = lax.axis_index("head")
    batch_place = lax.axis_index("batch")
    device = (batch_place * planes + plane) * MEMBERS + core * 2 + head_place
    seq_length = pick(lengths, plane // spread_planes)
    part = plane % spread_planes

    def places(other_plane):
        source = (other_plane - jnp.arange(planes, dtype=jnp.int32)) % planes
        member = jnp.arange(MEMBERS, dtype=jnp.int32)
        cores = core ^ (member // 2)
        heads = head_place ^ (member % 2)
        base = (source[None, :] * CORES + cores[:, None]) * 2 + heads[:, None]
        offset = (other_plane % spread_planes) * piece + jnp.arange(piece, dtype=jnp.int32)
        return (base[:, :, None] * part_rows + offset).reshape(-1)

    def chunks_for_planes(array):
        chunks = array.reshape(planes, piece, width)
        return [pick(chunks, (plane + distance) % planes) for distance in range(planes)]

    def to_planes(array):
        chunks = chunks_for_planes(array)
        return [chunks[0]] + [shift_planes(chunks[k], k) for k in range(1, planes)]

    stage = lax.optimization_barrier

    own_group = core * 2 + head_place
    heads_here = HEADS // MEMBERS
    piece_rows = (share // 8 + 1) * 8
    kinds = jnp.stack([w_query, w_key, w_value], axis=1)
    kinds = kinds.reshape(share, 3, MEMBERS, group)
    by_group = jnp.moveaxis(kinds, 2, 0).reshape(MEMBERS, share, 3 * group)
    bias_row = jnp.pad(jnp.concatenate([b_query, b_value]), (0, 3 * group - 2 * share))
    tail_rows = jnp.pad(bias_row[None], ((0, piece_rows - share - 1), (0, 0)))
    tail_rows = jnp.broadcast_to(tail_rows, (MEMBERS,) + tail_rows.shape)
    by_group = jnp.concatenate([by_group, tail_rows], axis=1)
    by_member = reorder_members(by_group, core, head_place)

    valid_own = places(plane) < seq_length
    row_starts = (own_group ^ jnp.arange(MEMBERS, dtype=jnp.int32)) * group
    kept_rows = seq_length - places(plane)[:row_count:piece]
    info = jnp.concatenate([row_starts, kept_rows])

    def other_plane(distance):
        return (plane // spread_planes) * spread_planes + (part - distance) % spread_planes

    small = jnp.concatenate(
        [b_attn_out, norm1_gain, norm1_bias, b_outer, norm2_gain, norm2_bias, b_inner]
    )
    small_row = jnp.pad(small, (0, width - small.shape[0]))[None]
    inner_rows = jnp.swapaxes(w_inner.reshape(share, folds, width), 0, 1).reshape(-1, width)
    second_pack = jnp.concatenate([w_outer, inner_rows, w_attn_out, small_row])
    second_pack = pad_rows(second_pack, -second_pack.shape[0] % 8)
    valid = [valid_own]
    for distance in range(1, spread_planes):
        valid.append(places(other_plane(distance)) < seq_length)
    mask_row = jnp.where(jnp.concatenate(valid), 0.0, NEG_BIG).astype(BF16)[None]
    mask_rows = pad_rows(mask_row, EXTRA - 1)

    chunks = chunks_for_planes(layer_input)
    own_pieces = chunks[:1] + [shift_planes(chunks[k], k) for k in range(1, planes - 1)]
    head_pieces = [swap_member(own_pieces[0], 1)]
    gathered = [by_member[0]] + [
        swap_member(by_member[member], member) for member in range(1, MEMBERS)
    ]
    own_pieces, head_pieces, gathered, chunks, info, mask_rows, row_starts = stage(
        (own_pieces, head_pieces, gathered, chunks, info, mask_rows, row_starts)
    )
    own_pieces = own_pieces + [shift_planes(chunks[-1], planes - 1)]
    head_pieces = head_pieces + [swap_member(own_pieces[k], 1) for k in range(1, planes - 1)]
    core_pieces = [swap_member(own_pieces[0], 2)]
    both_pieces = [swap_member(head_pieces[0], 2)]
    gathered = reorder_members(jnp.stack(gathered), core, head_place)
    gathered = exchange_planes(jnp.broadcast_to(gathered[None], (planes,) + gathered.shape))
    own_pieces, head_pieces, core_pieces, both_pieces, gathered, second_pack = stage(
        (own_pieces, head_pieces, core_pieces, both_pieces, gathered, second_pack)
    )
    second = lax.all_gather(second_pack, ALL_AXES, axis=0, tiled=False)
    core_pieces = core_pieces + [swap_member(own_pieces[k], 2) for k in range(1, planes)]
    both_pieces = both_pieces + [swap_member(head_pieces[k], 2) for k in range(1, planes - 1)]
    head_pieces = head_pieces + [swap_member(own_pieces[-1], 1)]
    gathered = [gathered] + [shift_batch(gathered, distance) for distance in range(1, batches)]
    core_pieces, both_pieces, head_pieces, gathered = stage(
        (core_pieces, both_pieces, head_pieces, gathered)
    )
    both_pieces = both_pieces + [swap_member(head_pieces[-1], 2)]
    gathered = in_order(gathered, batch_place)
    gathered = gathered.reshape(devices, piece_rows, 3 * group)
    own_weight = gathered[:, :share].reshape(width, 3 * group)
    bias_query = gathered[:, share, :share].reshape(MEMBERS, group)
    bias_value = gathered[:, share, share : 2 * share].reshape(MEMBERS, group)
    own_bias = jnp.concatenate(
        [
            pick(bias_query, own_group),
            jnp.zeros((group,), BF16),
            pick(bias_value, own_group),
        ]
    ).astype(F32)

    all_pieces = own_pieces + head_pieces + core_pieces + both_pieces
    def shift_parts(array, distance):
        size = lax.axis_size("blk")
        route = []
        for i in range(size):
            start = i // CORES // spread_planes * spread_planes
            target = start + (i // CORES - start + distance) % spread_planes
            route.append((i, target * CORES + i % CORES))
        return lax.ppermute(array, "blk", route)

    qkv = project(own_weight, own_bias[:, None], all_pieces)
    late_cotangent, qkv = lax.optimization_barrier((cotangent, qkv))
    cot_pieces = to_planes(late_cotangent)

    slots = jnp.stack([w_query, w_key, w_value], axis=1)
    slots = slots.reshape(share, 3, MEMBERS, heads_here, HEAD_DIM)
    slots = jnp.transpose(slots, (3, 0, 2, 1, 4)).reshape(heads_here * share, width)
    slots, gate = lax.optimization_barrier((slots, qkv[0, 0]))
    third = lax.all_gather(slots, ALL_AXES, axis=0, tiled=False)

    inner_start = wide_share
    out_start = wide_share + share * folds
    small_all = second[:, out_start + share]
    vectors = jnp.swapaxes(small_all[:, : 6 * share].reshape(devices, 6, share), 0, 1)
    vectors = pad_rows(vectors.reshape(6, width).astype(F32), 2)
    bias_inner = small_all[:, 6 * share : 6 * share + wide_share].astype(F32)
    bias_inner = pad_rows(bias_inner.reshape(folds, width), 8 - folds)
    square = (width, width)
    if share % 8 == 0:
        narrow = (devices, share, width)
        layer_weights = (
            folds,
            (second, narrow, lambda j: (0, out_start // share, 0)),
            (second, narrow, lambda j: (0, inner_start // share + j, 0)),
            (second, (devices // folds, wide_share, width), lambda j: (j, 0, 0)),
        )
        slot_weights = [(third, narrow, (0, slot, 0)) for slot in range(heads_here)]
    else:
        inner = second[:, inner_start:out_start].reshape(devices, folds, share, width)
        inner = jnp.swapaxes(inner, 0, 1).reshape((folds,) + square)
        outer = second[:, :wide_share].reshape((folds,) + square)
        layer_weights = (
            folds,
            (second[:, out_start : out_start + share].reshape(square), square, lambda j: (0, 0)),
            (inner, (1,) + square, lambda j: (j, 0, 0)),
            (outer, (1,) + square, lambda j: (j, 0, 0)),
        )
        slot_weights = [
            (third[:, slot * share : (slot + 1) * share].reshape(square), square, (0, 0))
            for slot in range(heads_here)
        ]

    queries = keys = values = qkv
    starts = (0, heads_here, 2 * heads_here)
    if spread_planes > 1:
        sides = [qkv[group:]]
        for distance in range(1, spread_planes):
            sides.append(shift_parts(qkv[group:], distance))
        keys = values = jnp.concatenate(sides, axis=1)
        starts = (0, 0, heads_here)

    def to_members(pieces):
        return [pieces[0]] + [
            swap_member(pieces[member], member) for member in range(1, MEMBERS)
        ]

    far, near = range(1, MEMBERS, 2), range(0, MEMBERS, 2)
    outs, sums, parts = [], [], []
    for slot in range(heads_here):
        slot_at = tuple(start + slot for start in starts)
        chosen = [range(MEMBERS)] if slot < heads_here - 1 else [far, near]
        if slot == heads_here - 1:
            cot_pieces, mask_rows = stage((cot_pieces, mask_rows))
        out, total, moved = {}, {}, {}
        for members in chosen:
            found = attention_forward(queries, keys, values, slot_at, mask_rows, members)
            out.update(found[0])
            total.update(found[1])
            for member in members:
                piece_out = found[0][member]
                moved[member] = swap_member(piece_out, member) if member else piece_out
        outs.append([out[member] for member in range(MEMBERS)])
        sums.append([total[member] for member in range(MEMBERS)])
        parts.append(moved)
    att_parts = [parts[slot][member] for member in range(MEMBERS) for slot in range(heads_here)]
    final_pieces, grad_att, more = layer_rows(
        info, own_pieces, vectors, bias_inner, layer_weights, att_parts, cot_pieces
    )
    output_pieces = [final_pieces[0]] + [
        shift_planes(final_pieces[distance], -distance) for distance in range(1, planes)
    ]
    grad_input, grad_outer_w, grad_inner_w, grad_out_w, grad_vectors, grad_inner_bias = more

    vector_pack = jnp.swapaxes(grad_vectors[:6].reshape(6, devices, share), 0, 1)
    vector_pack = jnp.concatenate(
        [
            vector_pack.reshape(devices, 6 * share),
            grad_inner_bias[:folds].reshape(devices, wide_share),
        ],
        axis=1,
    ).astype(BF16)
    vector_pack = jnp.pad(vector_pack, ((0, 0), (0, width - vector_pack.shape[1])))
    pack_rows = out_start + share
    grad_pack = jnp.concatenate(
        [
            grad_outer_w.reshape(devices, wide_share, width),
            jnp.swapaxes(grad_inner_w.reshape(folds, devices, share, width), 0, 1).reshape(
                devices, folds * share, width
            ),
            grad_out_w.reshape(devices, share, width),
            jnp.pad(vector_pack[:, None], ((0, 0), (0, 7 - pack_rows % 8), (0, 0))),
        ],
        axis=1,
    )
    owned = lax.psum_scatter(grad_pack, ALL_AXES, scatter_dimension=0, tiled=True)[0].astype(F32)
    owned_outer = owned[:wide_share]
    owned_inner = owned[inner_start:out_start].reshape(folds, share, width)
    owned_inner = jnp.swapaxes(owned_inner, 0, 1).reshape(share, hidden)
    owned_out = owned[out_start : out_start + share]
    owned_vectors = owned[out_start + share]

    chunk_rows = width // (batches * planes)
    block_rows = chunk_rows + -chunk_rows % 16 + 16

    def own_places(found):
        own = {index: array for index, array in found.items() if index < MEMBERS}
        for index, array in found.items():
            if index >= MEMBERS:
                moved = shift_parts(array, -(index // MEMBERS)).astype(F32)
                kept = own[index % MEMBERS]
                own[index % MEMBERS] = (kept.astype(F32) + moved).astype(BF16)
        return own

    def send(member, array):
        return swap_member(array, member) if member else array

    pieces_here = MEMBERS * spread_planes
    kept_slots, sent_slots = [], []
    for slot in range(heads_here):
        if slot < 2:
            grad_sent = [send(member, grad_att[2 * member + slot]) for member in range(MEMBERS)]
        slot_at = tuple(start + slot for start in starts)
        given = (queries, keys, values, slot_at, mask_rows, sums[slot], outs[slot])
        place = max(slot - 1, 0)
        if slot == 1:
            output_pieces, grad_sent = lax.optimization_barrier((output_pieces, grad_sent))
        if slot < heads_here - 1:
            chosen = range(pieces_here)
            grad_side = [(array, place) for array in grad_sent]
            found, unused = attention_backward(*given, grad_side, chosen)
            own = own_places(dict(zip(chosen, found)))
            kept_slots.append([[own[member]] for member in range(MEMBERS)])
            sent_slots.append([[send(member, own[member])] for member in range(MEMBERS)])
            continue
        output = collect(output_pieces, plane)
        sent_slots[:-1], grad_sent, output = stage((sent_slots[:-1], grad_sent, output))
        grad_side = [(array, place) for array in grad_sent]
        chosen = range(1, pieces_here, 2)
        found, (partial,) = attention_backward(*given, grad_side, chosen, last=False)
        own = own_places(dict(zip(chosen, found)))
        sent = {member: send(member, own[member]) for member in far}
        partial, sent_slots = stage((partial, sent_slots))
        chosen = range(0, pieces_here, 2)
        found, query_grads = attention_backward(*given, grad_side, chosen, start=partial)
        own.update(own_places(dict(zip(chosen, found))))
        sent.update({member: send(member, own[member]) for member in near})
        kept_slots.append([[query_grads[member], own[member]] for member in range(MEMBERS)])
        last_sent = [
            [send(member, query_grads[member]), sent[member]] for member in range(MEMBERS)
        ]
    input_pieces = input_grad_step(
        row_starts, grad_input, slot_weights, sent_slots + [last_sent], planes
    )
    chunks = weight_grad(all_pieces, kept_slots, batches * planes, chunk_rows, block_rows)
    chunks = chunks.reshape((batches, planes) + chunks.shape[1:])
    parts = [pick(chunks, (batch_place + distance) % batches) for distance in range(batches)]

    def move(first, last):
        return [shift_planes(input_pieces[k], -k) for k in range(first, last)]

    parts, input_pieces = stage((parts, input_pieces))
    arrived = move(1, 2)
    moved = [shift_batch(parts[distance], distance) for distance in range(1, batches)]
    arrived, moved = stage((arrived, moved))
    total = sum([part_in.astype(F32) for part_in in [parts[0]] + moved])
    sending = total.astype(BF16)
    sending = [pick(sending, (plane + distance) % planes) for distance in range(1, planes)]
    arrived = arrived + move(2, planes - 1)
    moved = [shift_planes(sending[k - 1], k) for k in range(1, planes)]
    arrived, moved, total = stage((arrived, moved, total))
    arrived = arrived + move(planes - 1, planes)
    total = pick(total, plane) + sum([part_in.astype(F32) for part_in in moved])
    columns = total.shape[-1]
    member_rows = total[:chunk_rows].reshape(MEMBERS, share, columns)
    member_rows = reorder_members(member_rows, core, head_place)
    tail = jnp.broadcast_to(total[chunk_rows], (MEMBERS, piece_rows - share, columns))
    sending = jnp.concatenate([member_rows, tail], axis=1)
    got = [sending[0]] + [
        swap_member(sending[member], member) for member in range(1, MEMBERS)
    ]
    got = reorder_members(jnp.stack(got), core, head_place)
    got = got.reshape(MEMBERS, piece_rows, heads_here, 3, HEAD_DIM)
    output = output.reshape(seqs, part_rows, width)
    matrices = [
        jnp.swapaxes(got[:, :share, :, i], 0, 1).reshape(share, width) for i in range(3)
    ]
    biases = [
        lax.dynamic_slice_in_dim(got[:, share, :, i].reshape(width), device * share, share)
        for i in (0, 2)
    ]

    arrived, matrices, biases = stage((arrived, matrices, biases))
    input_grad = collect([input_pieces[0]] + arrived, plane).reshape(seqs, part_rows, width)

    def vector(index):
        return owned_vectors[index * share : (index + 1) * share]

    return (
        output,
        input_grad,
        matrices[0],
        biases[0],
        matrices[1],
        matrices[2],
        biases[1],
        owned_out,
        vector(0),
        vector(1),
        vector(2),
        owned_inner,
        owned_vectors[6 * share : 6 * share + wide_share],
        owned_outer,
        vector(3),
        vector(4),
        vector(5),
    )


def solution(mesh):
    rows = P("batch", ("blk", "head"), None)
    matrix = P(ALL_AXES, None)
    vector = P(ALL_AXES)
    parameters = (
        matrix,
        vector,
        matrix,
        matrix,
        vector,
        matrix,
        vector,
        vector,
        vector,
        matrix,
        vector,
        matrix,
        vector,
        vector,
        vector,
    )
    return jax.shard_map(
        local,
        mesh=mesh,
        in_specs=(rows, P("batch"), rows) + parameters,
        out_specs=(rows, rows) + parameters,
        check_vma=False,
    )
```

```python
import functools
import math

import jax
import jax.numpy as jnp
from jax import lax
from jax.experimental import pallas as pl
from jax.experimental.pallas import tpu as pltpu
from jax.sharding import PartitionSpec as P

HEADS = 12
HEAD_DIM = 64
CORES = 2
MEMBERS = 4
EXTRA = 16
NEG_BIG = -1e30
EPSILON = 1e-06
F32 = jnp.float32
BF16 = jnp.bfloat16
ALL_AXES = ("batch", "blk", "head")
VMEM_LIMIT = 56 * 2**20
LAYER_VMEM = 60 * 2**20


def dot(left_op, right_op, left_dim, right_dim):
    return lax.dot_general(
        left_op, right_op, (((left_dim,), (right_dim,)), ((), ())), preferred_element_type=F32
    )


def shift_planes(array, distance):
    size = lax.axis_size("blk")
    route = [(i, (i + CORES * distance) % size) for i in range(size)]
    return lax.ppermute(array, "blk", route)


def exchange_planes(stack):
    size = lax.axis_size("blk")
    groups = [list(range(core, size, CORES)) for core in range(CORES)]
    return lax.all_to_all(stack, "blk", 0, 0, axis_index_groups=groups, tiled=True)


def shift_batch(array, distance):
    size = lax.axis_size("batch")
    return lax.ppermute(array, "batch", [(i, (i + distance) % size) for i in range(size)])


def swap_member(array, member):
    size = lax.axis_size("blk")
    if member == 1:
        return lax.ppermute(array, "head", [(0, 1), (1, 0)])
    if member == 2:
        return lax.ppermute(array, "blk", [(i, i ^ 1) for i in range(size)])
    route = [(i * 2 + j, (i ^ 1) * 2 + (j ^ 1)) for i in range(size) for j in range(2)]
    return lax.ppermute(array, ("blk", "head"), route)


def pick(array, index):
    return lax.dynamic_index_in_dim(array, index, 0, keepdims=False)


def reorder_members(stack, core, head_place):
    stack = jnp.where(core == 1, jnp.concatenate([stack[2:], stack[:2]]), stack)
    swapped = jnp.stack([stack[1], stack[0], stack[3], stack[2]])
    return jnp.where(head_place == 1, swapped, stack)


def in_order(pieces, place):
    stack = jnp.stack(pieces[::-1] * 2)
    return lax.dynamic_slice_in_dim(stack, len(pieces) - 1 - place, len(pieces), 0)


def split_three(row):
    high = row.astype(BF16)
    rest = row - high.astype(F32)
    middle = rest.astype(BF16)
    low = (rest - middle.astype(F32)).astype(BF16)
    return high, middle, low


def forward_kernel(block_k, members, q_ref, k_ref, v_ref, mask_ref, *rest):
    count = len(members)
    out_refs, sum_refs, (keys, values) = rest[:count], rest[count : 2 * count], rest[2 * count :]
    key_count = k_ref.shape[1]
    block_q = q_ref.shape[1] // MEMBERS
    rows = lax.broadcasted_iota(jnp.int32, (EXTRA, key_count), 0)
    joined = jnp.concatenate([k_ref[...]] * 3 + [mask_ref[...]], axis=0)
    keys[...] = joined.astype(F32).T.astype(BF16)
    values[:HEAD_DIM, :] = v_ref[...]
    values[HEAD_DIM:, :] = jnp.where(rows == 0, 1.0, 0.0).astype(BF16)
    rows_q = lax.broadcasted_iota(jnp.int32, (EXTRA, block_q), 0)
    ones_row = jnp.where(rows_q == 0, 1.0, 0.0).astype(BF16)
    scale = math.log2(math.e) / math.sqrt(HEAD_DIM)

    def prepared(member):
        scaled = q_ref[:, pl.ds(member * block_q, block_q)].astype(F32) * scale
        return jnp.concatenate(list(split_three(scaled)) + [ones_row], axis=0)

    def advance(state, scores, value_part):
        top, acc = state
        new_top = jnp.maximum(top, jnp.max(scores, axis=0, keepdims=True))
        probs = jnp.exp2(scores - new_top).astype(BF16)
        return new_top, acc * jnp.exp2(top - new_top) + dot(value_part, probs, 1, 0)

    for start in range(0, count, 2):
        queries = [prepared(member) for member in members[start : start + 2]]

        def key_block(j, states):
            k_start = pl.multiple_of(j * block_k, block_k)
            key_part = keys[pl.ds(k_start, block_k), :]
            value_part = values[:, pl.ds(k_start, block_k)]
            scores = [dot(key_part, query, 1, 0) for query in queries]
            return tuple(
                advance(state, score, value_part) for state, score in zip(states, scores)
            )

        begin = (jnp.full((1, block_q), NEG_BIG, F32), jnp.zeros((HEAD_DIM + EXTRA, block_q), F32))
        states = lax.fori_loop(0, key_count // block_k, key_block, (begin,) * len(queries))
        for index, (top, acc) in enumerate(states):
            total = acc[HEAD_DIM : HEAD_DIM + 1, :]
            out_refs[start + index][...] = (acc[:HEAD_DIM, :] / total).astype(BF16)
            sum_refs[start + index][...] = top * math.log(2.0) + jnp.log(total)


def head_specs(arrays, places):
    return [
        pl.BlockSpec((HEAD_DIM, array.shape[1]), functools.partial(lambda at, i: (at, 0), place))
        for array, place in zip(arrays, places)
    ]


def whole(shape):
    return pl.BlockSpec(shape, lambda *unused: (0,) * len(shape))


def attention_forward(queries, keys, values, places, mask_rows, members):
    part_count = queries.shape[1] // MEMBERS
    key_count = keys.shape[1]
    count = len(members)
    result = pl.pallas_call(
        functools.partial(forward_kernel, min(512, key_count), members),
        grid=(1,),
        in_specs=head_specs((queries, keys, values), places) + [whole((EXTRA, key_count))],
        out_specs=[whole((HEAD_DIM, part_count))] * count + [whole((1, part_count))] * count,
        out_shape=[jax.ShapeDtypeStruct((HEAD_DIM, part_count), BF16)] * count
        + [jax.ShapeDtypeStruct((1, part_count), F32)] * count,
        scratch_shapes=[
            pltpu.VMEM((key_count, 3 * HEAD_DIM + EXTRA), BF16),
            pltpu.VMEM((HEAD_DIM + EXTRA, key_count), BF16),
        ],
        compiler_params=pltpu.CompilerParams(vmem_limit_bytes=VMEM_LIMIT),
        cost_estimate=pl.CostEstimate(
            flops=16 * HEAD_DIM * count * part_count * key_count,
            transcendentals=count * part_count * key_count,
            bytes_accessed=8 * HEAD_DIM * key_count,
        ),
    )(queries, keys, values, mask_rows)
    return dict(zip(members, result[:count])), dict(zip(members, result[count:]))


def backward_kernel(block_q, chosen, first, last, q_ref, k_ref, v_ref, mask_ref, *rest):
    sum_refs, rest = rest[:MEMBERS], rest[MEMBERS:]
    out_refs, rest = rest[:MEMBERS], rest[MEMBERS:]
    grad_refs, rest = rest[:MEMBERS], rest[MEMBERS:]
    if not first:
        start_ref, rest = rest[0], rest[1:]
    result_refs, rest = rest[: len(chosen)], rest[len(chosen) :]
    if not last:
        partial_ref, rest = rest[0], rest[1:]
    elif not first:
        dq_refs, rest = rest[:MEMBERS], rest[MEMBERS:]
    query_rows, keys, grad_rows, values, scaled_q, grads, dq_acc, dkv = rest
    key_count = k_ref.shape[1]
    query_count = q_ref.shape[1]
    part = query_count // MEMBERS
    scale = 1.0 / math.sqrt(HEAD_DIM)
    places_q = lax.broadcasted_iota(jnp.int32, (EXTRA, query_count), 0)
    places_k = lax.broadcasted_iota(jnp.int32, (EXTRA, key_count), 0)

    def extra_rows(row, fourth):
        high, middle, low = [piece.astype(F32) for piece in split_three(row)]
        rows = jnp.where(
            places_q == 0, high, jnp.where(places_q == 1, middle, jnp.where(places_q == 2, low, 0.0))
        )
        return jnp.where(places_q == 3, fourth, rows).astype(BF16)

    query = (q_ref[...].astype(F32) * scale).astype(BF16)
    scaled_q[...] = query
    deltas = []
    for member in range(MEMBERS):
        grad = grad_refs[member][...]
        grads[:, member * part : (member + 1) * part] = grad
        product = grad.astype(F32) * out_refs[member][...].astype(F32)
        deltas.append(jnp.sum(product, axis=0, keepdims=True))
    deltas = jnp.concatenate(deltas, axis=1)
    sums = jnp.concatenate([sum_ref[...] for sum_ref in sum_refs], axis=1)
    joined_q = jnp.concatenate([query, extra_rows(-sums, 1.0)], axis=0)
    query_rows[...] = joined_q.astype(F32).T.astype(BF16)
    joined_g = jnp.concatenate([grads[...], extra_rows(-deltas, 0.0)], axis=0)
    grad_rows[...] = joined_g.astype(F32).T.astype(BF16)
    ones_rows = jnp.where(places_k < 3, 1.0, 0.0)
    mask_row = mask_ref[0:1, :].astype(F32)
    keys[:HEAD_DIM, :] = k_ref[...]
    keys[HEAD_DIM:, :] = jnp.where(places_k == 3, mask_row, ones_rows).astype(BF16)
    values[:HEAD_DIM, :] = v_ref[...]
    values[HEAD_DIM:, :] = ones_rows.astype(BF16)
    dq_acc[...] = jnp.zeros_like(dq_acc) if first else start_ref[...]

    def key_block(j, unused):
        k_start = pl.multiple_of((chosen.start + j * chosen.step) * part, part)
        key_part = keys[:, pl.ds(k_start, part)]
        value_part = values[:, pl.ds(k_start, part)]
        plain_keys = k_ref[:, pl.ds(k_start, part)]

        def query_block(i, carry):
            dk, dv = carry
            q_start = pl.multiple_of(i * block_q, block_q)
            probs = jnp.exp(dot(query_rows[pl.ds(q_start, block_q), :], key_part, 1, 0))
            moved = dot(grad_rows[pl.ds(q_start, block_q), :], value_part, 1, 0)
            grad_scores = (probs * moved).astype(BF16)
            dv = dv + dot(grads[:, pl.ds(q_start, block_q)], probs.astype(BF16), 1, 0)
            dk = dk + dot(scaled_q[:, pl.ds(q_start, block_q)], grad_scores, 1, 0)
            dq_acc[:, pl.ds(q_start, block_q)] += dot(plain_keys, grad_scores, 1, 1)
            return dk, dv

        zeros = jnp.zeros((HEAD_DIM, part), F32)
        dk, dv = lax.fori_loop(0, query_count // block_q, query_block, (zeros, zeros))
        place = pl.multiple_of(j * part, part)
        dkv[:HEAD_DIM, pl.ds(place, part)] = dk.astype(BF16)
        dkv[HEAD_DIM:, pl.ds(place, part)] = dv.astype(BF16)
        return 0

    lax.fori_loop(0, len(chosen), key_block, 0)

    def query_grads(member):
        return (dq_acc[:, member * part : (member + 1) * part] * scale).astype(BF16)

    together = first and last
    for index, result_ref in enumerate(result_refs):
        found = dkv[:, index * part : (index + 1) * part]
        if together:
            if chosen[index] < MEMBERS:
                result_ref[:HEAD_DIM, :] = query_grads(chosen[index])
            else:
                result_ref[:HEAD_DIM, :] = jnp.zeros((HEAD_DIM, part), BF16)
            result_ref[HEAD_DIM:, :] = found
        else:
            result_ref[...] = found
    if not last:
        partial_ref[...] = dq_acc[...]
    elif not first:
        for member in range(MEMBERS):
            dq_refs[member][...] = query_grads(member)


def attention_backward(
    queries, keys, values, places, mask_rows, sums, outs, grads, chosen, start=None, last=True
):
    query_count = queries.shape[1]
    key_count = keys.shape[1]
    part = query_count // MEMBERS
    wide = HEAD_DIM + EXTRA
    first = start is None
    height = (3 if first and last else 2) * HEAD_DIM
    count = len(chosen)
    results = [((height, part), BF16)] * count
    if not last:
        results.append(((HEAD_DIM, query_count), F32))
    elif not first:
        results += [((HEAD_DIM, part), BF16)] * MEMBERS
    extra = [] if first else [start]
    found = pl.pallas_call(
        functools.partial(backward_kernel, min(2048, query_count), chosen, first, last),
        grid=(1,),
        in_specs=head_specs((queries, keys, values), places)
        + [whole((EXTRA, key_count))]
        + [whole((1, part))] * MEMBERS
        + [whole((HEAD_DIM, part))] * MEMBERS
        + head_specs([grad for grad, place in grads], [place for grad, place in grads])
        + [whole(array.shape) for array in extra],
        out_specs=[whole(dims) for dims, dtype in results],
        out_shape=[jax.ShapeDtypeStruct(dims, dtype) for dims, dtype in results],
        scratch_shapes=[
            pltpu.VMEM((query_count, wide), BF16),
            pltpu.VMEM((wide, key_count), BF16),
            pltpu.VMEM((query_count, wide), BF16),
            pltpu.VMEM((wide, key_count), BF16),
            pltpu.VMEM((HEAD_DIM, query_count), BF16),
            pltpu.VMEM((HEAD_DIM, query_count), BF16),
            pltpu.VMEM((HEAD_DIM, query_count), F32),
            pltpu.VMEM((2 * HEAD_DIM, count * part), BF16),
        ],
        compiler_params=pltpu.CompilerParams(vmem_limit_bytes=VMEM_LIMIT),
        cost_estimate=pl.CostEstimate(
            flops=40 * HEAD_DIM * query_count * count * part,
            transcendentals=query_count * count * part,
            bytes_accessed=16 * HEAD_DIM * key_count,
        ),
    )(queries, keys, values, mask_rows, *sums, *outs, *[grad for grad, place in grads], *extra)
    return list(found[:count]), list(found[count:])


def joined_rows(refs, member):
    count = len(refs) // MEMBERS
    return jnp.concatenate([ref[...] for ref in refs[member * count : (member + 1) * count]])


def project_kernel(weight_ref, bias_ref, *rest):
    piece_refs, (out_ref, weight) = rest[:-2], rest[-2:]
    step = pl.program_id(0)

    @pl.when(step == 0)
    def _():
        weight[...] = weight_ref[...].astype(F32).T.astype(BF16)

    for member in range(MEMBERS):

        @pl.when(step == member)
        def _(member=member):
            rows = joined_rows(piece_refs, member)
            out_ref[...] = (dot(weight[...], rows, 1, 1) + bias_ref[...]).astype(BF16)


def project(weight, bias_column, pieces):
    count, (rows, width) = len(pieces), pieces[0].shape
    columns = weight.shape[1]
    return pl.pallas_call(
        project_kernel,
        grid=(MEMBERS,),
        in_specs=[whole(weight.shape), whole(bias_column.shape)] + [whole((rows, width))] * count,
        out_specs=pl.BlockSpec((columns, count * rows // MEMBERS), lambda i: (0, i)),
        out_shape=jax.ShapeDtypeStruct((columns, count * rows), BF16),
        scratch_shapes=[pltpu.VMEM((columns, width), BF16)],
        compiler_params=pltpu.CompilerParams(vmem_limit_bytes=VMEM_LIMIT),
        cost_estimate=pl.CostEstimate(
            flops=2 * count * rows * width * columns,
            transcendentals=0,
            bytes_accessed=4 * count * rows * width,
        ),
    )(weight, bias_column, *pieces)


def stacked(refs):
    parts = [ref[...] for ref in refs]
    return parts[0] if len(parts) == 1 else jnp.concatenate(parts)


def flatten(nested):
    return [array for slot in nested for member in slot for array in member]


def regroup(refs, counts):
    refs = list(refs)
    return [[[refs.pop(0) for _ in range(n)] for n in slot] for slot in counts]


def counts_of(nested):
    return [[len(member) for member in slot] for slot in nested]


def weight_grad_kernel(counts, pieces, chunk_rows, *rest):
    row_refs, grad_refs, out_ref = rest[:pieces], rest[pieces:-1], rest[-1]
    slots = regroup(grad_refs, counts)
    chunks = out_ref.shape[0]
    columns = out_ref.shape[2] // len(slots)
    part = slots[0][0][0].shape[1]
    ones = jnp.ones((8, part), BF16)
    totals, biases = [0.0] * len(slots), [0.0] * len(slots)
    for member in range(MEMBERS):
        rows = joined_rows(row_refs, member)
        for slot, members in enumerate(slots):
            grad = stacked(members[member])
            totals[slot] = totals[slot] + dot(grad, rows, 1, 0)
            biases[slot] = biases[slot] + dot(ones, grad, 1, 1)
    for slot in range(len(slots)):
        lanes = slice(slot * columns, (slot + 1) * columns)
        turned = totals[slot].T.astype(BF16)
        bias = biases[slot][0:1].astype(BF16)
        bias = jnp.broadcast_to(bias, (out_ref.shape[1] - chunk_rows, columns))
        for chunk in range(chunks):
            out_ref[chunk, :chunk_rows, lanes] = turned[chunk * chunk_rows : (chunk + 1) * chunk_rows]
            out_ref[chunk, chunk_rows:, lanes] = bias


def weight_grad(row_pieces, slots, chunks, chunk_rows, block_rows):
    arrays = flatten(slots)
    shape = (chunks, block_rows, len(slots) * 3 * HEAD_DIM)
    return pl.pallas_call(
        functools.partial(weight_grad_kernel, counts_of(slots), len(row_pieces), chunk_rows),
        grid=(1,),
        in_specs=[whole(array.shape) for array in list(row_pieces) + arrays],
        out_specs=whole(shape),
        out_shape=jax.ShapeDtypeStruct(shape, BF16),
        compiler_params=pltpu.CompilerParams(vmem_limit_bytes=VMEM_LIMIT),
        cost_estimate=pl.CostEstimate(
            flops=2 * shape[2] * len(row_pieces) * row_pieces[0].size,
            transcendentals=0,
            bytes_accessed=2 * len(row_pieces) * row_pieces[0].size,
        ),
    )(*row_pieces, *arrays)


def input_grad_kernel(counts, info_ref, acc_ref, *rest):
    slots = len(counts)
    weight_refs, rest = rest[:slots], rest[slots:]
    grads = regroup(rest[: sum(map(sum, counts))], counts)
    out_refs, (joined, weights) = rest[sum(map(sum, counts)) : -2], rest[-2:]
    width = acc_ref.shape[1]
    step = pl.program_id(0)

    @pl.when(step == 0)
    def _():
        for slot in range(slots):
            weights[slot] = weight_refs[slot][...].reshape(width, width)

    total = acc_ref[...]
    for slot, members in enumerate(grads):
        for member, refs in enumerate(members):
            start = info_ref[member]
            for ref in refs:
                height = ref.shape[0]
                joined[slot, pl.ds(pl.multiple_of(start, HEAD_DIM), height), :] = ref[...]
                start = start + height
        total = total + dot(joined[slot], weights[slot], 0, 1)
    each = len(out_refs) // MEMBERS
    rows = acc_ref.shape[0] // each
    for index, out_ref in enumerate(out_refs):

        @pl.when(step == index // each)
        def _(index=index, out_ref=out_ref):
            start = index % each * rows
            out_ref[...] = total[start : start + rows].astype(out_ref.dtype)


def input_grad_step(info, acc, weights, slots, out_count):
    arrays = flatten(slots)
    rows, width = acc.shape
    block = rows // MEMBERS
    out = (rows // out_count, width)
    row_spec = pl.BlockSpec((block, width), lambda i, info: (i, 0))
    return pl.pallas_call(
        functools.partial(input_grad_kernel, counts_of(slots)),
        grid_spec=pltpu.PrefetchScalarGridSpec(
            num_scalar_prefetch=1,
            grid=(MEMBERS,),
            in_specs=[row_spec]
            + [pl.BlockSpec(dims, functools.partial(lambda at, i, info: at, place))
               for array, dims, place in weights]
            + [pl.BlockSpec((array.shape[0], block), lambda i, info: (0, i)) for array in arrays],
            out_specs=[whole(out)] * out_count,
            scratch_shapes=[
                pltpu.VMEM((len(slots), width, block), BF16),
                pltpu.VMEM((len(slots), width, width), BF16),
            ],
        ),
        out_shape=[jax.ShapeDtypeStruct(out, BF16)] * out_count,
        compiler_params=pltpu.CompilerParams(vmem_limit_bytes=VMEM_LIMIT),
        cost_estimate=pl.CostEstimate(
            flops=2 * rows * width * width * len(slots),
            transcendentals=0,
            bytes_accessed=8 * rows * width,
        ),
    )(info, acc, *[array for array, dims, place in weights], *arrays)


def collect_kernel(count, place_ref, *rest):
    piece_refs, out_ref = rest[:count], rest[count]
    for index, piece_ref in enumerate(piece_refs):
        out_ref[lax.rem(place_ref[0] + index, count)] = piece_ref[...]


def collect(pieces, place):
    count, shape = len(pieces), pieces[0].shape
    return pl.pallas_call(
        functools.partial(collect_kernel, count),
        grid_spec=pltpu.PrefetchScalarGridSpec(
            num_scalar_prefetch=1,
            grid=(1,),
            in_specs=[whole(shape)] * count,
            out_specs=whole((count,) + shape),
        ),
        out_shape=jax.ShapeDtypeStruct((count,) + shape, pieces[0].dtype),
        compiler_params=pltpu.CompilerParams(vmem_limit_bytes=VMEM_LIMIT),
    )(place[None], *pieces)


def gelu_parts(value):
    t = 1.0 / (1.0 + (0.3275911 * math.sqrt(0.5)) * jnp.abs(value))
    bell = jnp.exp2(value * value * (-0.5 * math.log2(math.e)))
    poly = (0.5 * 1.061405429) * t - 0.5 * 1.453152027
    poly = poly * t + 0.5 * 1.421413741
    poly = poly * t - 0.5 * 0.284496736
    poly = poly * t + 0.5 * 0.254829592
    tail = poly * t * bell
    share = jnp.where(value < 0, tail, 1.0 - tail)
    return value * share, share + value * (bell * (1.0 / math.sqrt(2.0 * math.pi)))


def row_mean(array):
    return jnp.mean(array, axis=-1, keepdims=True)


def column_sum(array):
    return jnp.sum(array, axis=0, keepdims=True)


def layer_kernel(blocks, planes, parts, info_ref, vectors_ref, inner_bias_ref, *rest):
    row_refs, rest = rest[:planes], rest[planes:]
    packed_out, packed_inner, packed_outer = rest[:3]
    att_refs, rest = rest[3 : 3 + parts], rest[3 + parts :]
    cot_refs, rest = rest[:planes], rest[planes:]
    final_refs, rest = rest[:planes], rest[planes:]
    grad_att_refs, rest = rest[: 2 * MEMBERS], rest[2 * MEMBERS :]
    resid_ref, grad_outer_w, grad_inner_w, grad_out_w, grad_vectors, grad_inner_bias = rest[:6]
    attended, hat1, scale1, low, acc, active, slope, grad_low, grad_hidden, weight_out = rest[6:]
    step = pl.program_id(0)
    row_count, width = acc.shape
    piece = row_count // planes
    group = width // MEMBERS
    block = jnp.where(step < blocks, step, step - blocks)
    pieces = [slice(k * piece, (k + 1) * piece) for k in range(planes)]

    def group_rows(member):
        return pl.ds(pl.multiple_of(info_ref[member], HEAD_DIM), group)

    def vector(index):
        return vectors_ref[index : index + 1, :]

    @pl.when(step == 0)
    def _():
        for index, att_ref in enumerate(att_refs):
            attended[index * HEAD_DIM : (index + 1) * HEAD_DIM, :] = att_ref[...]
        weight_out[...] = packed_out[...].reshape(width, width)
        weight = jnp.concatenate([weight_out[group_rows(m), :] for m in range(MEMBERS)])
        for k in range(planes):
            branch = dot(attended[:, pieces[k]], weight, 0, 0) + vector(0)
            value = row_refs[k][...].astype(F32) + branch
            centred = value - row_mean(value)
            scale = lax.rsqrt(row_mean(centred * centred) + EPSILON)
            hat = centred * scale
            normed = hat * vector(1) + vector(2)
            hat1[pieces[k], :] = hat
            scale1[pieces[k], :] = scale
            low[pieces[k], :] = normed.astype(BF16)
            acc[pieces[k], :] = normed + vector(3)
        grad_vectors[...] = jnp.zeros_like(grad_vectors)
        grad_inner_bias[...] = jnp.zeros_like(grad_inner_bias)

    @pl.when(step < blocks)
    def _():
        bias = inner_bias_ref[pl.ds(block, 1), :]
        weight_inner = packed_inner[...].reshape(width, width)
        weight_outer = packed_outer[...].reshape(width, width)
        ahead = dot(low[pieces[0], :], weight_inner, 1, 0)
        for k in range(planes):
            inner = ahead + bias
            if k + 1 < planes:
                ahead = dot(low[pieces[k + 1], :], weight_inner, 1, 0)
            value, derivative = gelu_parts(inner)
            value = value.astype(BF16)
            active[block, pieces[k], :] = value
            slope[block, pieces[k], :] = derivative
            acc[pieces[k], :] += dot(value, weight_outer, 1, 0)

    @pl.when(step == blocks)
    def _():
        gain_sum, shift_sum, bias_sum = 0.0, 0.0, 0.0
        for k in range(planes):
            value = acc[pieces[k], :]
            centred = value - row_mean(value)
            scale = lax.rsqrt(row_mean(centred * centred) + EPSILON)
            hat = centred * scale
            final_refs[k][...] = (hat * vector(4) + vector(5)).astype(BF16)
            places = lax.broadcasted_iota(jnp.int32, (piece, width), 0)
            grad = jnp.where(
                places < info_ref[MEMBERS + k], cot_refs[k][...].astype(F32), 0.0
            )
            gain_sum += column_sum(grad * hat)
            shift_sum += column_sum(grad)
            grad = grad * vector(4)
            grad = scale * (grad - row_mean(grad) - hat * row_mean(grad * hat))
            rounded = grad.astype(BF16)
            bias_sum += column_sum(rounded.astype(F32))
            grad_low[pieces[k], :] = rounded
            acc[pieces[k], :] = grad
        grad_vectors[3:4, :] = bias_sum
        grad_vectors[4:5, :] = gain_sum
        grad_vectors[5:6, :] = shift_sum

    @pl.when(step >= blocks)
    def _():
        bias_sum = 0.0
        weight_inner = packed_inner[...].reshape(width, width)
        weight_outer = packed_outer[...].reshape(width, width)
        ahead = dot(grad_low[pieces[0], :], weight_outer, 1, 1)
        for k in range(planes):
            moved = ahead
            if k + 1 < planes:
                ahead = dot(grad_low[pieces[k + 1], :], weight_outer, 1, 1)
            grad = (moved * slope[block, pieces[k], :]).astype(BF16)
            grad_hidden[pieces[k], :] = grad
            bias_sum += column_sum(grad.astype(F32))
            acc[pieces[k], :] += dot(grad, weight_inner, 1, 1)
        grad_inner_bias[pl.ds(block, 1), :] = bias_sum
        for m in range(MEMBERS // 2):
            lanes = slice(m * 2 * group, (m + 1) * 2 * group)
            grad_outer_w[lanes, :] = dot(active[block, :, lanes], grad_low[...], 0, 0).astype(BF16)
            grad_inner_w[lanes, :] = dot(low[:, lanes], grad_hidden[...], 0, 0).astype(BF16)

    @pl.when(step == 2 * blocks - 1)
    def _():
        gain_sum, shift_sum, bias_sum = 0.0, 0.0, 0.0
        for k in range(planes):
            grad, hat = acc[pieces[k], :], hat1[pieces[k], :]
            gain_sum += column_sum(grad * hat)
            shift_sum += column_sum(grad)
            grad = grad * vector(1)
            grad = scale1[pieces[k], :] * (grad - row_mean(grad) - hat * row_mean(grad * hat))
            resid_ref[pieces[k], :] = grad
            rounded = grad.astype(BF16)
            bias_sum += column_sum(rounded.astype(F32))
            grad_low[pieces[k], :] = rounded
        grad_vectors[0:1, :] = bias_sum
        grad_vectors[1:2, :] = gain_sum
        grad_vectors[2:3, :] = shift_sum
        for m in range(MEMBERS):
            rows = slice(m * group, (m + 1) * group)
            grad_out_w[group_rows(m), :] = dot(attended[rows, :], grad_low[...], 1, 0).astype(BF16)
            moved = dot(weight_out[group_rows(m), :], grad_low[...], 1, 1).astype(BF16)
            grad_att_refs[2 * m][...] = moved[:HEAD_DIM, :]
            grad_att_refs[2 * m + 1][...] = moved[HEAD_DIM:, :]


def layer_rows(info, row_pieces, vectors, inner_bias, weights, att_parts, cot_pieces):
    width = row_pieces[0].shape[1]
    blocks, planes, parts = weights[0], len(cot_pieces), len(att_parts)
    hidden = blocks * width
    row_count = att_parts[0].shape[1]
    piece = row_count // planes
    group = width // MEMBERS
    once = pl.Buffered(1)

    def fixed(shape):
        return pl.BlockSpec(shape, lambda *unused: (0,) * len(shape), pipeline_mode=once)

    square = (width, width)
    weight_specs = [
        pl.BlockSpec(
            dims,
            functools.partial(lambda at, i, info: at(lax.rem(i, blocks)), place),
            pipeline_mode=pl.Buffered(1 if index == 0 else 2),
        )
        for index, (array, dims, place) in enumerate(weights[1:])
    ]
    grad_spec = pl.BlockSpec(square, lambda i, info: (jnp.maximum(i - blocks, 0), 0))
    small = [fixed((8, width)), fixed((8, width))]

    def shape(dims, dtype):
        return jax.ShapeDtypeStruct(dims, dtype)

    result = pl.pallas_call(
        functools.partial(layer_kernel, blocks, planes, parts),
        grid_spec=pltpu.PrefetchScalarGridSpec(
            num_scalar_prefetch=1,
            grid=(2 * blocks,),
            in_specs=small
            + [fixed((piece, width))] * planes
            + weight_specs
            + [fixed((HEAD_DIM, row_count))] * parts
            + [fixed((piece, width))] * planes,
            out_specs=[fixed((piece, width))] * planes
            + [fixed((HEAD_DIM, row_count)), fixed((group - HEAD_DIM, row_count))] * MEMBERS
            + [fixed((row_count, width)), grad_spec, grad_spec, fixed(square)]
            + small,
            scratch_shapes=[
                pltpu.VMEM((width, row_count), BF16),
                pltpu.VMEM((row_count, width), F32),
                pltpu.VMEM((row_count, 1), F32),
                pltpu.VMEM((row_count, width), BF16),
                pltpu.VMEM((row_count, width), F32),
                pltpu.VMEM((blocks, row_count, width), BF16),
                pltpu.VMEM((blocks, row_count, width), F32),
                pltpu.VMEM((row_count, width), BF16),
                pltpu.VMEM((row_count, width), BF16),
                pltpu.VMEM(square, BF16),
            ],
        ),
        out_shape=[shape((piece, width), BF16)] * planes
        + [shape((HEAD_DIM, row_count), BF16), shape((group - HEAD_DIM, row_count), BF16)] * MEMBERS
        + [
            shape((row_count, width), F32),
            shape((hidden, width), BF16),
            shape((hidden, width), BF16),
            shape(square, BF16),
            shape((8, width), F32),
            shape((8, width), F32),
        ],
        compiler_params=pltpu.CompilerParams(vmem_limit_bytes=LAYER_VMEM),
        cost_estimate=pl.CostEstimate(
            flops=12 * row_count * width * hidden,
            transcendentals=row_count * hidden,
            bytes_accessed=8 * width * hidden,
        ),
    )(
        info,
        vectors,
        inner_bias,
        *row_pieces,
        *[array for array, dims, place in weights[1:]],
        *att_parts,
        *cot_pieces,
    )
    return result[:planes], result[planes : planes + 2 * MEMBERS], result[planes + 2 * MEMBERS :]


def pad_rows(array, count):
    return jnp.concatenate([array, jnp.zeros((count,) + array.shape[1:], array.dtype)])


def local(
    layer_input,
    lengths,
    cotangent,
    w_query,
    b_query,
    w_key,
    w_value,
    b_value,
    w_attn_out,
    b_attn_out,
    norm1_gain,
    norm1_bias,
    w_inner,
    b_inner,
    w_outer,
    b_outer,
    norm2_gain,
    norm2_bias,
):
    seqs, part_rows, width = layer_input.shape
    batches = lax.axis_size("batch")
    planes = lax.axis_size("blk") // CORES
    devices = batches * planes * MEMBERS
    spread_planes = planes // seqs
    piece = part_rows // spread_planes
    row_count = planes * piece
    share = width // devices
    wide_share = w_outer.shape[0]
    hidden = wide_share * devices
    folds = hidden // width
    group = width // MEMBERS

    plane = lax.axis_index("blk") // CORES
    core = lax.axis_index("blk") % CORES
    head_place = lax.axis_index("head")
    batch_place = lax.axis_index("batch")
    device = (batch_place * planes + plane) * MEMBERS + core * 2 + head_place
    seq_length = pick(lengths, plane // spread_planes)
    part = plane % spread_planes

    def places(other_plane):
        source = (other_plane - jnp.arange(planes, dtype=jnp.int32)) % planes
        member = jnp.arange(MEMBERS, dtype=jnp.int32)
        cores = core ^ (member // 2)
        heads = head_place ^ (member % 2)
        base = (source[None, :] * CORES + cores[:, None]) * 2 + heads[:, None]
        offset = (other_plane % spread_planes) * piece + jnp.arange(piece, dtype=jnp.int32)
        return (base[:, :, None] * part_rows + offset).reshape(-1)

    def chunks_for_planes(array):
        chunks = array.reshape(planes, piece, width)
        return [pick(chunks, (plane + distance) % planes) for distance in range(planes)]

    def to_planes(array):
        chunks = chunks_for_planes(array)
        return [chunks[0]] + [shift_planes(chunks[k], k) for k in range(1, planes)]

    stage = lax.optimization_barrier

    own_group = core * 2 + head_place
    heads_here = HEADS // MEMBERS
    piece_rows = (share // 8 + 1) * 8
    kinds = jnp.stack([w_query, w_key, w_value], axis=1)
    kinds = kinds.reshape(share, 3, MEMBERS, group)
    by_group = jnp.moveaxis(kinds, 2, 0).reshape(MEMBERS, share, 3 * group)
    bias_row = jnp.pad(jnp.concatenate([b_query, b_value]), (0, 3 * group - 2 * share))
    tail_rows = jnp.pad(bias_row[None], ((0, piece_rows - share - 1), (0, 0)))
    tail_rows = jnp.broadcast_to(tail_rows, (MEMBERS,) + tail_rows.shape)
    by_group = jnp.concatenate([by_group, tail_rows], axis=1)
    by_member = reorder_members(by_group, core, head_place)

    valid_own = places(plane) < seq_length
    row_starts = (own_group ^ jnp.arange(MEMBERS, dtype=jnp.int32)) * group
    kept_rows = seq_length - places(plane)[:row_count:piece]
    info = jnp.concatenate([row_starts, kept_rows])

    def other_plane(distance):
        return (plane // spread_planes) * spread_planes + (part - distance) % spread_planes

    small = jnp.concatenate(
        [b_attn_out, norm1_gain, norm1_bias, b_outer, norm2_gain, norm2_bias, b_inner]
    )
    small_row = jnp.pad(small, (0, width - small.shape[0]))[None]
    inner_rows = jnp.swapaxes(w_inner.reshape(share, folds, width), 0, 1).reshape(-1, width)
    second_pack = jnp.concatenate([w_outer, inner_rows, w_attn_out, small_row])
    second_pack = pad_rows(second_pack, -second_pack.shape[0] % 8)
    valid = [valid_own]
    for distance in range(1, spread_planes):
        valid.append(places(other_plane(distance)) < seq_length)
    mask_row = jnp.where(jnp.concatenate(valid), 0.0, NEG_BIG).astype(BF16)[None]
    mask_rows = pad_rows(mask_row, EXTRA - 1)

    chunks = chunks_for_planes(layer_input)
    own_pieces = chunks[:1] + [shift_planes(chunks[k], k) for k in range(1, planes - 1)]
    head_pieces = [swap_member(own_pieces[0], 1)]
    gathered = [by_member[0]] + [
        swap_member(by_member[member], member) for member in range(1, MEMBERS)
    ]
    own_pieces, head_pieces, gathered, chunks, info, mask_rows, row_starts = stage(
        (own_pieces, head_pieces, gathered, chunks, info, mask_rows, row_starts)
    )
    own_pieces = own_pieces + [shift_planes(chunks[-1], planes - 1)]
    head_pieces = head_pieces + [swap_member(own_pieces[k], 1) for k in range(1, planes - 1)]
    core_pieces = [swap_member(own_pieces[0], 2)]
    both_pieces = [swap_member(head_pieces[0], 2)]
    gathered = reorder_members(jnp.stack(gathered), core, head_place)
    gathered = exchange_planes(jnp.broadcast_to(gathered[None], (planes,) + gathered.shape))
    own_pieces, head_pieces, core_pieces, both_pieces, gathered, second_pack = stage(
        (own_pieces, head_pieces, core_pieces, both_pieces, gathered, second_pack)
    )
    second = lax.all_gather(second_pack, ALL_AXES, axis=0, tiled=False)
    core_pieces = core_pieces + [swap_member(own_pieces[k], 2) for k in range(1, planes)]
    both_pieces = both_pieces + [swap_member(head_pieces[k], 2) for k in range(1, planes - 1)]
    head_pieces = head_pieces + [swap_member(own_pieces[-1], 1)]
    gathered = [gathered] + [shift_batch(gathered, distance) for distance in range(1, batches)]
    core_pieces, both_pieces, head_pieces, gathered = stage(
        (core_pieces, both_pieces, head_pieces, gathered)
    )
    both_pieces = both_pieces + [swap_member(head_pieces[-1], 2)]
    gathered = in_order(gathered, batch_place)
    gathered = gathered.reshape(devices, piece_rows, 3 * group)
    own_weight = gathered[:, :share].reshape(width, 3 * group)
    bias_query = gathered[:, share, :share].reshape(MEMBERS, group)
    bias_value = gathered[:, share, share : 2 * share].reshape(MEMBERS, group)
    own_bias = jnp.concatenate(
        [
            pick(bias_query, own_group),
            jnp.zeros((group,), BF16),
            pick(bias_value, own_group),
        ]
    ).astype(F32)

    all_pieces = own_pieces + head_pieces + core_pieces + both_pieces
    def shift_parts(array, distance):
        size = lax.axis_size("blk")
        route = []
        for i in range(size):
            start = i // CORES // spread_planes * spread_planes
            target = start + (i // CORES - start + distance) % spread_planes
            route.append((i, target * CORES + i % CORES))
        return lax.ppermute(array, "blk", route)

    qkv = project(own_weight, own_bias[:, None], all_pieces)
    late_cotangent, qkv = lax.optimization_barrier((cotangent, qkv))
    cot_pieces = to_planes(late_cotangent)

    slots = jnp.stack([w_query, w_key, w_value], axis=1)
    slots = slots.reshape(share, 3, MEMBERS, heads_here, HEAD_DIM)
    slots = jnp.transpose(slots, (3, 0, 2, 1, 4)).reshape(heads_here * share, width)
    slots, gate = lax.optimization_barrier((slots, qkv[0, 0]))
    third = lax.all_gather(slots, ALL_AXES, axis=0, tiled=False)

    inner_start = wide_share
    out_start = wide_share + share * folds
    small_all = second[:, out_start + share]
    vectors = jnp.swapaxes(small_all[:, : 6 * share].reshape(devices, 6, share), 0, 1)
    vectors = pad_rows(vectors.reshape(6, width).astype(F32), 2)
    bias_inner = small_all[:, 6 * share : 6 * share + wide_share].astype(F32)
    bias_inner = pad_rows(bias_inner.reshape(folds, width), 8 - folds)
    square = (width, width)
    if share % 8 == 0:
        narrow = (devices, share, width)
        layer_weights = (
            folds,
            (second, narrow, lambda j: (0, out_start // share, 0)),
            (second, narrow, lambda j: (0, inner_start // share + j, 0)),
            (second, (devices // folds, wide_share, width), lambda j: (j, 0, 0)),
        )
        slot_weights = [(third, narrow, (0, slot, 0)) for slot in range(heads_here)]
    else:
        inner = second[:, inner_start:out_start].reshape(devices, folds, share, width)
        inner = jnp.swapaxes(inner, 0, 1).reshape((folds,) + square)
        outer = second[:, :wide_share].reshape((folds,) + square)
        layer_weights = (
            folds,
            (second[:, out_start : out_start + share].reshape(square), square, lambda j: (0, 0)),
            (inner, (1,) + square, lambda j: (j, 0, 0)),
            (outer, (1,) + square, lambda j: (j, 0, 0)),
        )
        slot_weights = [
            (third[:, slot * share : (slot + 1) * share].reshape(square), square, (0, 0))
            for slot in range(heads_here)
        ]

    queries = keys = values = qkv
    starts = (0, heads_here, 2 * heads_here)
    if spread_planes > 1:
        sides = [qkv[group:]]
        for distance in range(1, spread_planes):
            sides.append(shift_parts(qkv[group:], distance))
        keys = values = jnp.concatenate(sides, axis=1)
        starts = (0, 0, heads_here)

    def to_members(pieces):
        return [pieces[0]] + [
            swap_member(pieces[member], member) for member in range(1, MEMBERS)
        ]

    far, near = range(1, MEMBERS, 2), range(0, MEMBERS, 2)
    outs, sums, parts = [], [], []
    for slot in range(heads_here):
        slot_at = tuple(start + slot for start in starts)
        chosen = [range(MEMBERS)] if slot < heads_here - 1 else [far, near]
        if slot == heads_here - 1:
            cot_pieces, mask_rows = stage((cot_pieces, mask_rows))
        out, total, moved = {}, {}, {}
        for members in chosen:
            found = attention_forward(queries, keys, values, slot_at, mask_rows, members)
            out.update(found[0])
            total.update(found[1])
            for member in members:
                piece_out = found[0][member]
                moved[member] = swap_member(piece_out, member) if member else piece_out
        outs.append([out[member] for member in range(MEMBERS)])
        sums.append([total[member] for member in range(MEMBERS)])
        parts.append(moved)
    att_parts = [parts[slot][member] for member in range(MEMBERS) for slot in range(heads_here)]
    final_pieces, grad_att, more = layer_rows(
        info, own_pieces, vectors, bias_inner, layer_weights, att_parts, cot_pieces
    )
    output_pieces = [final_pieces[0]] + [
        shift_planes(final_pieces[distance], -distance) for distance in range(1, planes)
    ]
    grad_input, grad_outer_w, grad_inner_w, grad_out_w, grad_vectors, grad_inner_bias = more

    vector_pack = jnp.swapaxes(grad_vectors[:6].reshape(6, devices, share), 0, 1)
    vector_pack = jnp.concatenate(
        [
            vector_pack.reshape(devices, 6 * share),
            grad_inner_bias[:folds].reshape(devices, wide_share),
        ],
        axis=1,
    ).astype(BF16)
    vector_pack = jnp.pad(vector_pack, ((0, 0), (0, width - vector_pack.shape[1])))
    pack_rows = out_start + share
    grad_pack = jnp.concatenate(
        [
            grad_outer_w.reshape(devices, wide_share, width),
            jnp.swapaxes(grad_inner_w.reshape(folds, devices, share, width), 0, 1).reshape(
                devices, folds * share, width
            ),
            grad_out_w.reshape(devices, share, width),
            jnp.pad(vector_pack[:, None], ((0, 0), (0, 7 - pack_rows % 8), (0, 0))),
        ],
        axis=1,
    )
    owned = lax.psum_scatter(grad_pack, ALL_AXES, scatter_dimension=0, tiled=True)[0].astype(F32)
    owned_outer = owned[:wide_share]
    owned_inner = owned[inner_start:out_start].reshape(folds, share, width)
    owned_inner = jnp.swapaxes(owned_inner, 0, 1).reshape(share, hidden)
    owned_out = owned[out_start : out_start + share]
    owned_vectors = owned[out_start + share]

    chunk_rows = width // (batches * planes)
    block_rows = chunk_rows + -chunk_rows % 8 + 8

    def own_places(found):
        own = {index: array for index, array in found.items() if index < MEMBERS}
        for index, array in found.items():
            if index >= MEMBERS:
                moved = shift_parts(array, -(index // MEMBERS)).astype(F32)
                kept = own[index % MEMBERS]
                own[index % MEMBERS] = (kept.astype(F32) + moved).astype(BF16)
        return own

    def send(member, array):
        return swap_member(array, member) if member else array

    pieces_here = MEMBERS * spread_planes
    kept_slots, sent_slots = [], []
    for slot in range(heads_here):
        if slot < 2:
            grad_sent = [send(member, grad_att[2 * member + slot]) for member in range(MEMBERS)]
        slot_at = tuple(start + slot for start in starts)
        given = (queries, keys, values, slot_at, mask_rows, sums[slot], outs[slot])
        place = max(slot - 1, 0)
        if slot == 1:
            output_pieces, grad_sent = lax.optimization_barrier((output_pieces, grad_sent))
        if slot < heads_here - 1:
            chosen = range(pieces_here)
            grad_side = [(array, place) for array in grad_sent]
            found, unused = attention_backward(*given, grad_side, chosen)
            own = own_places(dict(zip(chosen, found)))
            kept_slots.append([[own[member]] for member in range(MEMBERS)])
            sent_slots.append([[send(member, own[member])] for member in range(MEMBERS)])
            continue
        sent_slots[:-1], grad_sent = stage((sent_slots[:-1], grad_sent))
        grad_side = [(array, place) for array in grad_sent]
        chosen = range(1, pieces_here, 2)
        found, (partial,) = attention_backward(*given, grad_side, chosen, last=False)
        own = own_places(dict(zip(chosen, found)))
        sent = {member: send(member, own[member]) for member in far}
        partial, sent_slots = stage((partial, sent_slots))
        chosen = range(0, pieces_here, 2)
        found, query_grads = attention_backward(*given, grad_side, chosen, start=partial)
        own.update(own_places(dict(zip(chosen, found))))
        sent.update({member: send(member, own[member]) for member in near})
        kept_slots.append([[query_grads[member], own[member]] for member in range(MEMBERS)])
        last_sent = [
            [send(member, query_grads[member]), sent[member]] for member in range(MEMBERS)
        ]
    input_pieces = input_grad_step(
        row_starts, grad_input, slot_weights, sent_slots + [last_sent], planes
    )
    chunks = weight_grad(all_pieces, kept_slots, batches * planes, chunk_rows, block_rows)
    chunks = chunks.reshape((batches, planes) + chunks.shape[1:])
    parts = [pick(chunks, (batch_place + distance) % batches) for distance in range(batches)]

    def move(first, last):
        return [shift_planes(input_pieces[k], -k) for k in range(first, last)]

    parts, input_pieces = stage((parts, input_pieces))
    arrived = move(1, 2)
    moved = [shift_batch(parts[distance], distance) for distance in range(1, batches)]
    arrived, moved = stage((arrived, moved))
    total = sum([part_in.astype(F32) for part_in in [parts[0]] + moved])
    sending = total.astype(BF16)
    sending = [pick(sending, (plane + distance) % planes) for distance in range(1, planes)]
    arrived = arrived + move(2, planes - 1)
    moved = [shift_planes(sending[k - 1], k) for k in range(1, planes)]
    arrived, moved, total = stage((arrived, moved, total))
    arrived = arrived + move(planes - 1, planes)
    total = pick(total, plane) + sum([part_in.astype(F32) for part_in in moved])
    columns = total.shape[-1]
    member_rows = total[:chunk_rows].reshape(MEMBERS, share, columns)
    member_rows = reorder_members(member_rows, core, head_place)
    tail = jnp.broadcast_to(total[chunk_rows], (MEMBERS, piece_rows - share, columns))
    sending = jnp.concatenate([member_rows, tail], axis=1)
    got = [sending[0]] + [
        swap_member(sending[member], member) for member in range(1, MEMBERS)
    ]
    got = reorder_members(jnp.stack(got), core, head_place)
    got = got.reshape(MEMBERS, piece_rows, heads_here, 3, HEAD_DIM)
    matrices = [
        jnp.swapaxes(got[:, :share, :, i], 0, 1).reshape(share, width) for i in range(3)
    ]
    biases = [
        lax.dynamic_slice_in_dim(got[:, share, :, i].reshape(width), device * share, share)
        for i in (0, 2)
    ]

    output = collect(output_pieces, plane).reshape(seqs, part_rows, width)
    arrived, matrices, biases, output = stage((arrived, matrices, biases, output))
    input_grad = collect([input_pieces[0]] + arrived, plane).reshape(seqs, part_rows, width)

    def vector(index):
        return owned_vectors[index * share : (index + 1) * share]

    return (
        output,
        input_grad,
        matrices[0],
        biases[0],
        matrices[1],
        matrices[2],
        biases[1],
        owned_out,
        vector(0),
        vector(1),
        vector(2),
        owned_inner,
        owned_vectors[6 * share : 6 * share + wide_share],
        owned_outer,
        vector(3),
        vector(4),
        vector(5),
    )


def solution(mesh):
    rows = P("batch", ("blk", "head"), None)
    matrix = P(ALL_AXES, None)
    vector = P(ALL_AXES)
    parameters = (
        matrix,
        vector,
        matrix,
        matrix,
        vector,
        matrix,
        vector,
        vector,
        vector,
        matrix,
        vector,
        matrix,
        vector,
        vector,
        vector,
    )
    return jax.shard_map(
        local,
        mesh=mesh,
        in_specs=(rows, P("batch"), rows) + parameters,
        out_specs=(rows, rows) + parameters,
        check_vma=False,
    )
```
